32 devices in a mesh: dp: 16 (over z, y, x), seq: 2 (over core).
Axes of the slice: x: 2, y: 2, z: 4, core: 2. Of those that a mesh axis runs over, the one named last changes fastest.
Arguments:
- inputs: bfloat16 [2, 16, 1024, 1024], P(None, 'dp', 'seq'), may hold values from -6 to 6
- w_query: bfloat16 [1024, 256], P(('dp', 'seq')), may hold values from -0.1875 to 0.1875
- w_key: bfloat16 [1024, 256], P(('dp', 'seq')), may hold values from -0.1875 to 0.1875
- w_value: bfloat16 [1024, 1024], P(('dp', 'seq')), may hold values from -0.1875 to 0.1875
- w_out: bfloat16 [1024, 1024], P(('dp', 'seq')), may hold values from -1 to 1
- w_gate: bfloat16 [1024, 2752], P(('dp', 'seq')), may hold values from -0.1875 to 0.1875
- w_up: bfloat16 [1024, 2752], P(('dp', 'seq')), may hold values from -0.1875 to 0.1875
- w_down: bfloat16 [2752, 1024], P(None, ('dp', 'seq')), may hold values from -0.109375 to 0.109375
- gain_one: bfloat16 [1024], P(('dp', 'seq')), may hold values from 0.25 to 1.75
- gain_two: bfloat16 [1024], P(('dp', 'seq')), may hold values from 0.25 to 1.75
- cotangent: bfloat16 [2, 16, 1024, 1024], P(None, 'dp', 'seq'), may hold values from -6 to 6
Outputs:
- output: bfloat16 [2, 16, 1024, 1024], P(None, 'dp', 'seq')
- input_grad: bfloat16 [2, 16, 1024, 1024], P(None, 'dp', 'seq')
- grad_w_query: float32 [1024, 256], P(('dp', 'seq'))
- grad_w_key: float32 [1024, 256], P(('dp', 'seq'))
- grad_w_value: float32 [1024, 1024], P(('dp', 'seq'))
- grad_w_out: float32 [1024, 1024], P(('dp', 'seq'))
- grad_w_gate: float32 [1024, 2752], P(('dp', 'seq'))
- grad_w_up: float32 [1024, 2752], P(('dp', 'seq'))
- grad_w_down: float32 [2752, 1024], P(None, ('dp', 'seq'))
- grad_gain_one: float32 [1024], P(('dp', 'seq'))
- grad_gain_two: float32 [1024], P(('dp', 'seq'))
The draws below stay inside these ranges and needn't reach their ends.
All inputs are finite; a program needn't handle non-finite values.
Results may differ from the reference program's by a relative error of at most 0.014.
Values may be sent and summed in bfloat16 or wider, within the bound.
No kernel may reach another device: no remote copies, remote signals or barrier semaphores. Data moves between devices by JAX's collectives and lax.ppermute only.
A program may use at most 320 MiB of HBM per device.

```python
import jax
import jax.numpy as jnp
from jax import lax

D = 1024
H = 16
F = 16
DV = 64
FF = 2752
LEN = 1024
MICRO = 2
SEQS = 16
BLOCK = 512
N_SEQ = 2


def raised(drawn, rng, source, target, blocks, factor):
    def block_of(dim):
        return (jnp.arange(drawn.shape[dim]) // (drawn.shape[dim] // blocks)).reshape((-1,) + (1,) * (drawn.ndim - 1 - dim))

    near = jax.random.permutation(rng, blocks)[block_of(target)]
    far = (block_of(target) + blocks // 2) % blocks
    return jnp.where((block_of(source) == near) | (block_of(source) == far), factor * drawn, drawn)


def level_of(key, shape, split, low, high):
    level = 1.0
    for dim, shards_of in split:
        steps = jax.random.uniform(jax.random.fold_in(jax.random.fold_in(key, 6), dim), (shards_of,), jnp.float32, low / len(split), high / len(split))
        level = level * jnp.repeat(jnp.exp(steps), shape[dim] // shards_of).reshape((-1,) + (1,) * (len(shape) - 1 - dim))
    return level


def scatter_about(own_key, dims, scale, bound, split=(), held_as=jnp.bfloat16):
    values = jax.random.normal(own_key, dims, jnp.float32) * scale
    if len(split) > 0:
        values = level_of(own_key, dims, split, -0.22, 0.18) * values
    return jnp.clip(values, min=-bound, max=bound).astype(held_as)


def heavy_noise(stream_key, shape, scale, limit, cuts, heavy, kind=jnp.bfloat16):
    entries = scale * jax.random.normal(stream_key, shape, jnp.float32)
    if cuts:
        entries = entries * level_of(stream_key, shape, cuts, -0.22, 0.18)
    return jnp.clip(raised(entries, jax.random.fold_in(stream_key, 3), *heavy), -limit, limit).astype(kind)


def setup_inputs(seed: int = 0) -> dict:
    seeds = jax.random.split(jax.random.key(seed), 12)
    return {
        "inputs": heavy_noise(seeds[0], (MICRO, SEQS, LEN, D), 1.0, 6.0, ((1, 16), (2, 2)), (1, 3, 16, 2.0)),
        "w_query": scatter_about(seeds[1], (D, H * F), D ** -0.5, 0.1875, ((0, 32),)),
        "w_key": scatter_about(seeds[2], (D, H * F), D ** -0.5, 0.1875, ((0, 32),)),
        "w_value": scatter_about(seeds[3], (D, H * DV), D ** -0.5, 0.1875, ((0, 32),)),
        "w_out": scatter_about(seeds[4], (H * DV, D), (D // 32) ** -0.5, 1.0, ((0, 32),)),
        "w_gate": scatter_about(seeds[5], (D, FF), D ** -0.5, 0.1875, ((0, 32),)),
        "w_up": scatter_about(seeds[6], (D, FF), D ** -0.5, 0.1875, ((0, 32),)),
        "w_down": scatter_about(seeds[7], (FF, D), FF ** -0.5, 0.109375, ((1, 32),)),
        "gain_one": jnp.clip(1.0 + 0.15 * jax.random.normal(seeds[8], (D,), jnp.float32), 0.25, 1.75).astype(jnp.bfloat16),
        "gain_two": jnp.clip(1.0 + 0.15 * jax.random.normal(seeds[9], (D,), jnp.float32), 0.25, 1.75).astype(jnp.bfloat16),
        "cotangent": heavy_noise(seeds[10], (MICRO, SEQS, LEN, D), 1.0, 6.0, ((1, 16), (2, 2)), (1, 3, 16, 2.0)),
    }


epsilon = 1e-06
highest_precision = lax.Precision.HIGHEST

@jax.custom_vjp
def low(v):
    return lax.optimization_barrier(v.astype(jnp.bfloat16)).astype(jnp.float32)

@jax.custom_vjp
def reduced_backward(v):
    return v

def low_keep(v):
    return (low(v), None)

def low_pass(kept, grad):
    return (grad,)

def back_keep(v):
    return (v, None)

def back_low(kept, grad):
    return (low(grad),)
low.defvjp(low_keep, low_pass)
reduced_backward.defvjp(back_keep, back_low)

def features(vectors):
    feature_width = vectors.shape[-1]
    outer_product = vectors[..., :, None] * vectors[..., None, :]
    outer_product = outer_product.reshape(vectors.shape[:-1] + (feature_width * feature_width,))
    constant = jnp.ones_like(vectors[..., :1])
    return jnp.concatenate([constant, vectors * feature_width ** (-0.25), outer_product * (2.0 * feature_width) ** (-0.5)], axis=-1)

def rms_norm(values, gain):
    return values * lax.rsqrt(lax.optimization_barrier(jnp.mean(values * values, axis=-1, keepdims=True)) + epsilon) * gain

def block_attend(packed):
    query_tile_rows, key_tile_rows, value_block, prior_state, prior_norm = packed
    block_rows = query_tile_rows.shape[0]
    attention_score = reduced_backward(jnp.einsum('ejx,djx->jed', query_tile_rows, key_tile_rows, precision=highest_precision) * query_tile_rows.shape[-1] ** (-0.5))
    causal = jnp.tril(jnp.ones((block_rows, block_rows), query_tile_rows.dtype))
    kernel = (1.0 + attention_score + 0.5 * attention_score * attention_score) * causal
    numerator = reduced_backward(jnp.einsum('hqk,khd->qhd', low(kernel), value_block, precision=highest_precision))
    denominator = lax.optimization_barrier(jnp.sum(kernel, axis=-1)).T
    query_feats = features(query_tile_rows)
    numerator = numerator + jnp.einsum('qhe,hed->qhd', query_feats, prior_state, precision=highest_precision)
    denominator = denominator + jnp.einsum('qhe,he->qh', query_feats, prior_norm, precision=highest_precision)
    return numerator / denominator[..., None]

def attend_sequence(query_sequence, key_sequence, value_seq):
    query_blocks = query_sequence.reshape(N_SEQ, BLOCK, H, F)
    key_blocks = key_sequence.reshape(N_SEQ, BLOCK, H, F)
    value_blocks = value_seq.reshape(N_SEQ, BLOCK, H, DV)
    key_feats = features(key_blocks)
    state_s = jnp.einsum('nkhe,nkhd->nhed', key_feats, value_blocks, precision=highest_precision)
    state_z = lax.optimization_barrier(jnp.sum(key_feats, axis=1))
    prior_state = jnp.concatenate([jnp.zeros_like(state_s[:1]), jnp.cumsum(state_s[:-1], axis=0)], axis=0)
    prior_norm = jnp.concatenate([jnp.zeros_like(state_z[:1]), jnp.cumsum(state_z[:-1], axis=0)], axis=0)
    attended = lax.map(jax.checkpoint(block_attend), (query_blocks, key_blocks, value_blocks, prior_state, prior_norm))
    return attended.reshape(LEN, H * DV)

def layer_sequence(values, params):
    w_query, w_key, w_value, w_out, w_gate, w_up, w_down, gain_one, gain_two = params
    normed = low(rms_norm(values, gain_one))
    query = reduced_backward(low(jnp.dot(normed, w_query, precision=highest_precision)))
    keys = reduced_backward(low(jnp.dot(normed, w_key, precision=highest_precision)))
    value_proj = reduced_backward(low(jnp.dot(normed, w_value, precision=highest_precision)))
    attended = low(attend_sequence(query, keys, value_proj))
    residual = values + reduced_backward(jnp.dot(attended, w_out, precision=highest_precision))
    normed_two = low(rms_norm(residual, gain_two))
    gate_proj = reduced_backward(jnp.dot(normed_two, w_gate, precision=highest_precision))
    up_proj = reduced_backward(jnp.dot(normed_two, w_up, precision=highest_precision))
    hidden = low(jax.nn.silu(gate_proj) * up_proj)
    return residual + jnp.dot(hidden, w_down, precision=highest_precision)

def reference(inputs, w_query, w_key, w_value, w_out, w_gate, w_up, w_down, gain_one, gain_two, cotangent):
    params = tuple((weight.astype(jnp.float32) for weight in (w_query, w_key, w_value, w_out, w_gate, w_up, w_down, gain_one, gain_two)))
    flat_inputs = inputs.astype(jnp.float32).reshape(MICRO * SEQS, LEN, D)

    def forward(sequences, weights):
        return lax.map(jax.checkpoint(lambda single: layer_sequence(single, weights)), sequences)
    result, pullback = jax.vjp(forward, flat_inputs, params)
    input_grad, weight_grads = pullback(cotangent.astype(jnp.float32).reshape(MICRO * SEQS, LEN, D))
    full_shape = inputs.shape
    return (result.reshape(full_shape).astype(jnp.bfloat16), input_grad.reshape(full_shape).astype(jnp.bfloat16), weight_grads[0], weight_grads[1], weight_grads[2], weight_grads[3], weight_grads[4], weight_grads[5], weight_grads[6], weight_grads[7], weight_grads[8])
```

```python
import functools

import jax
import jax.numpy as jnp
import numpy as np
from jax import lax
from jax.experimental import pallas as pl
from jax.experimental.pallas import tpu as pltpu
from jax.sharding import PartitionSpec as P

H = 16
F = 16
DV = 64
AXES = ("dp", "seq")
EPS = 1e-06
TB = 256
TILE = 256
F32 = jnp.float32
BF16 = jnp.bfloat16

NN = (((1,), (0,)), ((), ()))
NT = (((1,), (1,)), ((), ()))
TN = (((0,), (0,)), ((), ()))


def dot(a, b, dims=NN):
    return lax.dot_general(a, b, dims, preferred_element_type=F32)


VMEM = pl.BlockSpec(memory_space=pltpu.VMEM)
SMEM = pl.BlockSpec(memory_space=pltpu.SMEM)


def params(mib, **kw):
    return pltpu.CompilerParams(vmem_limit_bytes=mib << 20, **kw)


def cost(flops, nbytes, trans=0):
    return pl.CostEstimate(flops=int(flops), bytes_accessed=int(nbytes), transcendentals=int(trans))


def sds(shape, dtype):
    return jax.ShapeDtypeStruct(shape, dtype)


def stage_orders(bits):
    straight = list(range(bits))
    swapped = [1, 0] + list(range(2, bits)) if bits > 1 else straight
    return (straight, swapped)


def stage_pairs(dp, bits, stage):
    orders = stage_orders(bits)
    return [
        (d * 2 + c, (d ^ (1 << orders[c][stage])) * 2 + c) for d in range(dp) for c in range(2)
    ]


def core_pairs(dp):
    return [(i, i ^ 1) for i in range(2 * dp)]


def block_tables(dp, bits):
    orders = stage_orders(bits)
    count = 2 * dp
    position = np.arange(count)
    masks = []
    for c in range(2):
        mask = np.zeros(count, np.int32)
        for stage in range(bits):
            mask |= ((position >> (bits - 1 - stage)) & 1) << orders[c][stage]
        masks.append(mask)
    d = lax.axis_index("dp").astype(jnp.int32)
    c = lax.axis_index("seq").astype(jnp.int32)
    owner_core = jnp.asarray(position >> bits, jnp.int32) ^ c
    mask = jnp.where(owner_core == 0, jnp.asarray(masks[0]), jnp.asarray(masks[1]))
    block_at = (d ^ mask) * 2 + owner_core
    block_core = jnp.asarray(position & 1, jnp.int32)
    apart = jnp.asarray(position >> 1, jnp.int32) ^ d
    places = []
    for k in range(2):
        place = jnp.zeros(count, jnp.int32)
        for stage in range(bits):
            place = place | (((apart >> orders[k][stage]) & 1) << (bits - 1 - stage))
        places.append(place)
    place_of = jnp.where(block_core == 0, places[0], places[1]) | ((block_core ^ c) << bits)
    return jnp.concatenate([block_at, place_of, c[None], jnp.zeros(7, jnp.int32)]), c


def gather(shard, dp, bits):
    held = shard
    for stage in reversed(range(bits)):
        came = lax.ppermute(held, AXES, stage_pairs(dp, bits, stage))
        if stage > 0:
            held = jnp.concatenate([held, came], axis=-2)
    swap = core_pairs(dp)
    return (held, came, lax.ppermute(held, AXES, swap), lax.ppermute(came, AXES, swap))


def reduce_rows(keep, send, dp, bits):
    came = lax.ppermute(send, AXES, core_pairs(dp))
    for stage in range(bits):
        half = keep.shape[-2] // 2
        send = (
            lax.slice_in_dim(keep, half, 2 * half, axis=keep.ndim - 2).astype(F32)
            + lax.slice_in_dim(came, half, 2 * half, axis=keep.ndim - 2).astype(F32)
        ).astype(BF16)
        keep = (
            lax.slice_in_dim(keep, 0, half, axis=keep.ndim - 2).astype(F32)
            + lax.slice_in_dim(came, 0, half, axis=keep.ndim - 2).astype(F32)
        ).astype(BF16)
        came = lax.ppermute(send, AXES, stage_pairs(dp, bits, stage))
    return keep.astype(F32) + came.astype(F32)


def pre_kernel(rows, count, tab, x, xr, y, yr, xt, r1, yt, yn, buf):
    c = tab[2 * count]
    half, width = xr.shape
    total = jnp.zeros((1, 2 * half), F32)
    for src, rec, dst in ((x, xr, xt), (y, yr, yt)):
        for i in range(half // 128):
            own = pl.multiple_of(c * half + i * 128, 128)
            other = pl.multiple_of((1 - c) * half + i * 128, 128)
            buf[:, pl.ds(own, 128)] = src[c, i * 128 : (i + 1) * 128, :].T.astype(buf.dtype)
            buf[:, pl.ds(other, 128)] = rec[i * 128 : (i + 1) * 128, :].T.astype(buf.dtype)

        def move(p, _):
            at = pl.multiple_of(tab[p] * rows, rows)
            dst[pl.ds(pl.multiple_of(p * rows, rows), rows), :] = buf[pl.ds(at, rows), :]
            return 0

        lax.fori_loop(0, count, move, 0)
    for i in range(width // 128):
        part = xt[i * 128 : (i + 1) * 128, :].astype(F32)
        total = total + jnp.sum(part * part, axis=0, keepdims=True)
        yn[:, i * 128 : (i + 1) * 128] = yt[i * 128 : (i + 1) * 128, :].T.astype(BF16)
    r1[...] = lax.rsqrt(total / width + EPS)


def pre(tab, x, xr, y, yr, rows, count, kind):
    half, width = xr.shape
    tokens = 2 * half
    return pl.pallas_call(
        functools.partial(pre_kernel, rows, count),
        out_shape=(
            sds((width, tokens), kind),
            sds((1, tokens), F32),
            sds((width, tokens), kind),
            sds((tokens, width), BF16),
        ),
        in_specs=[SMEM] + [VMEM] * 4,
        out_specs=[VMEM] * 4,
        scratch_shapes=[pltpu.VMEM((width, tokens), kind)],
        compiler_params=params(40),
        cost_estimate=cost(8 * width * tokens, 14 * width * tokens),
        name="pre",
    )(tab, x, xr, y, yr)


def project_kernel(xt, r1, w0, w1, w2, w3, normed, out):
    scale = r1[...]
    wide = out.shape[0]
    quarter = w0.shape[0]
    for q, w in enumerate((w0, w1, w2, w3)):
        gain = w[:, wide : wide + 1].astype(F32)
        part = xt[q * quarter : (q + 1) * quarter, :].astype(F32)
        normed[q * quarter : (q + 1) * quarter, :] = (part * scale * gain).astype(BF16)

    def tile(i, _):
        at = pl.multiple_of(i * 256, 256)
        acc = dot(w0[:, pl.ds(at, 256)], normed[0:quarter, :], TN)
        for q, w in ((1, w1), (2, w2), (3, w3)):
            acc = acc + dot(
                w[:, pl.ds(at, 256)], normed[q * quarter : (q + 1) * quarter, :], TN
            )
        out[pl.ds(at, 256), :] = acc.astype(BF16)
        return 0

    lax.fori_loop(0, wide // 256, tile, 0)


def project(xt, r1, bufs, wide):
    width, tokens = xt.shape
    return pl.pallas_call(
        project_kernel,
        out_shape=(sds((width, tokens), BF16), sds((wide, tokens), BF16)),
        in_specs=[VMEM] * 6,
        out_specs=[VMEM] * 2,
        compiler_params=params(40),
        cost_estimate=cost(2 * width * tokens * wide, 2 * (2 * width * tokens + 2 * wide * tokens)),
        name="project",
    )(xt, r1, *bufs)


def unit_rows(tokens, ones):
    row = lax.broadcasted_iota(jnp.int32, (16, tokens), 0)
    return jnp.where(row < ones, 1.0, 0.0).astype(BF16)


def causal(shape):
    j = lax.broadcasted_iota(jnp.int32, shape, 0)
    t = lax.broadcasted_iota(jnp.int32, shape, 1)
    return j <= t


def attend_kernel(rows, count, tab, q, k, v, att, den):
    h = pl.program_id(0)
    tokens = q.shape[1]
    one = unit_rows(tokens, 1)
    qa = jnp.concatenate([q[...] * jnp.asarray(F ** -0.5, BF16), one], axis=0)
    ka = jnp.concatenate([k[...], one], axis=0)
    va = jnp.concatenate([v[...], one], axis=0)
    below = causal((TB, TB))
    for b in range(tokens // TB):
        lo, hi = b * TB, (b + 1) * TB
        u = dot(ka[:, :hi], qa[:, lo:hi], TN)
        p = u * u + 1.0
        last = jnp.where(below, p[lo:], 0.0).astype(BF16)
        p = jnp.concatenate([p[:lo].astype(BF16), last], axis=0) if b else last
        o = dot(va[:, :hi], p)
        d = o[DV : DV + 1]
        done = o[:DV] / d
        den[0, :, lo:hi] = d
        for i in range(DV // rows):
            at = tab[count + h * (DV // rows) + i]
            att[pl.ds(pl.multiple_of(at * rows, rows), rows), lo:hi] = done[
                i * rows : (i + 1) * rows
            ].astype(att.dtype)


def head_specs(tokens):
    return [
        pl.BlockSpec((F, tokens), lambda h: (h, 0)),
        pl.BlockSpec((F, tokens), lambda h: (H + h, 0)),
        pl.BlockSpec((DV, tokens), lambda h: (2 * H * F // DV + h, 0)),
    ]


def attend(tab, qkv, rows, count, kind):
    tokens = qkv.shape[1]
    return pl.pallas_call(
        functools.partial(attend_kernel, rows, count),
        grid=(H,),
        out_shape=(sds((H * DV, tokens), kind), sds((H, 1, tokens), F32)),
        in_specs=[SMEM] + head_specs(tokens),
        out_specs=[
            pl.BlockSpec((H * DV, tokens), lambda h: (0, 0)),
            pl.BlockSpec((1, 1, tokens), lambda h: (h, 0, 0)),
        ],
        compiler_params=params(40),
        cost_estimate=cost(H * tokens * tokens * 256 * 2, 4 * H * DV * tokens * 2),
        name="attend",
    )(tab, qkv, qkv, qkv)


def middle_kernel(rows, count, tab, att, w0, w1, w2, w3, xt, gains, res, r2, x2t, x2, buf):
    width, tokens = xt.shape
    quarter = w0.shape[0]

    def tile(i, _):
        at = pl.multiple_of(i * 256, 256)
        acc = dot(w0[:, pl.ds(at, 256)], att[0:quarter, :], TN)
        for q, w in ((1, w1), (2, w2), (3, w3)):
            acc = acc + dot(w[:, pl.ds(at, 256)], att[q * quarter : (q + 1) * quarter, :], TN)
        buf[pl.ds(at, 256), :] = acc
        return 0

    lax.fori_loop(0, width // 256, tile, 0)

    def join(p, total):
        here = pl.ds(pl.multiple_of(p * rows, rows), rows)
        part = buf[pl.ds(pl.multiple_of(tab[p] * rows, rows), rows), :] + xt[here, :].astype(F32)
        res[here, :] = part
        return total + jnp.sum(part * part, axis=0, keepdims=True)

    total = lax.fori_loop(0, count, join, jnp.zeros((1, tokens), F32))
    scale = lax.rsqrt(total / width + EPS)
    r2[...] = scale

    def finish(i, _):
        at = pl.multiple_of(i * 128, 128)
        part = res[pl.ds(at, 128), :]
        low = (part * scale * gains[pl.ds(at, 128), 1:2].astype(F32)).astype(BF16)
        x2t[pl.ds(at, 128), :] = low
        x2[:, pl.ds(at, 128)] = low.T
        return 0

    lax.fori_loop(0, width // 128, finish, 0)


def middle(tab, att, bufs, xt, gains, rows, count):
    width, tokens = xt.shape
    return pl.pallas_call(
        functools.partial(middle_kernel, rows, count),
        out_shape=(
            sds((width, tokens), F32),
            sds((1, tokens), F32),
            sds((width, tokens), BF16),
            sds((tokens, width), BF16),
        ),
        in_specs=[SMEM] + [VMEM] * 7,
        out_specs=[VMEM] * 4,
        scratch_shapes=[pltpu.VMEM((width, tokens), F32)],
        compiler_params=params(48),
        cost_estimate=cost(2 * width * tokens * H * DV, 16 * width * tokens),
        name="middle",
    )(tab, att, *bufs, xt, gains)


def forward_kernel(x2, x2t, dy, dyt, w0, w1, w2, w3, hid, dgate, dup, send, keep):
    quarter = w0.shape[1]
    bufs = (w0, w1, w2, w3)

    def over(a, which):
        acc = dot(a[:, 0:quarter], w0[which])
        for q in range(1, 4):
            acc = acc + dot(a[:, q * quarter : (q + 1) * quarter], bufs[q][which])
        return acc

    gate = over(x2, 0)
    up = over(x2, 1)
    back = over(dy, 2)
    sig = 1.0 / (1.0 + jnp.exp(-gate))
    act = gate * sig
    h = (act * up).astype(BF16)
    dg = (back * up * sig * (1.0 + gate * (1.0 - sig))).astype(BF16)
    du = (back * act).astype(BF16)
    hid[...] = h
    dgate[...] = dg
    dup[...] = du
    half = keep.shape[1]
    for i, (a, b) in enumerate(((x2t, dg), (x2t, du), (dyt, h))):
        keep[i] = dot(a[:half, :], b).astype(BF16)
        send[i] = dot(a[half:, :], b).astype(BF16)


def forward_group(x2, x2t, dy, dyt, bufs):
    tokens, width = x2.shape
    cols = bufs[0].shape[-1]
    quarter = bufs[0].shape[1]
    col = pl.BlockSpec((tokens, TILE), lambda i: (0, i))
    return pl.pallas_call(
        forward_kernel,
        grid=(cols // TILE,),
        out_shape=(sds((tokens, cols), BF16),) * 3 + (sds((3, width // 2, cols), BF16),) * 2,
        in_specs=[VMEM] * 4 + [pl.BlockSpec((3, quarter, TILE), lambda i: (0, 0, i))] * 4,
        out_specs=[col] * 3 + [pl.BlockSpec((3, width // 2, TILE), lambda i: (0, 0, i))] * 2,
        compiler_params=params(40),
        cost_estimate=cost(12 * tokens * width * cols, 2 * (4 * tokens * width + 9 * width * cols)),
        name="forward_group",
    )(x2, x2t, dy, dyt, *bufs)


def group_layout(groups):
    tiles = [g // TILE for g in groups]
    starts = [sum(tiles[:i]) for i in range(len(tiles))]
    return tiles, starts


def pulled(groups, which, left_refs, weight_refs, acc):
    tiles, starts = group_layout(groups)
    step = pl.program_id(0)

    @pl.when(step == 0)
    def _():
        acc[...] = jnp.zeros_like(acc)

    for g in range(len(groups)):

        @pl.when((step >= starts[g]) & (step < starts[g] + tiles[g]))
        def _(g=g):
            for b in range(4):
                w = weight_refs[g * 4 + b]
                quarter = w.shape[1]
                part = acc[:, b * quarter : (b + 1) * quarter]
                for k in range(len(which)):
                    part = part + dot(left_refs[g * len(which) + k][...], w[k], NT)
                acc[:, b * quarter : (b + 1) * quarter] = part


def pull_specs(groups, first, many, tokens, quarter):
    tiles, starts = group_layout(groups)
    left, weights = [], []
    for g in range(len(groups)):
        col = functools.partial(
            lambda i, s, n: jnp.clip(i - s, 0, n - 1), s=starts[g], n=tiles[g]
        )
        left += [pl.BlockSpec((tokens, TILE), lambda i, col=col: (0, col(i)))] * many
        weights += [
            pl.BlockSpec(
                (many, quarter, TILE), lambda i, col=col: (first // many, 0, col(i))
            )
        ] * 4
    return left, weights


def back_kernel(groups, rows, count, tab, *refs):
    G = len(groups)
    lefts, weights = refs[: 2 * G], refs[2 * G : 6 * G]
    res, r2, yt, gains, dres, dm, acc, dmf = refs[6 * G :]
    pulled(groups, (0, 1), lefts, weights, acc)

    @pl.when(pl.program_id(0) == pl.num_programs(0) - 1)
    def _():
        tokens, width = acc.shape
        scale = r2[...]

        def first(i, total):
            at = pl.multiple_of(i * 128, 128)
            part = acc[:, pl.ds(at, 128)].T * gains[pl.ds(at, 128), 1:2].astype(F32)
            dres[pl.ds(at, 128), :] = part
            return total + jnp.sum(part * res[pl.ds(at, 128), :], axis=0, keepdims=True)

        total = lax.fori_loop(0, width // 128, first, jnp.zeros((1, tokens), F32))
        pull = total / width * scale * scale * scale

        def second(p, _):
            here = pl.ds(pl.multiple_of(p * rows, rows), rows)
            part = yt[here, :].astype(F32) + scale * dres[here, :] - res[here, :] * pull
            dres[here, :] = part
            dmf[pl.ds(pl.multiple_of(tab[p] * rows, rows), rows), :] = part.astype(dmf.dtype)
            return 0

        lax.fori_loop(0, count, second, 0)
        dm[...] = dmf[...].astype(BF16)


def back(tab, dgates, dups, bufs, res, r2, yt, gains, groups, rows, count, kind):
    width, tokens = res.shape
    quarter = width // 4
    cols = sum(groups)
    lefts = [a for pair in zip(dgates, dups) for a in pair]
    weights = [b for four in bufs for b in four]
    left, weight = pull_specs(groups, 0, 2, tokens, quarter)
    return pl.pallas_call(
        functools.partial(back_kernel, groups, rows, count),
        grid=(cols // TILE,),
        out_shape=(sds((width, tokens), F32), sds((width, tokens), BF16)),
        in_specs=[SMEM] + left + weight + [VMEM] * 4,
        out_specs=[VMEM] * 2,
        scratch_shapes=[pltpu.VMEM((tokens, width), F32), pltpu.VMEM((width, tokens), kind)],
        compiler_params=params(52),
        cost_estimate=cost(4 * tokens * width * cols, 8 * width * cols + 16 * width * tokens),
        name="back",
    )(tab, *lefts, *weights, res, r2, yt, gains)


def output_kernel(groups, rows, count, tab, *refs):
    G = len(groups)
    lefts, weights = refs[:G], refs[G : 5 * G]
    res, out, acc, nat = refs[5 * G :]
    pulled(groups, (2,), lefts, weights, acc)

    @pl.when(pl.program_id(0) == pl.num_programs(0) - 1)
    def _():
        tokens, width = acc.shape

        def first(i, _):
            at = pl.multiple_of(i * 128, 128)
            part = acc[:, pl.ds(at, 128)].T + res[pl.ds(at, 128), :]
            for k in range(128 // rows):
                to = tab[i * (128 // rows) + k]
                nat[pl.ds(pl.multiple_of(to * rows, rows), rows), :] = part[
                    k * rows : (k + 1) * rows
                ].astype(nat.dtype)
            return 0

        lax.fori_loop(0, width // 128, first, 0)

        def second(i, _):
            at = pl.multiple_of(i * 128, 128)
            out[:, pl.ds(at, 128)] = nat[pl.ds(at, 128), :].T.astype(BF16)
            return 0

        lax.fori_loop(0, width // 128, second, 0)


def output_of(tab, hids, bufs, res, groups, rows, count, kind):
    width, tokens = res.shape
    quarter = width // 4
    cols = sum(groups)
    weights = [b for four in bufs for b in four]
    left, weight = pull_specs(groups, 2, 1, tokens, quarter)
    return pl.pallas_call(
        functools.partial(output_kernel, groups, rows, count),
        grid=(cols // TILE,),
        out_shape=sds((tokens, width), BF16),
        in_specs=[SMEM] + left + weight + [VMEM],
        out_specs=VMEM,
        scratch_shapes=[pltpu.VMEM((tokens, width), F32), pltpu.VMEM((width, tokens), kind)],
        compiler_params=params(40),
        cost_estimate=cost(2 * tokens * width * cols, 4 * width * cols + 6 * width * tokens),
        name="output_of",
    )(tab, *hids, *weights, res)


def mixed_kernel(dm, att, w0, w1, w2, w3, send, keep, datt):
    quarter = w0.shape[0]
    half = keep.shape[0]
    for q, w in enumerate((w0, w1, w2, w3)):
        datt[q * quarter : (q + 1) * quarter, :] = dot(w[...], dm[...])

    def tile(i, _):
        at = pl.multiple_of(i * 256, 256)
        right = dm[pl.ds(at, 256), :]
        keep[:, pl.ds(at, 256)] = dot(att[:half, :], right, NT).astype(BF16)
        send[:, pl.ds(at, 256)] = dot(att[half:, :], right, NT).astype(BF16)
        return 0

    lax.fori_loop(0, dm.shape[0] // 256, tile, 0)


def mixed(dm, att, bufs):
    width, tokens = dm.shape
    rows = att.shape[0]
    return pl.pallas_call(
        mixed_kernel,
        out_shape=(sds((rows // 2, width), BF16),) * 2 + (sds((rows, tokens), F32),),
        in_specs=[VMEM] * 6,
        out_specs=[VMEM] * 3,
        compiler_params=params(40),
        cost_estimate=cost(4 * width * tokens * rows, 12 * width * tokens),
        name="mixed",
    )(dm, att, *bufs)


def attend_back_kernel(rows, count, tab, q, k, v, datt, att, den, dq, dk, dv, acc):
    h = pl.program_id(0)
    tokens = q.shape[1]
    scale = jnp.asarray(F ** -0.5, BF16)
    da, done = [], []
    for i in range(DV // rows):
        at = pl.multiple_of(tab[count + h * (DV // rows) + i] * rows, rows)
        da.append(datt[pl.ds(at, rows), :])
        done.append(att[pl.ds(at, rows), :].astype(F32))
    da = jnp.concatenate(da, axis=0) if len(da) > 1 else da[0]
    done = jnp.concatenate(done, axis=0) if len(done) > 1 else done[0]
    inv = 2.0 / den[0]
    dn = (da * inv).astype(BF16)
    dd = -jnp.sum(da * done, axis=0, keepdims=True) * inv
    dd_high = dd.astype(BF16).astype(F32)
    row = lax.broadcasted_iota(jnp.int32, (16, tokens), 0)
    tail = jnp.where(row == 0, dd_high, jnp.where(row == 1, dd - dd_high, 0.0)).astype(BF16)
    one = unit_rows(tokens, 1)
    qs = q[...] * scale
    ks = k[...] * scale
    qa = jnp.concatenate([qs, one], axis=0)
    ka = jnp.concatenate([k[...], one], axis=0)
    va = jnp.concatenate([v[...], unit_rows(tokens, 2)], axis=0)
    na = jnp.concatenate([dn, tail], axis=0)
    zero = jnp.zeros((DV, tokens), BF16)
    right_p = jnp.concatenate([dn * jnp.asarray(0.5, BF16), zero], axis=0).T
    right_s = jnp.concatenate([zero, qs, jnp.zeros((DV - F, tokens), BF16)], axis=0).T
    below = causal((TB, TB))
    for b in range(tokens // TB):
        lo, hi = b * TB, (b + 1) * TB
        u = dot(ka[:, :hi], qa[:, lo:hi], TN)
        g = dot(va[:, :hi], na[:, lo:hi], TN)
        p = u * u + 1.0
        s = g * u
        p_last = jnp.where(below, p[lo:], 0.0).astype(BF16)
        s_last = jnp.where(below, s[lo:], 0.0).astype(BF16)
        if b:
            p = jnp.concatenate([p[:lo].astype(BF16), p_last], axis=0)
            s = jnp.concatenate([s[:lo].astype(BF16), s_last], axis=0)
        else:
            p, s = p_last, s_last
        dq[:, lo:hi] = dot(ks[:, :hi], s).astype(BF16)
        both = dot(p, right_p[lo:hi]) + dot(s, right_s[lo:hi])
        if b:
            acc[:lo, :] = acc[:lo, :] + both[:lo]
        acc[lo:hi, :] = both[lo:]
    turned = acc[...].T
    dv[...] = turned[:DV].astype(BF16)
    dk[...] = turned[DV : DV + F].astype(BF16)


def attend_back(tab, qkv, datt, att, den, rows, count):
    tokens = qkv.shape[1]
    return pl.pallas_call(
        functools.partial(attend_back_kernel, rows, count),
        grid=(H,),
        out_shape=(
            sds((H * F, tokens), BF16),
            sds((H * F, tokens), BF16),
            sds((H * DV, tokens), BF16),
        ),
        in_specs=[SMEM]
        + head_specs(tokens)
        + [VMEM, VMEM, pl.BlockSpec((1, 1, tokens), lambda h: (h, 0, 0))],
        out_specs=[
            pl.BlockSpec((F, tokens), lambda h: (h, 0)),
            pl.BlockSpec((F, tokens), lambda h: (h, 0)),
            pl.BlockSpec((DV, tokens), lambda h: (h, 0)),
        ],
        scratch_shapes=[pltpu.VMEM((tokens, 2 * DV), F32)],
        compiler_params=params(40),
        cost_estimate=cost(H * tokens * tokens * 256 * 6, 8 * H * DV * tokens * 2),
        name="attend_back",
    )(tab, qkv, qkv, qkv, datt, att, den)


def weights_kernel(normed, dq, dk, dv, send, keep):
    half = keep.shape[0]
    at = 0
    for ref in (dq, dk, dv):
        for i in range(ref.shape[0] // 256):
            right = ref[i * 256 : (i + 1) * 256, :]
            keep[:, at : at + 256] = dot(normed[:half, :], right, NT).astype(BF16)
            send[:, at : at + 256] = dot(normed[half:, :], right, NT).astype(BF16)
            at += 256


def weights_of(normed, dq, dk, dv):
    width, tokens = normed.shape
    wide = dq.shape[0] + dk.shape[0] + dv.shape[0]
    return pl.pallas_call(
        weights_kernel,
        out_shape=(sds((width // 2, wide), BF16),) * 2,
        in_specs=[VMEM] * 4,
        out_specs=[VMEM] * 2,
        compiler_params=params(32),
        cost_estimate=cost(2 * width * tokens * wide, 6 * width * tokens + 4 * width * wide),
        name="weights_of",
    )(normed, dq, dk, dv)


def input_kernel(rows, count, tab, dq, dk, dv, w0, w1, w2, w3, gains, dres, xt, r1, out, buf, nat):
    width, tokens = xt.shape
    quarter = w0.shape[0]
    a, b, c = dq.shape[0], dk.shape[0], dv.shape[0]
    total = jnp.zeros((1, tokens), F32)
    scale = r1[...]
    for q, w in enumerate((w0, w1, w2, w3)):
        here = slice(q * quarter, (q + 1) * quarter)
        part = dot(w[:, :a], dq[...]) + dot(w[:, a : a + b], dk[...])
        part = part + dot(w[:, a + b : a + b + c], dv[...])
        part = part * gains[here, 0:1].astype(F32)
        buf[here, :] = part
        total = total + jnp.sum(part * xt[here, :].astype(F32), axis=0, keepdims=True)
    pull = total / width * scale * scale * scale

    def second(p, _):
        here = pl.ds(pl.multiple_of(p * rows, rows), rows)
        part = dres[here, :] + scale * buf[here, :] - xt[here, :].astype(F32) * pull
        nat[pl.ds(pl.multiple_of(tab[p] * rows, rows), rows), :] = part.astype(nat.dtype)
        return 0

    lax.fori_loop(0, count, second, 0)

    def third(i, _):
        at = pl.multiple_of(i * 128, 128)
        out[:, pl.ds(at, 128)] = nat[pl.ds(at, 128), :].T.astype(BF16)
        return 0

    lax.fori_loop(0, width // 128, third, 0)


def input_of(tab, dq, dk, dv, bufs, gains, dres, xt, r1, rows, count, kind):
    width, tokens = xt.shape
    wide = dq.shape[0] + dk.shape[0] + dv.shape[0]
    return pl.pallas_call(
        functools.partial(input_kernel, rows, count),
        out_shape=sds((tokens, width), BF16),
        in_specs=[SMEM] + [VMEM] * 11,
        out_specs=VMEM,
        scratch_shapes=[pltpu.VMEM((width, tokens), F32), pltpu.VMEM((width, tokens), kind)],
        compiler_params=params(48),
        cost_estimate=cost(2 * width * tokens * wide, 12 * width * tokens + 2 * wide * tokens),
        name="input_of",
    )(tab, dq, dk, dv, *bufs, gains, dres, xt, r1)


def split_columns(total):
    tiles = -(-total // TILE)
    first = -(-tiles // 3)
    second = -(-(tiles - first) // 2)
    return [n * TILE for n in (first, second, tiles - first - second)]


def per_device(
    inputs, w_query, w_key, w_value, w_out, w_gate, w_up, w_down, gain_one, gain_two, cotangent
):
    dp = lax.axis_size("dp")
    bits = dp.bit_length() - 1
    count = 2 * dp
    micro, _, half, width = inputs.shape
    rows = width // count
    kind = BF16 if rows % 16 == 0 else F32
    hidden = w_gate.shape[1]
    groups = split_columns(hidden)
    padded = sum(groups)
    tab, core = block_tables(dp, bits)
    swap = core_pairs(dp)

    x = inputs.reshape(micro, half, width)
    y = cotangent.reshape(micro, half, width)
    x_sent = lax.dynamic_index_in_dim(x, 1 - core, 0, keepdims=False)
    y_sent = lax.dynamic_index_in_dim(y, 1 - core, 0, keepdims=False)
    x_came = lax.ppermute(x_sent, AXES, swap)
    y_came = lax.ppermute(y_sent, AXES, swap)

    wide = w_query.shape[1] + w_key.shape[1] + w_value.shape[1]
    pair = jnp.pad(jnp.stack([gain_one, gain_two], axis=1), ((0, 0), (0, 126)))
    own_qkv = jnp.concatenate([w_query, w_key, w_value], axis=1)
    qkv_bufs = gather(jnp.concatenate([own_qkv, pair], axis=1), dp, bits)
    out_bufs = gather(w_out, dp, bits)
    fill = ((0, 0), (0, padded - hidden))
    ff_own = jnp.stack([jnp.pad(w_gate, fill), jnp.pad(w_up, fill), jnp.pad(w_down.T, fill)])
    ff_bufs, at = [], 0
    for n in groups:
        ff_bufs.append(gather(ff_own[:, :, at : at + n], dp, bits))
        at += n

    xt, r1, yt, yn = pre(tab, x, x_came, y, y_came, rows, count, kind)
    xt, yt_low = xt.astype(BF16), yt.astype(BF16)
    gains = jnp.concatenate([b[:, wide:] for b in qkv_bufs], axis=0)
    normed, qkv = project(xt, r1, qkv_bufs, wide)
    att_any, den = attend(tab, qkv, rows, count, kind)
    att = att_any.astype(BF16)
    res, r2, x2t, x2 = middle(tab, att, out_bufs, xt, gains, rows, count)
    hids, dgates, dups, ff_grads = [], [], [], []
    for bufs in ff_bufs:
        hid, dgate, dup, send, keep = forward_group(x2, x2t, yn, yt_low, bufs)
        hids.append(hid)
        dgates.append(dgate)
        dups.append(dup)
        ff_grads.append(reduce_rows(keep, send, dp, bits))
    dres, dm = back(tab, dgates, dups, ff_bufs, res, r2, yt_low, gains, groups, rows, count, kind)
    send, keep, datt = mixed(dm, att, out_bufs)
    grad_out = reduce_rows(keep, send, dp, bits)
    dq, dk, dv = attend_back(tab, qkv, datt, att_any, den, rows, count)
    send, keep = weights_of(normed, dq, dk, dv)
    grad_qkv = reduce_rows(keep, send, dp, bits)
    output = output_of(tab, hids, ff_bufs, res, groups, rows, count, kind)
    dx = input_of(tab, dq, dk, dv, qkv_bufs, gains, dres, xt, r1, rows, count, kind)

    def give_back(value):
        mine = lax.dynamic_slice_in_dim(value, core * half, half, 0)
        other = lax.dynamic_slice_in_dim(value, (1 - core) * half, half, 0)
        came = lax.ppermute(other, AXES, swap)
        both = jnp.where(core == 0, jnp.stack([mine, came]), jnp.stack([came, mine]))
        return both.reshape(micro, 1, half, width)

    ff = jnp.concatenate(ff_grads, axis=-1)[:, :, :hidden]
    a, b = w_query.shape[1], w_query.shape[1] + w_key.shape[1]
    gain_one_grad = jnp.sum(own_qkv.astype(F32) * grad_qkv, axis=1) / gain_one.astype(F32)
    gain_two_grad = (
        jnp.sum(w_gate.astype(F32) * ff[0] + w_up.astype(F32) * ff[1], axis=1)
    ) / gain_two.astype(F32)
    return (
        give_back(output),
        give_back(dx),
        grad_qkv[:, :a],
        grad_qkv[:, a:b],
        grad_qkv[:, b:],
        grad_out,
        ff[0],
        ff[1],
        ff[2].T,
        gain_one_grad,
        gain_two_grad,
    )


def solution(mesh):
    shard = P(AXES, None)
    batch = P(None, "dp", "seq", None)
    return jax.shard_map(
        per_device,
        mesh=mesh,
        in_specs=(batch,) + (shard,) * 6 + (P(None, AXES), P(AXES), P(AXES), batch),
        out_specs=(batch,) * 2 + (shard,) * 6 + (P(None, AXES), P(AXES), P(AXES)),
        check_vma=False,
    )
```

```python
import functools

import jax
import jax.numpy as jnp
import numpy as np
from jax import lax
from jax.experimental import pallas as pl
from jax.experimental.pallas import tpu as pltpu
from jax.sharding import PartitionSpec as P

H = 16
F = 16
DV = 64
AXES = ("dp", "seq")
EPS = 1e-06
TB = 256
HEADS = 2
BACK_HEADS = 2
BACK_PARTS = 4
TILE = 256
F32 = jnp.float32
BF16 = jnp.bfloat16

NN = (((1,), (0,)), ((), ()))
NT = (((1,), (1,)), ((), ()))
TN = (((0,), (0,)), ((), ()))


def dot(a, b, dims=NN):
    return lax.dot_general(a, b, dims, preferred_element_type=F32)


VMEM = pl.BlockSpec(memory_space=pltpu.VMEM)
SMEM = pl.BlockSpec(memory_space=pltpu.SMEM)


def params(mib):
    return pltpu.CompilerParams(vmem_limit_bytes=mib << 20)


def cost(flops, nbytes, trans=0):
    return pl.CostEstimate(flops=int(flops), bytes_accessed=int(nbytes), transcendentals=int(trans))


def sds(shape, dtype):
    return jax.ShapeDtypeStruct(shape, dtype)


def far(shape, dtype):
    return pltpu.HBM(shape, dtype)


def keep_far(*values):
    return [pltpu.with_memory_space_constraint(v, pltpu.HBM) for v in values]


def stage_orders(bits):
    straight = list(range(bits))
    swapped = [1, 0] + list(range(2, bits)) if bits > 1 else straight
    return (straight, swapped)


def stage_pairs(dp, bits, stage):
    orders = stage_orders(bits)
    return [
        (d * 2 + c, (d ^ (1 << orders[c][stage])) * 2 + c) for d in range(dp) for c in range(2)
    ]


def core_pairs(dp):
    return [(i, i ^ 1) for i in range(2 * dp)]


def far_groups(dp, bits):
    many = dp >> 2
    order = []
    for q in range(many):
        d = 0
        for stage in range(2, bits):
            d |= ((q >> (bits - 1 - stage)) & 1) << stage
        order.append(d)
    return [[low + d for d in order] for low in range(4)]


def block_tables(dp, bits):
    orders = stage_orders(bits)
    count = 2 * dp
    position = np.arange(count)
    masks, fixed = [], np.zeros(count, np.int32)
    for c in range(2):
        mask = np.zeros(count, np.int32)
        for stage in range(2):
            mask |= ((position >> (bits - 1 - stage)) & 1) << orders[c][stage]
        masks.append(mask)
    for stage in range(2, bits):
        fixed |= ((position >> (bits - 1 - stage)) & 1) << stage
    d = lax.axis_index("dp").astype(jnp.int32)
    c = lax.axis_index("seq").astype(jnp.int32)
    owner_core = jnp.asarray(position >> bits, jnp.int32) ^ c
    mask = jnp.where(owner_core == 0, jnp.asarray(masks[0]), jnp.asarray(masks[1]))
    block_at = (((d & 3) ^ mask) | jnp.asarray(fixed)) * 2 + owner_core
    block_core = jnp.asarray(position & 1, jnp.int32)
    owner = position >> 1
    low = np.zeros(count, np.int32)
    for stage in range(2, bits):
        low |= ((owner >> stage) & 1) << (bits - 1 - stage)
    apart = jnp.asarray(owner & 3, jnp.int32) ^ (d & 3)
    places = []
    for k in range(2):
        place = jnp.asarray(low)
        for stage in range(2):
            place = place | (((apart >> orders[k][stage]) & 1) << (bits - 1 - stage))
        places.append(place)
    place_of = jnp.where(block_core == 0, places[0], places[1]) | ((block_core ^ c) << bits)
    return jnp.concatenate([block_at, place_of, c[None], jnp.zeros(7, jnp.int32)]), c


class Plan:
    def __init__(self, dp, bits):
        self.dp, self.bits = dp, bits
        self.live, self.parts, self.air = {}, {}, {}

    def fence(self):
        self.live.update(lax.optimization_barrier(dict(self.live)))
        self.live.update(self.air)
        self.air = {}

    def pairs(self, stage):
        return core_pairs(self.dp) if stage < 0 else stage_pairs(self.dp, self.bits, stage)

    def send(self, value, stage):
        return lax.ppermute(value, AXES, self.pairs(stage))

    def gather(self, name, shard):
        self.live[name] = shard

    def bit(self, stage):
        return (lax.axis_index("dp") >> stage) & 1

    def double(self, name, stage, long=False):
        live = self.live
        if 0 <= stage < self.bits - 1:
            self.join(name, stage + 1)
        if stage >= 0:
            (self.air if long else live)[name + "+"] = self.send(live[name], stage)
        else:
            live[name + "-"] = self.send(live[name], -1)
            live[name + "-+"] = self.send(live[name + "+"], -1)

    def join(self, name, stage):
        held, came = self.live[name], self.live.pop(name + "+")
        if stage >= 2:
            first = self.bit(stage) == 0
            held, came = jnp.where(first, held, came), jnp.where(first, came, held)
        self.live[name] = jnp.concatenate([held, came], axis=-2)

    def gathered(self, name):
        return tuple(self.live[name + end] for end in ("", "+", "-", "-+"))

    def reduce(self, name, send, keep):
        self.live[name + ".send"], self.live[name] = send, keep
        self.parts[name] = [(name, 0)]

    def halve(self, name, stage, long=False):
        live = self.live
        if stage < 0:
            send = live.pop(name + ".send")
        else:
            half = live[name].shape[-2] >> (stage + 1)
            parts = self.parts[name]
            if stage < 2:
                send = self.total(parts, half, half)
            else:
                bit = self.bit(stage)
                send = self.total(parts, (1 - bit) * half, half)
                self.parts[name] = [(key, off + bit * half) for key, off in parts]
            send = send.astype(BF16)
        key = f"{name}.{stage}"
        (self.air if long else live)[key] = self.send(send, stage)
        self.parts[name] = self.parts[name] + [(key, 0)]

    def total(self, parts, start, size):
        acc = None
        for key, off in parts:
            part = self.live[key]
            part = lax.dynamic_slice_in_dim(part, off + start, size, axis=part.ndim - 2)
            acc = part.astype(F32) if acc is None else acc + part.astype(F32)
        return acc

    def reduced(self, name):
        return self.total(self.parts[name], 0, self.live[name].shape[-2] >> self.bits)

    def scatter_far(self, name, key):
        part = self.total(self.parts[name], 0, self.live[name].shape[-2] >> 2).astype(BF16)
        for piece, _ in self.parts.pop(name):
            self.live.pop(piece)
        self.air[key] = lax.psum_scatter(
            part,
            "dp",
            scatter_dimension=part.ndim - 2,
            axis_index_groups=far_groups(self.dp, self.bits),
            tiled=True,
        )


def pre_kernel(rows, count, blocks, tab, x, xr, y, yr, xt, r1, yt, yn, buf):
    own = pl.program_id(0) // blocks == tab[2 * count]
    width = xt.shape[0]
    total = jnp.zeros(r1.shape, F32)
    for src, rec, dst in ((x, xr, xt), (y, yr, yt)):
        for i in range(width // 256):
            here = slice(i * 256, (i + 1) * 256)
            part = jnp.where(own, src[0, :, here], rec[:, here]).T
            buf[here, :] = part.astype(buf.dtype)
            if src is x:
                wide = part.astype(F32)
                total = total + jnp.sum(wide * wide, axis=0, keepdims=True)

        def move(p, _):
            at = pl.multiple_of(tab[p] * rows, rows)
            dst[pl.ds(pl.multiple_of(p * rows, rows), rows), :] = buf[pl.ds(at, rows), :]
            return 0

        lax.fori_loop(0, count, move, 0, unroll=4)
    for i in range(width // 256):
        here = slice(i * 256, (i + 1) * 256)
        yn[:, here] = yt[here, :].T.astype(BF16)
    r1[...] = lax.rsqrt(total / width + EPS)


def pre(tab, x, xr, y, yr, rows, count, kind):
    half, width = xr.shape
    tokens = 2 * half
    blocks = half // TB
    own = pl.BlockSpec((1, TB, width), lambda i, tab: (tab[2 * count], i % blocks, 0))
    came = pl.BlockSpec((TB, width), lambda i, tab: (i % blocks, 0))
    turned = pl.BlockSpec((width, TB), lambda i, tab: (0, i))
    return pl.pallas_call(
        functools.partial(pre_kernel, rows, count, blocks),
        grid_spec=pltpu.PrefetchScalarGridSpec(
            num_scalar_prefetch=1,
            grid=(tokens // TB,),
            in_specs=[own, came, own, came],
            out_specs=[
                turned,
                pl.BlockSpec((1, TB), lambda i, tab: (0, i)),
                turned,
                pl.BlockSpec((TB, width), lambda i, tab: (i, 0)),
            ],
            scratch_shapes=[pltpu.VMEM((width, TB), kind)],
        ),
        out_shape=(
            sds((width, tokens), kind),
            sds((1, tokens), F32),
            sds((width, tokens), kind),
            sds((tokens, width), BF16),
        ),
        compiler_params=params(14),
        cost_estimate=cost(8 * width * tokens, 14 * width * tokens),
        name="pre",
    )(tab, x, xr, y, yr)


def project_kernel(xt, r1, gains, w0, w1, w2, w3, normed, out):
    quarter = w0.shape[0]

    @pl.when(pl.program_id(0) == 0)
    def _():
        for q in range(4):
            here = slice(q * quarter, (q + 1) * quarter)
            part = xt[here, :].astype(F32) * r1[...] * gains[here, 0:1].astype(F32)
            normed[here, :] = part.astype(BF16)

    acc = dot(w0[...], normed[0:quarter, :], TN)
    for q, w in ((1, w1), (2, w2), (3, w3)):
        acc = acc + dot(w[...], normed[q * quarter : (q + 1) * quarter, :], TN)
    out[...] = acc.astype(BF16)


def project(xt, r1, gains, bufs, wide):
    width, tokens = xt.shape
    quarter = bufs[0].shape[0]
    return pl.pallas_call(
        project_kernel,
        grid=(wide // 256,),
        out_shape=(sds((width, tokens), BF16), sds((wide, tokens), BF16)),
        in_specs=[
            pl.BlockSpec((width, tokens), lambda i: (0, 0), pipeline_mode=pl.Buffered(1)),
            pl.BlockSpec((1, tokens), lambda i: (0, 0)),
            pl.BlockSpec((width, 128), lambda i: (0, 0)),
        ]
        + [pl.BlockSpec((quarter, 256), lambda i: (0, i))] * 4,
        out_specs=[
            pl.BlockSpec((width, tokens), lambda i: (0, 0)),
            pl.BlockSpec((256, tokens), lambda i: (i, 0)),
        ],
        compiler_params=params(16),
        cost_estimate=cost(2 * width * tokens * wide, 2 * (2 * width * tokens + 2 * wide * tokens)),
        name="project",
    )(xt, r1, gains, *keep_far(*bufs))


def unit_rows(tokens, ones):
    row = lax.broadcasted_iota(jnp.int32, (16, tokens), 0)
    return jnp.where(row < ones, 1.0, 0.0).astype(BF16)


def causal(shape):
    j = lax.broadcasted_iota(jnp.int32, shape, 0)
    t = lax.broadcasted_iota(jnp.int32, shape, 1)
    return j <= t


def attend_kernel(rows, count, tab, q, k, v, att, den):
    tokens = q.shape[1]
    blocks = tokens // TB
    one = unit_rows(tokens, 1)
    below = causal((TB, TB))
    heads = range(q.shape[0] // F)
    us, vas = [], []
    for n in heads:
        qa = q[n * F : (n + 1) * F, :] * jnp.asarray(F ** -0.5, BF16)
        qa = jnp.concatenate([qa, one], axis=0)
        ka = jnp.concatenate([k[n * F : (n + 1) * F, :], one], axis=0)
        vas.append(jnp.concatenate([v[n * DV : (n + 1) * DV, :], one], axis=0))
        us.append(
            [dot(ka[:, : (b + 1) * TB], qa[:, b * TB : (b + 1) * TB], TN) for b in range(blocks)]
        )
    ps = []
    for n in heads:
        ps.append([])
        for b in range(blocks):
            lo = b * TB
            p = us[n][b] * us[n][b] + 1.0
            last = jnp.where(below, p[lo:], 0.0).astype(BF16)
            ps[n].append(jnp.concatenate([p[:lo].astype(BF16), last], axis=0) if b else last)
    for n in heads:
        h = pl.program_id(0) * len(heads) + n
        for b in range(blocks):
            lo, hi = b * TB, (b + 1) * TB
            o = dot(vas[n][:, :hi], ps[n][b])
            d = o[DV : DV + 1]
            done = o[:DV] / d
            den[n, :, lo:hi] = d
            for i in range(DV // rows):
                at = tab[count + h * (DV // rows) + i]
                att[pl.ds(pl.multiple_of(at * rows, rows), rows), lo:hi] = done[
                    i * rows : (i + 1) * rows
                ].astype(att.dtype)


def head_specs(tokens, heads, off=0):
    return [
        pl.BlockSpec((F * heads, tokens), lambda h, *_: (off + h, 0)),
        pl.BlockSpec((F * heads, tokens), lambda h, *_: (H // heads + off + h, 0)),
        pl.BlockSpec((DV * heads, tokens), lambda h, *_: (2 * H * F // DV // heads + off + h, 0)),
    ]


def attend(tab, qkv, rows, count, kind):
    tokens = qkv.shape[1]
    heads = HEADS
    return pl.pallas_call(
        functools.partial(attend_kernel, rows, count),
        grid=(H // heads,),
        out_shape=(sds((H * DV, tokens), kind), sds((H, 1, tokens), F32)),
        in_specs=[SMEM] + head_specs(tokens, heads),
        out_specs=[
            pl.BlockSpec((H * DV, tokens), lambda h: (0, 0)),
            pl.BlockSpec((heads, 1, tokens), lambda h: (h, 0, 0)),
        ],
        compiler_params=params(28),
        cost_estimate=cost(H * tokens * tokens * 256 * 2, 4 * H * DV * tokens * 2),
        name="attend",
    )(tab, qkv, qkv, qkv)


def middle_kernel(rows, count, tab, w0, w1, w2, w3, att, xt, gains, res, r2, x2t, x2, wt, buf):
    width, tokens = xt.shape
    quarter = w0.shape[0]

    @pl.when(pl.program_id(0) == 0)
    def _():
        for q, w in enumerate((w0, w1, w2, w3)):
            for i in range(width // 256):
                wt[i * 256 : (i + 1) * 256, q * quarter : (q + 1) * quarter] = w[
                    :, i * 256 : (i + 1) * 256
                ].T

    buf[...] = dot(wt[...], att[...])

    def join(p, total):
        here = pl.ds(pl.multiple_of(p * rows, rows), rows)
        part = buf[pl.ds(pl.multiple_of(tab[p] * rows, rows), rows), :] + xt[here, :].astype(F32)
        res[here, :] = part
        return total + jnp.sum(part * part, axis=0, keepdims=True)

    total = lax.fori_loop(0, count, join, jnp.zeros((1, tokens), F32), unroll=4)
    scale = lax.rsqrt(total / width + EPS)
    r2[...] = scale
    for i in range(width // 256):
        here = slice(i * 256, (i + 1) * 256)
        low = (res[here, :] * scale * gains[here, 1:2].astype(F32)).astype(BF16)
        x2t[here, :] = low
        x2[:, here] = low.T


def middle(tab, att, bufs, xt, gains, rows, count):
    width, tokens = xt.shape
    inner = att.shape[0]
    quarter = bufs[0].shape[0]
    once = pl.BlockSpec((quarter, width), lambda i: (0, 0), pipeline_mode=pl.Buffered(1))
    return pl.pallas_call(
        functools.partial(middle_kernel, rows, count),
        grid=(tokens // TB,),
        out_shape=(
            far((width, tokens), F32),
            sds((1, tokens), F32),
            sds((width, tokens), BF16),
            sds((tokens, width), BF16),
        ),
        in_specs=[SMEM]
        + [once] * 4
        + [
            pl.BlockSpec((inner, TB), lambda i: (0, i)),
            pl.BlockSpec((width, TB), lambda i: (0, i)),
            pl.BlockSpec((width, 128), lambda i: (0, 0)),
        ],
        out_specs=[
            pl.BlockSpec((width, TB), lambda i: (0, i)),
            pl.BlockSpec((1, TB), lambda i: (0, i)),
            pl.BlockSpec((width, TB), lambda i: (0, i)),
            pl.BlockSpec((TB, width), lambda i: (i, 0)),
        ],
        scratch_shapes=[pltpu.VMEM((width, inner), BF16), pltpu.VMEM((width, TB), F32)],
        compiler_params=params(22),
        cost_estimate=cost(2 * width * tokens * inner, 16 * width * tokens),
        name="middle",
    )(tab, *keep_far(*bufs), att, *keep_far(xt), gains)


def feed_kernel(first, x2, x2t, dy, dyt, w0, w1, w2, w3, *refs):
    send, keep, pull, push = refs[-4:]
    quarter = w0.shape[1]
    bufs = (w0, w1, w2, w3)
    half = keep.shape[1]

    if first:

        @pl.when(pl.program_id(0) == 0)
        def _():
            pull[...] = jnp.zeros_like(pull)
            push[...] = jnp.zeros_like(push)

    def over(a, which):
        acc = dot(a[:, 0:quarter], w0[which])
        for q in range(1, 4):
            acc = acc + dot(a[:, q * quarter : (q + 1) * quarter], bufs[q][which])
        return acc

    def grad(i, a, b):
        whole = dot(a[...], b).astype(BF16)
        keep[i] = whole[:half]
        send[i] = whole[half:]

    gate = over(x2, 0)
    up = over(x2, 1)
    sig = 0.5 * jnp.tanh(0.5 * gate) + 0.5
    act = gate * sig
    h = (act * up).astype(BF16)
    back = over(dy, 2)
    dg = (back * up * (sig + act * (1.0 - sig))).astype(BF16)
    du = (back * act).astype(BF16)
    ht, dgt, dut = h.T, dg.T, du.T
    grad(2, dyt, h)
    for q, w in enumerate(bufs):
        here = slice(q * quarter, (q + 1) * quarter)
        push[here, :] = push[here, :] + dot(w[2], ht)
    grad(0, x2t, dg)
    grad(1, x2t, du)
    for q, w in enumerate(bufs):
        here = slice(q * quarter, (q + 1) * quarter)
        pull[here, :] = pull[here, :] + (dot(w[0], dgt) + dot(w[1], dut))


def feed(x2, x2t, dy, dyt, bufs, sums, slots=3):
    tokens, width = x2.shape
    cols = bufs[0].shape[-1]
    quarter = bufs[0].shape[1]
    return pl.pallas_call(
        functools.partial(feed_kernel, not sums),
        grid=(cols // TILE,),
        out_shape=(far((slots, width // 2, cols), BF16),) * 2 + (sds((width, tokens), F32),) * 2,
        in_specs=[VMEM] * 4
        + [pl.BlockSpec((3, quarter, TILE), lambda i: (0, 0, i))] * 4
        + [VMEM] * len(sums),
        out_specs=[pl.BlockSpec((3, width // 2, TILE), lambda i: (0, 0, i))] * 2 + [VMEM] * 2,
        input_output_aliases={8: 2, 9: 3} if sums else {},
        compiler_params=params(26),
        cost_estimate=cost(18 * tokens * width * cols, 2 * (4 * tokens * width + 9 * width * cols)),
        name="feed",
    )(x2, x2t, dy, dyt, *keep_far(*bufs), *sums)


def back_kernel(rows, count, tab, pull, res, r2, yt, gains, dres, dm, acc):
    width, tokens = acc.shape
    part = pull[...] * gains[:, 1:2].astype(F32)
    acc[...] = part
    total = jnp.sum(part * res[...], axis=0, keepdims=True)
    scale = r2[...]
    side = total / width * scale * scale * scale

    def second(p, _):
        here = pl.ds(pl.multiple_of(p * rows, rows), rows)
        part = yt[here, :].astype(F32) + scale * acc[here, :] - res[here, :] * side
        dres[here, :] = part
        dm[pl.ds(pl.multiple_of(tab[p] * rows, rows), rows), :] = part.astype(dm.dtype)
        return 0

    lax.fori_loop(0, count, second, 0, unroll=4)


def back(tab, pull, res, r2, yt, gains, rows, count, kind):
    width, tokens = res.shape
    block = pl.BlockSpec((width, TB), lambda i: (0, i))
    return pl.pallas_call(
        functools.partial(back_kernel, rows, count),
        grid=(tokens // TB,),
        out_shape=(far((width, tokens), F32), sds((width, tokens), kind)),
        in_specs=[
            SMEM,
            block,
            block,
            pl.BlockSpec((1, TB), lambda i: (0, i)),
            block,
            pl.BlockSpec((width, 128), lambda i: (0, 0)),
        ],
        out_specs=[block] * 2,
        scratch_shapes=[pltpu.VMEM((width, TB), F32)],
        compiler_params=params(20),
        cost_estimate=cost(10 * tokens * width, 16 * width * tokens),
        name="back",
    )(tab, pull, *keep_far(res), r2, *keep_far(yt), gains)


def output_kernel(rows, count, tab, push, res, out, acc, nat):
    width, tokens = acc.shape
    acc[...] = push[...] + res[...]

    def move(p, _):
        here = pl.ds(pl.multiple_of(p * rows, rows), rows)
        to = pl.ds(pl.multiple_of(tab[p] * rows, rows), rows)
        nat[to, :] = acc[here, :].astype(nat.dtype)
        return 0

    lax.fori_loop(0, count, move, 0, unroll=4)
    for i in range(width // 256):
        here = slice(i * 256, (i + 1) * 256)
        out[:, here] = nat[here, :].T.astype(BF16)


def output_of(tab, push, res, rows, count, kind):
    width, tokens = res.shape
    block = pl.BlockSpec((width, TB), lambda i: (0, i))
    return pl.pallas_call(
        functools.partial(output_kernel, rows, count),
        grid=(tokens // TB,),
        out_shape=sds((tokens, width), BF16),
        in_specs=[SMEM, block, block],
        out_specs=pl.BlockSpec((TB, width), lambda i: (i, 0)),
        scratch_shapes=[pltpu.VMEM((width, TB), F32), pltpu.VMEM((width, TB), kind)],
        compiler_params=params(16),
        cost_estimate=cost(tokens * width, 10 * width * tokens),
        name="output_of",
    )(tab, *keep_far(push, res))


def mixed_kernel(dm, dm_rows, att, w0, w1, w2, w3, send_in, keep_in, send, keep, datt):
    quarter = w0.shape[0]
    half = keep.shape[1]
    right = dm[...]
    for q, w in enumerate((w0, w1, w2, w3)):
        datt[q * quarter : (q + 1) * quarter, :] = dot(w[...], right)
    whole = dot(att[...], dm_rows[...], NT).astype(BF16)
    keep[0] = whole[:half]
    send[0] = whole[half:]


def mixed(dm, att, bufs, send, keep):
    width, tokens = dm.shape
    rows = att.shape[0]
    quarter = bufs[0].shape[0]
    slot = keep.shape[0] - 1
    cols = width * TB // tokens
    return pl.pallas_call(
        mixed_kernel,
        grid=(tokens // TB,),
        out_shape=(far(send.shape, BF16), far(keep.shape, BF16), far((rows, tokens), F32)),
        in_specs=[
            pl.BlockSpec((width, TB), lambda i: (0, i)),
            pl.BlockSpec((cols, tokens), lambda i: (i, 0)),
            pl.BlockSpec((rows, tokens), lambda i: (0, 0), pipeline_mode=pl.Buffered(1)),
        ]
        + [pl.BlockSpec((quarter, width), lambda i: (0, 0), pipeline_mode=pl.Buffered(1))] * 4
        + [pl.BlockSpec(memory_space=pl.ANY)] * 2,
        out_specs=[pl.BlockSpec((1, rows // 2, cols), lambda i: (slot, 0, i))] * 2
        + [pl.BlockSpec((rows, TB), lambda i: (0, i))],
        input_output_aliases={7: 0, 8: 1},
        compiler_params=params(18),
        cost_estimate=cost(4 * width * tokens * rows, 12 * width * tokens),
        name="mixed",
    )(dm, dm, att, *keep_far(*bufs, send, keep))


def attend_back_kernel(rows, tab, q, k, v, den, *refs):
    many = q.shape[0] // F * (DV // rows)
    datts, atts = refs[:many], refs[many : 2 * many]
    dq, dk, dv, pt, st = refs[2 * many :]
    tokens = q.shape[1]
    blocks = tokens // TB
    scale = jnp.asarray(F ** -0.5, BF16)
    row = lax.broadcasted_iota(jnp.int32, (16, tokens), 0)
    one = unit_rows(tokens, 1)
    two = unit_rows(tokens, 2)
    zero = jnp.zeros((DV, tokens), BF16)
    below = causal((TB, TB))
    heads = range(q.shape[0] // F)
    us, gs, kss, rights_p, rights_s = [], [], [], [], []
    for n in heads:
        here = slice(n * (DV // rows), (n + 1) * (DV // rows))
        da = jnp.concatenate([r[...] for r in datts[here]], axis=0)
        done = jnp.concatenate([r[...].astype(F32) for r in atts[here]], axis=0)
        inv = 2.0 / den[n]
        dn = (da * inv).astype(BF16)
        dd = -jnp.sum(da * done, axis=0, keepdims=True) * inv
        dd_high = dd.astype(BF16).astype(F32)
        tail = jnp.where(row == 0, dd_high, jnp.where(row == 1, dd - dd_high, 0.0)).astype(BF16)
        qh, kh = q[n * F : (n + 1) * F, :], k[n * F : (n + 1) * F, :]
        qs = qh * scale
        kss.append(kh * scale)
        qa = jnp.concatenate([qs, one], axis=0)
        ka = jnp.concatenate([kh, one], axis=0)
        va = jnp.concatenate([v[n * DV : (n + 1) * DV, :], two], axis=0)
        na = jnp.concatenate([dn, tail], axis=0)
        rights_p.append(jnp.concatenate([dn * jnp.asarray(0.5, BF16), zero], axis=0).T)
        rights_s.append(jnp.concatenate([zero, qs, jnp.zeros((DV - F, tokens), BF16)], axis=0).T)
        us.append([dot(ka[:, : (b + 1) * TB], qa[:, b * TB : (b + 1) * TB], TN) for b in range(blocks)])
        gs.append([dot(va[:, : (b + 1) * TB], na[:, b * TB : (b + 1) * TB], TN) for b in range(blocks)])
    for n in heads:
        for b in range(blocks):
            lo, hi = b * TB, (b + 1) * TB
            u = us[n][b]
            p = u * u + 1.0
            s = gs[n][b] * u
            if b:
                pt[n, :lo, lo:hi] = p[:lo].astype(BF16)
                st[n, :lo, lo:hi] = s[:lo].astype(BF16)
            pt[n, lo:hi, lo:hi] = jnp.where(below, p[lo:], 0.0).astype(BF16)
            st[n, lo:hi, lo:hi] = jnp.where(below, s[lo:], 0.0).astype(BF16)
    for n in heads:
        for b in range(blocks):
            lo, hi = b * TB, (b + 1) * TB
            dq[n * F : (n + 1) * F, lo:hi] = dot(kss[n][:, :hi], st[n, :hi, lo:hi]).astype(BF16)
        for b in range(blocks):
            lo, hi = b * TB, (b + 1) * TB
            both = dot(pt[n, lo:hi, lo:], rights_p[n][lo:]) + dot(st[n, lo:hi, lo:], rights_s[n][lo:])
            turned = both.T
            dv[n * DV : (n + 1) * DV, lo:hi] = turned[:DV].astype(BF16)
            dk[n * F : (n + 1) * F, lo:hi] = turned[DV : DV + F].astype(BF16)


def attend_back(tab, qkv, datt, att, den, part, rows, count):
    tokens = qkv.shape[1]
    heads = BACK_HEADS
    many = H // BACK_PARTS
    off = part * many // heads
    each = DV // rows

    def piece(i):
        return pl.BlockSpec(
            (rows, tokens),
            lambda h, tab: (tab[count + (part * many + h * heads) * each + i], 0),
        )

    pieces = [piece(i) for i in range(heads * each)]
    return pl.pallas_call(
        functools.partial(attend_back_kernel, rows),
        grid_spec=pltpu.PrefetchScalarGridSpec(
            num_scalar_prefetch=1,
            grid=(many // heads,),
            in_specs=head_specs(tokens, heads, off)
            + [pl.BlockSpec((heads, 1, tokens), lambda h, tab: (off + h, 0, 0))]
            + pieces * 2,
            out_specs=[
                pl.BlockSpec((F * heads, tokens), lambda h, tab: (h, 0)),
                pl.BlockSpec((F * heads, tokens), lambda h, tab: (h, 0)),
                pl.BlockSpec((DV * heads, tokens), lambda h, tab: (h, 0)),
            ],
            scratch_shapes=[pltpu.VMEM((heads, tokens, tokens), BF16)] * 2,
        ),
        out_shape=(
            sds((many * F, tokens), BF16),
            sds((many * F, tokens), BF16),
            sds((many * DV, tokens), BF16),
        ),
        compiler_params=params(44),
        cost_estimate=cost(many * tokens * tokens * 256 * 6, 8 * many * DV * tokens * 2),
        name="attend_back",
    )(tab, *keep_far(qkv, qkv, qkv, den), *keep_far(datt) * len(pieces), *keep_far(att) * len(pieces))


def weights_kernel(normed, right, send, keep):
    half = keep.shape[0]
    whole = dot(normed[...], right[...], NT).astype(BF16)
    keep[...] = whole[:half]
    send[...] = whole[half:]


def weights_of(normed, grads):
    width, tokens = normed.shape
    wide = grads.shape[0]
    col = pl.BlockSpec((width // 2, TILE), lambda i: (0, i))
    return pl.pallas_call(
        weights_kernel,
        grid=(wide // TILE,),
        out_shape=(far((width // 2, wide), BF16),) * 2,
        in_specs=[
            pl.BlockSpec((width, tokens), lambda i: (0, 0), pipeline_mode=pl.Buffered(1)),
            pl.BlockSpec((TILE, tokens), lambda i: (i, 0)),
        ],
        out_specs=[col] * 2,
        compiler_params=params(12),
        cost_estimate=cost(2 * width * tokens * wide, 6 * width * tokens + 4 * width * wide),
        name="weights_of",
    )(normed, grads)


def input_kernel(rows, count, tab, w0, w1, w2, w3, gains, grads, dres, xt, r1, out, buf, nat):
    width, tokens = xt.shape
    quarter = w0.shape[0]
    wide = grads.shape[0]
    total = jnp.zeros((1, tokens), F32)
    scale = r1[...]
    for q, w in enumerate((w0, w1, w2, w3)):
        here = slice(q * quarter, (q + 1) * quarter)
        part = dot(w[:, :wide], grads[...])
        part = part * gains[here, 0:1].astype(F32)
        buf[here, :] = part
        total = total + jnp.sum(part * xt[here, :].astype(F32), axis=0, keepdims=True)
    pull = total / width * scale * scale * scale

    def second(p, _):
        here = pl.ds(pl.multiple_of(p * rows, rows), rows)
        part = dres[here, :] + scale * buf[here, :] - xt[here, :].astype(F32) * pull
        nat[pl.ds(pl.multiple_of(tab[p] * rows, rows), rows), :] = part.astype(nat.dtype)
        return 0

    lax.fori_loop(0, count, second, 0, unroll=4)
    for i in range(width // 256):
        here = slice(i * 256, (i + 1) * 256)
        out[:, here] = nat[here, :].T.astype(BF16)


def input_of(tab, grads, bufs, gains, dres, xt, r1, rows, count, kind):
    width, tokens = xt.shape
    wide = grads.shape[0]
    once = pl.BlockSpec(bufs[0].shape, lambda i: (0, 0), pipeline_mode=pl.Buffered(1))
    block = pl.BlockSpec((width, TB), lambda i: (0, i))
    return pl.pallas_call(
        functools.partial(input_kernel, rows, count),
        grid=(tokens // TB,),
        out_shape=sds((tokens, width), BF16),
        in_specs=[SMEM]
        + [once] * 4
        + [pl.BlockSpec((width, 128), lambda i: (0, 0))]
        + [pl.BlockSpec((wide, TB), lambda i: (0, i))]
        + [block, block, pl.BlockSpec((1, TB), lambda i: (0, i))],
        out_specs=pl.BlockSpec((TB, width), lambda i: (i, 0)),
        scratch_shapes=[pltpu.VMEM((width, TB), F32), pltpu.VMEM((width, TB), kind)],
        compiler_params=params(18),
        cost_estimate=cost(2 * width * tokens * wide, 12 * width * tokens + 2 * wide * tokens),
        name="input_of",
    )(tab, *keep_far(*bufs), gains, grads, *keep_far(dres, xt), r1)


def split_columns(total):
    tiles = -(-total // TILE)
    first = -(-tiles // 3)
    second = -(-(tiles - first) // 2)
    return [n * TILE for n in (tiles - first - second, second, first)]


def per_device(
    inputs, w_query, w_key, w_value, w_out, w_gate, w_up, w_down, gain_one, gain_two, cotangent
):
    dp = lax.axis_size("dp")
    bits = dp.bit_length() - 1
    count = 2 * dp
    micro, _, half, width = inputs.shape
    rows = width // count
    kind = BF16 if rows % 16 == 0 else F32
    hidden = w_gate.shape[1]
    groups = split_columns(hidden)
    padded = sum(groups)
    tab, core = block_tables(dp, bits)
    plan = Plan(dp, bits)
    plan.quarter = width // 4
    live = lambda: plan.live
    last = bits - 1

    x = inputs.reshape(micro, half, width)
    y = cotangent.reshape(micro, half, width)
    wide = w_query.shape[1] + w_key.shape[1] + w_value.shape[1]
    pair = jnp.pad(jnp.stack([gain_one, gain_two], axis=1), ((0, 0), (0, 126)))
    own_qkv = jnp.concatenate([w_query, w_key, w_value], axis=1)
    fill = ((0, 0), (0, padded - hidden))
    plan.gather("q", jnp.concatenate([own_qkv, pair], axis=1))
    plan.live.update(x=x, y=y, tab=tab)

    names = ["a", "b", "c"]
    downs = w_down.T

    def shard(k):
        at, size = sum(groups[:k]), groups[k]
        parts = [v[:, at : at + size] for v in (w_gate, w_up, downs)]
        short = size - parts[0].shape[1]
        if short:
            parts = [jnp.pad(p, ((0, 0), (0, short))) for p in parts]
        return jnp.stack(parts)

    def early(name, first=last):
        for stage in range(first, 1, -1):
            plan.double(name, stage)

    n = plan.live

    plan.double("q", last)
    plan.gather("o", w_out)
    n.update(w_gate=w_gate, w_up=w_up, downs=downs)
    plan.fence()
    early("q", last - 1)
    n["x_came"] = plan.send(lax.dynamic_index_in_dim(x, 1 - core, 0, keepdims=False), -1)
    n["y_came"] = plan.send(lax.dynamic_index_in_dim(y, 1 - core, 0, keepdims=False), -1)
    plan.fence()
    plan.double("q", 1)
    plan.double("o", last)
    w_gate, w_up, downs = n["w_gate"], n["w_up"], n["downs"]
    plan.gather("a", shard(0))
    plan.fence()
    plan.double("q", 0)
    early("o", last - 1)
    plan.double("a", last)
    n["xt"], n["r1"], n["yt"], n["yn"] = pre(
        n.pop("tab"), n.pop("x"), n.pop("x_came"), n.pop("y"), n.pop("y_came"), rows, count, kind
    )
    w_gate, w_up, downs = n.pop("w_gate"), n.pop("w_up"), n.pop("downs")
    plan.gather("b", shard(1))
    plan.gather("c", shard(2))
    plan.fence()
    plan.double("q", -1)
    plan.double("o", 1)
    early("a", last - 1)
    plan.fence()

    qkv_bufs = plan.gathered("q")
    n["gains"] = gains = jnp.concatenate([b[:, wide:] for b in qkv_bufs], axis=0)
    plan.double("o", 0)
    plan.double("b", last)
    n["normed"], n["qkv"] = project(n["xt"].astype(BF16), n["r1"], gains, qkv_bufs, wide)
    plan.fence()
    plan.double("o", -1)
    plan.double("a", 1)
    early("b", last - 1)
    n["att"], n["den"] = attend(tab, n["qkv"], rows, count, kind)
    plan.fence()
    plan.double("a", 0)
    plan.double("b", 1, True)
    plan.double("c", last)
    n["res"], n["r2"], n["x2t"], n["x2"] = middle(
        tab, n["att"].astype(BF16), plan.gathered("o"), n["xt"].astype(BF16), n["gains"], rows, count
    )
    plan.fence()
    plan.double("a", -1)
    early("c", last - 1)
    plan.fence()

    def feed_group(name):
        sums = (n["pull"], n["push"]) if "pull" in n else ()
        send, keep, n["pull"], n["push"] = feed(
            n["x2"], n["x2t"], n["yn"], n["yt"].astype(BF16), plan.gathered(name), sums,
            4 if name == names[-1] else 3,
        )
        for end in ("", "+", "-", "-+"):
            n.pop(name + end)
        plan.reduce("g" + name, send, keep)

    plan.double("b", 0)
    plan.double("c", 1, True)
    feed_group("a")
    plan.fence()
    plan.double("b", -1)
    plan.halve("ga", -1)
    plan.fence()
    plan.double("c", 0)
    feed_group("b")
    plan.fence()
    plan.double("c", -1)
    plan.halve("ga", 0, True)
    plan.fence()
    plan.halve("gb", -1)
    feed_group("c")
    plan.fence()
    plan.halve("ga", 1)
    plan.halve("gb", 0, True)
    n["dres"], n["dm"] = back(
        tab, n.pop("pull"), n["res"], n["r2"], n["yt"].astype(BF16), n["gains"], rows, count, kind
    )
    send, keep, n["datt"] = mixed(
        n.pop("dm").astype(BF16),
        n["att"].astype(BF16),
        plan.gathered("o"),
        n.pop("gc.send"),
        n.pop("gc"),
    )
    plan.reduce("gc", send, keep)
    plan.fence()

    def heads_back(part):
        for k, v in zip(
            ("dq", "dk", "dv"),
            attend_back(tab, n["qkv"], n["datt"], n["att"], n["den"], part, rows, count),
        ):
            n[k + str(part)] = v

    plan.scatter_far("ga", "sum_a")
    total_a = plan.air.pop("sum_a")
    plan.halve("gc", -1)
    heads_back(0)
    plan.fence()
    plan.halve("gb", 1)
    plan.halve("gc", 0, True)
    heads_back(1)
    plan.fence()
    plan.halve("gb", 2)
    heads_back(2)
    n["sum_a"] = total_a
    plan.fence()
    plan.halve("gc", 1)
    for stage in range(3, bits):
        plan.halve("gb", stage, stage == bits - 1)
    heads_back(3)
    n["grads"] = jnp.concatenate(
        [n.pop(k + str(p)) for k in ("dq", "dk", "dv") for p in range(BACK_PARTS)], axis=0
    )
    plan.fence()
    plan.halve("gc", 2, True)
    send, keep = weights_of(n["normed"], n["grads"])
    plan.reduce("gq", send, keep)
    plan.fence()
    plan.halve("gq", -1)
    n["sum_b"] = plan.reduced("gb")
    plan.fence()
    plan.halve("gq", 0)
    for stage in range(3, bits):
        plan.halve("gc", stage, stage == bits - 1)
    n["dx"] = input_of(
        tab, n["grads"], plan.gathered("q"), n["gains"], n["dres"], n["xt"].astype(BF16), n["r1"], rows, count, kind
    )
    plan.fence()

    def exchange(name):
        value = n.pop(name)
        n[name + "_own"] = lax.dynamic_slice_in_dim(value, core * half, half, 0)
        n[name + "_came"] = plan.send(lax.dynamic_slice_in_dim(value, (1 - core) * half, half, 0), -1)

    def give_back(name):
        own, came = n.pop(name + "_own"), n.pop(name + "_came")
        first = core == 0
        both = jnp.stack([jnp.where(first, own, came), jnp.where(first, came, own)])
        return both.reshape(micro, 1, half, width)

    plan.halve("gq", 1)
    exchange("dx")
    n["out"] = output_of(tab, n.pop("push"), n["res"], rows, count, kind)
    plan.fence()
    plan.halve("gq", 2)
    exchange("out")
    n["dx"] = give_back("dx")
    plan.fence()
    for stage in range(3, bits):
        plan.halve("gq", stage)
    n["out"] = give_back("out")
    n["sum_c"] = plan.reduced("gc")
    plan.fence()
    grad_qkv = plan.reduced("gq")
    grad_out = n["sum_c"][3]
    ff_grads = [n["sum_" + k][:3].astype(F32) for k in names]

    ff = jnp.concatenate(ff_grads, axis=-1)[:, :, :hidden]
    a, b = w_query.shape[1], w_query.shape[1] + w_key.shape[1]
    gain_one_grad = jnp.sum(own_qkv.astype(F32) * grad_qkv, axis=1) / gain_one.astype(F32)
    gain_two_grad = (
        jnp.sum(w_gate.astype(F32) * ff[0] + w_up.astype(F32) * ff[1], axis=1)
    ) / gain_two.astype(F32)
    return (
        n["out"],
        n["dx"],
        grad_qkv[:, :a],
        grad_qkv[:, a:b],
        grad_qkv[:, b:],
        grad_out,
        ff[0],
        ff[1],
        ff[2].T,
        gain_one_grad,
        gain_two_grad,
    )


def solution(mesh):
    shard = P(AXES, None)
    batch = P(None, "dp", "seq", None)
    return jax.shard_map(
        per_device,
        mesh=mesh,
        in_specs=(batch,) + (shard,) * 6 + (P(None, AXES), P(AXES), P(AXES), batch),
        out_specs=(batch,) * 2 + (shard,) * 6 + (P(None, AXES), P(AXES), P(AXES)),
        check_vma=False,
    )
```

```python
import functools

import jax
import jax.numpy as jnp
import numpy as np
from jax import lax
from jax.experimental import pallas as pl
from jax.experimental.pallas import tpu as pltpu
from jax.sharding import PartitionSpec as P

H = 16
F = 16
DV = 64
AXES = ("dp", "seq")
EPS = 1e-06
TB = 256
HEADS = 2
BACK_HEADS = 2
BACK_PARTS = ((0, 4), (4, 4), (8, 8))
TILE = 256
F32 = jnp.float32
BF16 = jnp.bfloat16

NN = (((1,), (0,)), ((), ()))
NT = (((1,), (1,)), ((), ()))
TN = (((0,), (0,)), ((), ()))


def dot(a, b, dims=NN):
    return lax.dot_general(a, b, dims, preferred_element_type=F32)


VMEM = pl.BlockSpec(memory_space=pltpu.VMEM)
SMEM = pl.BlockSpec(memory_space=pltpu.SMEM)


def params(mib):
    return pltpu.CompilerParams(vmem_limit_bytes=mib << 20)


def cost(flops, nbytes, trans=0):
    return pl.CostEstimate(flops=int(flops), bytes_accessed=int(nbytes), transcendentals=int(trans))


def sds(shape, dtype):
    return jax.ShapeDtypeStruct(shape, dtype)


def far(shape, dtype):
    return pltpu.HBM(shape, dtype)


def keep_far(*values):
    return [pltpu.with_memory_space_constraint(v, pltpu.HBM) for v in values]


def stage_orders(bits):
    straight = list(range(bits))
    swapped = [1, 0] + list(range(2, bits)) if bits > 1 else straight
    return (straight, swapped)


def stage_pairs(dp, bits, stage):
    orders = stage_orders(bits)
    return [
        (d * 2 + c, (d ^ (1 << orders[c][stage])) * 2 + c) for d in range(dp) for c in range(2)
    ]


def core_pairs(dp):
    return [(i, i ^ 1) for i in range(2 * dp)]


def block_tables(dp, bits):
    orders = stage_orders(bits)
    count = 2 * dp
    position = np.arange(count)
    masks, fixed = [], np.zeros(count, np.int32)
    for c in range(2):
        mask = np.zeros(count, np.int32)
        for stage in range(2):
            mask |= ((position >> (bits - 1 - stage)) & 1) << orders[c][stage]
        masks.append(mask)
    for stage in range(2, bits):
        fixed |= ((position >> (bits - 1 - stage)) & 1) << stage
    d = lax.axis_index("dp").astype(jnp.int32)
    c = lax.axis_index("seq").astype(jnp.int32)
    owner_core = jnp.asarray(position >> bits, jnp.int32) ^ c
    mask = jnp.where(owner_core == 0, jnp.asarray(masks[0]), jnp.asarray(masks[1]))
    block_at = (((d & 3) ^ mask) | jnp.asarray(fixed)) * 2 + owner_core
    block_core = jnp.asarray(position & 1, jnp.int32)
    owner = position >> 1
    low = np.zeros(count, np.int32)
    for stage in range(2, bits):
        low |= ((owner >> stage) & 1) << (bits - 1 - stage)
    apart = jnp.asarray(owner & 3, jnp.int32) ^ (d & 3)
    places = []
    for k in range(2):
        place = jnp.asarray(low)
        for stage in range(2):
            place = place | (((apart >> orders[k][stage]) & 1) << (bits - 1 - stage))
        places.append(place)
    place_of = jnp.where(block_core == 0, places[0], places[1]) | ((block_core ^ c) << bits)
    return jnp.concatenate([block_at, place_of, c[None], jnp.zeros(7, jnp.int32)]), c


class Plan:
    def __init__(self, dp, bits):
        self.dp, self.bits = dp, bits
        self.live, self.parts, self.air = {}, {}, {}

    def fence(self):
        self.live.update(lax.optimization_barrier(dict(self.live)))
        self.live.update(self.air)
        self.air = {}

    def pairs(self, stage):
        return core_pairs(self.dp) if stage < 0 else stage_pairs(self.dp, self.bits, stage)

    def send(self, value, stage):
        return lax.ppermute(value, AXES, self.pairs(stage))

    def gather(self, name, shard):
        self.live[name] = shard

    def bit(self, stage):
        return (lax.axis_index("dp") >> stage) & 1

    def double(self, name, stage, long=False):
        live = self.live
        if 0 <= stage < self.bits - 1:
            self.join(name, stage + 1)
        if stage >= 0:
            (self.air if long else live)[name + "+"] = self.send(live[name], stage)
            if stage == 0:
                live[name + "-"] = self.send(live[name], -1)
        else:
            live[name + "-+"] = self.send(live[name + "+"], -1)

    def join(self, name, stage):
        held, came = self.live[name], self.live.pop(name + "+")
        if stage >= 2:
            first = self.bit(stage) == 0
            held, came = jnp.where(first, held, came), jnp.where(first, came, held)
        self.live[name] = jnp.concatenate([held, came], axis=-2)

    def gathered(self, name):
        return tuple(self.live[name + end] for end in ("", "+", "-", "-+"))

    def reduce(self, name, send, keep):
        self.live[name + ".send"], self.live[name] = send, keep
        self.parts[name] = [(name, 0)]

    def halve(self, name, stage, long=False):
        live = self.live
        if stage < 0:
            send = live.pop(name + ".send")
        else:
            half = live[name].shape[-2] >> (stage + 1)
            parts = self.parts[name]
            if stage < 2:
                send = self.total(parts, half, half)
            else:
                bit = self.bit(stage)
                send = self.total(parts, (1 - bit) * half, half)
                self.parts[name] = [(key, off + bit * half) for key, off in parts]
            send = send.astype(BF16)
        key = f"{name}.{stage}"
        (self.air if long else live)[key] = self.send(send, stage)
        self.parts[name] = self.parts[name] + [(key, 0)]

    def total(self, parts, start, size):
        acc = None
        for key, off in parts:
            part = self.live[key]
            part = lax.dynamic_slice_in_dim(part, off + start, size, axis=part.ndim - 2)
            acc = part.astype(F32) if acc is None else acc + part.astype(F32)
        return acc

    def reduced(self, name):
        return self.total(self.parts[name], 0, self.live[name].shape[-2] >> self.bits)


def pre_kernel(rows, count, blocks, tab, x, xr, y, yr, xt, r1, yt, yn, buf):
    own = pl.program_id(0) // blocks == tab[2 * count]
    width = xt.shape[0]
    total = jnp.zeros(r1.shape, F32)
    for src, rec, dst in ((x, xr, xt), (y, yr, yt)):
        for i in range(width // 256):
            here = slice(i * 256, (i + 1) * 256)
            part = jnp.where(own, src[0, :, here], rec[:, here]).T
            buf[here, :] = part.astype(buf.dtype)
            if src is x:
                wide = part.astype(F32)
                total = total + jnp.sum(wide * wide, axis=0, keepdims=True)

        def move(p, _):
            at = pl.multiple_of(tab[p] * rows, rows)
            dst[pl.ds(pl.multiple_of(p * rows, rows), rows), :] = buf[pl.ds(at, rows), :]
            return 0

        lax.fori_loop(0, count, move, 0, unroll=4)
    for i in range(width // 256):
        here = slice(i * 256, (i + 1) * 256)
        yn[:, here] = yt[here, :].T.astype(BF16)
    r1[...] = lax.rsqrt(total / width + EPS)


def pre(tab, x, xr, y, yr, rows, count, kind):
    half, width = xr.shape
    tokens = 2 * half
    blocks = half // TB
    own = pl.BlockSpec((1, TB, width), lambda i, tab: (tab[2 * count], i % blocks, 0))
    came = pl.BlockSpec((TB, width), lambda i, tab: (i % blocks, 0))
    turned = pl.BlockSpec((width, TB), lambda i, tab: (0, i))
    return pl.pallas_call(
        functools.partial(pre_kernel, rows, count, blocks),
        grid_spec=pltpu.PrefetchScalarGridSpec(
            num_scalar_prefetch=1,
            grid=(tokens // TB,),
            in_specs=[own, came, own, came],
            out_specs=[
                turned,
                pl.BlockSpec((1, TB), lambda i, tab: (0, i)),
                turned,
                pl.BlockSpec((TB, width), lambda i, tab: (i, 0)),
            ],
            scratch_shapes=[pltpu.VMEM((width, TB), kind)],
        ),
        out_shape=(
            sds((width, tokens), kind),
            sds((1, tokens), F32),
            sds((width, tokens), kind),
            sds((tokens, width), BF16),
        ),
        compiler_params=params(14),
        cost_estimate=cost(8 * width * tokens, 14 * width * tokens),
        name="pre",
    )(tab, x, xr, y, yr)


def project_kernel(xt, r1, gains, w0, w1, w2, w3, normed, out):
    quarter = w0.shape[0]

    @pl.when(pl.program_id(0) == 0)
    def _():
        for q in range(4):
            here = slice(q * quarter, (q + 1) * quarter)
            part = xt[here, :].astype(F32) * r1[...] * gains[here, 0:1].astype(F32)
            normed[here, :] = part.astype(BF16)

    acc = dot(w0[...], normed[0:quarter, :], TN)
    for q, w in ((1, w1), (2, w2), (3, w3)):
        acc = acc + dot(w[...], normed[q * quarter : (q + 1) * quarter, :], TN)
    out[...] = acc.astype(BF16)


def project(xt, r1, gains, bufs, wide):
    width, tokens = xt.shape
    quarter = bufs[0].shape[0]
    return pl.pallas_call(
        project_kernel,
        grid=(wide // 256,),
        out_shape=(sds((width, tokens), BF16), sds((wide, tokens), BF16)),
        in_specs=[
            pl.BlockSpec((width, tokens), lambda i: (0, 0), pipeline_mode=pl.Buffered(1)),
            pl.BlockSpec((1, tokens), lambda i: (0, 0)),
            pl.BlockSpec((width, 128), lambda i: (0, 0)),
        ]
        + [pl.BlockSpec((quarter, 256), lambda i: (0, i))] * 4,
        out_specs=[
            pl.BlockSpec((width, tokens), lambda i: (0, 0)),
            pl.BlockSpec((256, tokens), lambda i: (i, 0)),
        ],
        compiler_params=params(16),
        cost_estimate=cost(2 * width * tokens * wide, 2 * (2 * width * tokens + 2 * wide * tokens)),
        name="project",
    )(xt, r1, gains, *keep_far(*bufs))


def unit_rows(tokens, ones):
    row = lax.broadcasted_iota(jnp.int32, (16, tokens), 0)
    return jnp.where(row < ones, 1.0, 0.0).astype(BF16)


def causal(shape):
    j = lax.broadcasted_iota(jnp.int32, shape, 0)
    t = lax.broadcasted_iota(jnp.int32, shape, 1)
    return j <= t


def attend_kernel(rows, count, tab, q, k, v, att, den):
    tokens = q.shape[1]
    blocks = tokens // TB
    one = unit_rows(tokens, 1)
    below = causal((TB, TB))
    heads = range(q.shape[0] // F)
    us, vas = [], []
    for n in heads:
        qa = q[n * F : (n + 1) * F, :] * jnp.asarray(F ** -0.5, BF16)
        qa = jnp.concatenate([qa, one], axis=0)
        ka = jnp.concatenate([k[n * F : (n + 1) * F, :], one], axis=0)
        vas.append(jnp.concatenate([v[n * DV : (n + 1) * DV, :], one], axis=0))
        us.append(
            [dot(ka[:, : (b + 1) * TB], qa[:, b * TB : (b + 1) * TB], TN) for b in range(blocks)]
        )
    ps = []
    for n in heads:
        ps.append([])
        for b in range(blocks):
            lo = b * TB
            p = us[n][b] * us[n][b] + 1.0
            last = jnp.where(below, p[lo:], 0.0).astype(BF16)
            ps[n].append(jnp.concatenate([p[:lo].astype(BF16), last], axis=0) if b else last)
    for n in heads:
        h = pl.program_id(0) * len(heads) + n
        for b in range(blocks):
            lo, hi = b * TB, (b + 1) * TB
            o = dot(vas[n][:, :hi], ps[n][b])
            d = o[DV : DV + 1]
            done = o[:DV] / d
            den[n, :, lo:hi] = d
            for i in range(DV // rows):
                at = tab[count + h * (DV // rows) + i]
                att[pl.ds(pl.multiple_of(at * rows, rows), rows), lo:hi] = done[
                    i * rows : (i + 1) * rows
                ].astype(att.dtype)


def head_specs(tokens, heads, off=0):
    return [
        pl.BlockSpec((F * heads, tokens), lambda h, *_: (off + h, 0)),
        pl.BlockSpec((F * heads, tokens), lambda h, *_: (H // heads + off + h, 0)),
        pl.BlockSpec((DV * heads, tokens), lambda h, *_: (2 * H * F // DV // heads + off + h, 0)),
    ]


def attend(tab, qkv, rows, count, kind):
    tokens = qkv.shape[1]
    heads = HEADS
    return pl.pallas_call(
        functools.partial(attend_kernel, rows, count),
        grid=(H // heads,),
        out_shape=(sds((H * DV, tokens), kind), sds((H, 1, tokens), F32)),
        in_specs=[SMEM] + head_specs(tokens, heads),
        out_specs=[
            pl.BlockSpec((H * DV, tokens), lambda h: (0, 0)),
            pl.BlockSpec((heads, 1, tokens), lambda h: (h, 0, 0)),
        ],
        compiler_params=params(28),
        cost_estimate=cost(H * tokens * tokens * 256 * 2, 4 * H * DV * tokens * 2),
        name="attend",
    )(tab, qkv, qkv, qkv)


def middle_kernel(rows, count, tab, w0, w1, w2, w3, att, xt, gains, res, r2, x2t, x2, wt, buf):
    width, tokens = xt.shape
    quarter = w0.shape[0]

    @pl.when(pl.program_id(0) == 0)
    def _():
        for q, w in enumerate((w0, w1, w2, w3)):
            for i in range(width // 256):
                wt[i * 256 : (i + 1) * 256, q * quarter : (q + 1) * quarter] = w[
                    :, i * 256 : (i + 1) * 256
                ].T

    buf[...] = dot(wt[...], att[...])

    def join(p, total):
        here = pl.ds(pl.multiple_of(p * rows, rows), rows)
        part = buf[pl.ds(pl.multiple_of(tab[p] * rows, rows), rows), :] + xt[here, :].astype(F32)
        res[here, :] = part
        return total + jnp.sum(part * part, axis=0, keepdims=True)

    total = lax.fori_loop(0, count, join, jnp.zeros((1, tokens), F32), unroll=4)
    scale = lax.rsqrt(total / width + EPS)
    r2[...] = scale
    for i in range(width // 256):
        here = slice(i * 256, (i + 1) * 256)
        low = (res[here, :] * scale * gains[here, 1:2].astype(F32)).astype(BF16)
        x2t[here, :] = low
        x2[:, here] = low.T


def middle(tab, att, bufs, xt, gains, rows, count):
    width, tokens = xt.shape
    inner = att.shape[0]
    quarter = bufs[0].shape[0]
    once = pl.BlockSpec((quarter, width), lambda i: (0, 0), pipeline_mode=pl.Buffered(1))
    return pl.pallas_call(
        functools.partial(middle_kernel, rows, count),
        grid=(tokens // TB,),
        out_shape=(
            far((width, tokens), F32),
            sds((1, tokens), F32),
            sds((width, tokens), BF16),
            sds((tokens, width), BF16),
        ),
        in_specs=[SMEM]
        + [once] * 4
        + [
            pl.BlockSpec((inner, TB), lambda i: (0, i)),
            pl.BlockSpec((width, TB), lambda i: (0, i)),
            pl.BlockSpec((width, 128), lambda i: (0, 0)),
        ],
        out_specs=[
            pl.BlockSpec((width, TB), lambda i: (0, i)),
            pl.BlockSpec((1, TB), lambda i: (0, i)),
            pl.BlockSpec((width, TB), lambda i: (0, i)),
            pl.BlockSpec((TB, width), lambda i: (i, 0)),
        ],
        scratch_shapes=[pltpu.VMEM((width, inner), BF16), pltpu.VMEM((width, TB), F32)],
        compiler_params=params(22),
        cost_estimate=cost(2 * width * tokens * inner, 16 * width * tokens),
        name="middle",
    )(tab, *keep_far(*bufs), att, *keep_far(xt), gains)


def feed_kernel(first, x2, x2t, dy, dyt, w0, w1, w2, w3, *refs):
    send, keep, pull, push = refs[-4:]
    quarter = w0.shape[1]
    bufs = (w0, w1, w2, w3)
    half = keep.shape[1]

    if first:

        @pl.when(pl.program_id(0) == 0)
        def _():
            pull[...] = jnp.zeros_like(pull)
            push[...] = jnp.zeros_like(push)

    def over(a, which):
        acc = dot(a[:, 0:quarter], w0[which])
        for q in range(1, 4):
            acc = acc + dot(a[:, q * quarter : (q + 1) * quarter], bufs[q][which])
        return acc

    def grad(i, a, b):
        whole = dot(a[...], b).astype(BF16)
        keep[i] = whole[:half]
        send[i] = whole[half:]

    gate = over(x2, 0)
    up = over(x2, 1)
    sig = 0.5 * jnp.tanh(0.5 * gate) + 0.5
    act = gate * sig
    h = (act * up).astype(BF16)
    back = over(dy, 2)
    dg = (back * up * (sig + act * (1.0 - sig))).astype(BF16)
    du = (back * act).astype(BF16)
    ht, dgt, dut = h.T, dg.T, du.T
    grad(2, dyt, h)
    for q, w in enumerate(bufs):
        here = slice(q * quarter, (q + 1) * quarter)
        push[here, :] = push[here, :] + dot(w[2], ht)
    grad(0, x2t, dg)
    grad(1, x2t, du)
    for q, w in enumerate(bufs):
        here = slice(q * quarter, (q + 1) * quarter)
        pull[here, :] = pull[here, :] + (dot(w[0], dgt) + dot(w[1], dut))


def feed(x2, x2t, dy, dyt, bufs, sums, slots=3):
    tokens, width = x2.shape
    cols = bufs[0].shape[-1]
    quarter = bufs[0].shape[1]
    return pl.pallas_call(
        functools.partial(feed_kernel, not sums),
        grid=(cols // TILE,),
        out_shape=(far((slots, width // 2, cols), BF16),) * 2 + (sds((width, tokens), F32),) * 2,
        in_specs=[VMEM] * 4
        + [pl.BlockSpec((3, quarter, TILE), lambda i: (0, 0, i))] * 4
        + [VMEM] * len(sums),
        out_specs=[pl.BlockSpec((3, width // 2, TILE), lambda i: (0, 0, i))] * 2 + [VMEM] * 2,
        input_output_aliases={8: 2, 9: 3} if sums else {},
        compiler_params=params(26),
        cost_estimate=cost(18 * tokens * width * cols, 2 * (4 * tokens * width + 9 * width * cols)),
        name="feed",
    )(x2, x2t, dy, dyt, *keep_far(*bufs), *sums)


def back_kernel(rows, count, tab, pull, res, r2, yt, gains, dres, dm, acc):
    width, tokens = acc.shape
    part = pull[...] * gains[:, 1:2].astype(F32)
    acc[...] = part
    total = jnp.sum(part * res[...], axis=0, keepdims=True)
    scale = r2[...]
    side = total / width * scale * scale * scale

    def second(p, _):
        here = pl.ds(pl.multiple_of(p * rows, rows), rows)
        part = yt[here, :].astype(F32) + scale * acc[here, :] - res[here, :] * side
        dres[here, :] = part
        dm[pl.ds(pl.multiple_of(tab[p] * rows, rows), rows), :] = part.astype(dm.dtype)
        return 0

    lax.fori_loop(0, count, second, 0, unroll=4)


def back(tab, pull, res, r2, yt, gains, rows, count, kind):
    width, tokens = res.shape
    block = pl.BlockSpec((width, TB), lambda i: (0, i))
    return pl.pallas_call(
        functools.partial(back_kernel, rows, count),
        grid=(tokens // TB,),
        out_shape=(far((width, tokens), F32), sds((width, tokens), kind)),
        in_specs=[
            SMEM,
            block,
            block,
            pl.BlockSpec((1, TB), lambda i: (0, i)),
            block,
            pl.BlockSpec((width, 128), lambda i: (0, 0)),
        ],
        out_specs=[block] * 2,
        scratch_shapes=[pltpu.VMEM((width, TB), F32)],
        compiler_params=params(20),
        cost_estimate=cost(10 * tokens * width, 16 * width * tokens),
        name="back",
    )(tab, pull, *keep_far(res), r2, *keep_far(yt), gains)


def output_kernel(rows, count, tab, push, res, out, acc, nat):
    width, tokens = acc.shape
    acc[...] = push[...] + res[...]

    def move(p, _):
        here = pl.ds(pl.multiple_of(p * rows, rows), rows)
        to = pl.ds(pl.multiple_of(tab[p] * rows, rows), rows)
        nat[to, :] = acc[here, :].astype(nat.dtype)
        return 0

    lax.fori_loop(0, count, move, 0, unroll=4)
    for i in range(width // 256):
        here = slice(i * 256, (i + 1) * 256)
        out[:, here] = nat[here, :].T.astype(BF16)


def output_of(tab, push, res, rows, count, kind):
    width, tokens = res.shape
    block = pl.BlockSpec((width, TB), lambda i: (0, i))
    return pl.pallas_call(
        functools.partial(output_kernel, rows, count),
        grid=(tokens // TB,),
        out_shape=sds((tokens, width), BF16),
        in_specs=[SMEM, block, block],
        out_specs=pl.BlockSpec((TB, width), lambda i: (i, 0)),
        scratch_shapes=[pltpu.VMEM((width, TB), F32), pltpu.VMEM((width, TB), kind)],
        compiler_params=params(16),
        cost_estimate=cost(tokens * width, 10 * width * tokens),
        name="output_of",
    )(tab, *keep_far(push, res))


def mixed_kernel(dm, dm_rows, att, w0, w1, w2, w3, send_in, keep_in, send, keep, datt):
    quarter = w0.shape[0]
    half = keep.shape[1]
    right = dm[...]
    for q, w in enumerate((w0, w1, w2, w3)):
        datt[q * quarter : (q + 1) * quarter, :] = dot(w[...], right)
    whole = dot(att[...], dm_rows[...], NT).astype(BF16)
    keep[0] = whole[:half]
    send[0] = whole[half:]


def mixed(dm, att, bufs, send, keep):
    width, tokens = dm.shape
    rows = att.shape[0]
    quarter = bufs[0].shape[0]
    slot = keep.shape[0] - 1
    cols = width * TB // tokens
    return pl.pallas_call(
        mixed_kernel,
        grid=(tokens // TB,),
        out_shape=(far(send.shape, BF16), far(keep.shape, BF16), far((rows, tokens), F32)),
        in_specs=[
            pl.BlockSpec((width, TB), lambda i: (0, i)),
            pl.BlockSpec((cols, tokens), lambda i: (i, 0)),
            pl.BlockSpec((rows, tokens), lambda i: (0, 0), pipeline_mode=pl.Buffered(1)),
        ]
        + [pl.BlockSpec((quarter, width), lambda i: (0, 0), pipeline_mode=pl.Buffered(1))] * 4
        + [pl.BlockSpec(memory_space=pl.ANY)] * 2,
        out_specs=[pl.BlockSpec((1, rows // 2, cols), lambda i: (slot, 0, i))] * 2
        + [pl.BlockSpec((rows, TB), lambda i: (0, i))],
        input_output_aliases={7: 0, 8: 1},
        compiler_params=params(18),
        cost_estimate=cost(4 * width * tokens * rows, 12 * width * tokens),
        name="mixed",
    )(dm, dm, att, *keep_far(*bufs, send, keep))


def attend_back_kernel(rows, tab, q, k, v, den, *refs):
    many = q.shape[0] // F * (DV // rows)
    datts, atts = refs[:many], refs[many : 2 * many]
    dq, dk, dv, pt, st = refs[2 * many :]
    tokens = q.shape[1]
    blocks = tokens // TB
    scale = jnp.asarray(F ** -0.5, BF16)
    row = lax.broadcasted_iota(jnp.int32, (16, tokens), 0)
    one = unit_rows(tokens, 1)
    two = unit_rows(tokens, 2)
    zero = jnp.zeros((DV, tokens), BF16)
    below = causal((TB, TB))
    heads = range(q.shape[0] // F)
    us, gs, kss, rights_p, rights_s = [], [], [], [], []
    for n in heads:
        here = slice(n * (DV // rows), (n + 1) * (DV // rows))
        da = jnp.concatenate([r[...] for r in datts[here]], axis=0)
        done = jnp.concatenate([r[...].astype(F32) for r in atts[here]], axis=0)
        inv = 2.0 / den[n]
        dn = (da * inv).astype(BF16)
        dd = -jnp.sum(da * done, axis=0, keepdims=True) * inv
        dd_high = dd.astype(BF16).astype(F32)
        tail = jnp.where(row == 0, dd_high, jnp.where(row == 1, dd - dd_high, 0.0)).astype(BF16)
        qh, kh = q[n * F : (n + 1) * F, :], k[n * F : (n + 1) * F, :]
        qs = qh * scale
        kss.append(kh * scale)
        qa = jnp.concatenate([qs, one], axis=0)
        ka = jnp.concatenate([kh, one], axis=0)
        va = jnp.concatenate([v[n * DV : (n + 1) * DV, :], two], axis=0)
        na = jnp.concatenate([dn, tail], axis=0)
        rights_p.append(jnp.concatenate([dn * jnp.asarray(0.5, BF16), zero], axis=0).T)
        rights_s.append(jnp.concatenate([zero, qs, jnp.zeros((DV - F, tokens), BF16)], axis=0).T)
        us.append([dot(ka[:, : (b + 1) * TB], qa[:, b * TB : (b + 1) * TB], TN) for b in range(blocks)])
        gs.append([dot(va[:, : (b + 1) * TB], na[:, b * TB : (b + 1) * TB], TN) for b in range(blocks)])
    for n in heads:
        for b in range(blocks):
            lo, hi = b * TB, (b + 1) * TB
            u = us[n][b]
            p = u * u + 1.0
            s = gs[n][b] * u
            if b:
                pt[n, :lo, lo:hi] = p[:lo].astype(BF16)
                st[n, :lo, lo:hi] = s[:lo].astype(BF16)
            pt[n, lo:hi, lo:hi] = jnp.where(below, p[lo:], 0.0).astype(BF16)
            st[n, lo:hi, lo:hi] = jnp.where(below, s[lo:], 0.0).astype(BF16)
    for n in heads:
        for b in range(blocks):
            lo, hi = b * TB, (b + 1) * TB
            dq[n * F : (n + 1) * F, lo:hi] = dot(kss[n][:, :hi], st[n, :hi, lo:hi]).astype(BF16)
        for b in range(blocks):
            lo, hi = b * TB, (b + 1) * TB
            both = dot(pt[n, lo:hi, lo:], rights_p[n][lo:]) + dot(st[n, lo:hi, lo:], rights_s[n][lo:])
            turned = both.T
            dv[n * DV : (n + 1) * DV, lo:hi] = turned[:DV].astype(BF16)
            dk[n * F : (n + 1) * F, lo:hi] = turned[DV : DV + F].astype(BF16)


def attend_back(tab, qkv, datt, att, den, part, rows, count):
    tokens = qkv.shape[1]
    heads = BACK_HEADS
    base, many = part
    off = base // heads
    each = DV // rows

    def piece(i):
        return pl.BlockSpec(
            (rows, tokens),
            lambda h, tab: (tab[count + (base + h * heads) * each + i], 0),
        )

    pieces = [piece(i) for i in range(heads * each)]
    return pl.pallas_call(
        functools.partial(attend_back_kernel, rows),
        grid_spec=pltpu.PrefetchScalarGridSpec(
            num_scalar_prefetch=1,
            grid=(many // heads,),
            in_specs=head_specs(tokens, heads, off)
            + [pl.BlockSpec((heads, 1, tokens), lambda h, tab: (off + h, 0, 0))]
            + pieces * 2,
            out_specs=[
                pl.BlockSpec((F * heads, tokens), lambda h, tab: (h, 0)),
                pl.BlockSpec((F * heads, tokens), lambda h, tab: (h, 0)),
                pl.BlockSpec((DV * heads, tokens), lambda h, tab: (h, 0)),
            ],
            scratch_shapes=[pltpu.VMEM((heads, tokens, tokens), BF16)] * 2,
        ),
        out_shape=(
            sds((many * F, tokens), BF16),
            sds((many * F, tokens), BF16),
            sds((many * DV, tokens), BF16),
        ),
        compiler_params=params(44),
        cost_estimate=cost(many * tokens * tokens * 256 * 6, 8 * many * DV * tokens * 2),
        name="attend_back",
    )(tab, *keep_far(qkv, qkv, qkv, den), *keep_far(datt) * len(pieces), *keep_far(att) * len(pieces))


def weights_kernel(normed, right, send, keep):
    half = keep.shape[0]
    whole = dot(normed[...], right[...], NT).astype(BF16)
    keep[...] = whole[:half]
    send[...] = whole[half:]


def weights_of(normed, grads):
    width, tokens = normed.shape
    wide = grads.shape[0]
    col = pl.BlockSpec((width // 2, TILE), lambda i: (0, i))
    return pl.pallas_call(
        weights_kernel,
        grid=(wide // TILE,),
        out_shape=(far((width // 2, wide), BF16),) * 2,
        in_specs=[
            pl.BlockSpec((width, tokens), lambda i: (0, 0), pipeline_mode=pl.Buffered(1)),
            pl.BlockSpec((TILE, tokens), lambda i: (i, 0)),
        ],
        out_specs=[col] * 2,
        compiler_params=params(12),
        cost_estimate=cost(2 * width * tokens * wide, 6 * width * tokens + 4 * width * wide),
        name="weights_of",
    )(normed, grads)


def input_kernel(rows, count, tab, w0, w1, w2, w3, gains, grads, dres, xt, r1, out, buf, nat):
    width, tokens = xt.shape
    quarter = w0.shape[0]
    wide = grads.shape[0]
    total = jnp.zeros((1, tokens), F32)
    scale = r1[...]
    for q, w in enumerate((w0, w1, w2, w3)):
        here = slice(q * quarter, (q + 1) * quarter)
        part = dot(w[:, :wide], grads[...])
        part = part * gains[here, 0:1].astype(F32)
        buf[here, :] = part
        total = total + jnp.sum(part * xt[here, :].astype(F32), axis=0, keepdims=True)
    pull = total / width * scale * scale * scale

    def second(p, _):
        here = pl.ds(pl.multiple_of(p * rows, rows), rows)
        part = dres[here, :] + scale * buf[here, :] - xt[here, :].astype(F32) * pull
        nat[pl.ds(pl.multiple_of(tab[p] * rows, rows), rows), :] = part.astype(nat.dtype)
        return 0

    lax.fori_loop(0, count, second, 0, unroll=4)
    for i in range(width // 256):
        here = slice(i * 256, (i + 1) * 256)
        out[:, here] = nat[here, :].T.astype(BF16)


def input_of(tab, grads, bufs, gains, dres, xt, r1, rows, count, kind):
    width, tokens = xt.shape
    wide = grads.shape[0]
    once = pl.BlockSpec(bufs[0].shape, lambda i: (0, 0), pipeline_mode=pl.Buffered(1))
    block = pl.BlockSpec((width, TB), lambda i: (0, i))
    return pl.pallas_call(
        functools.partial(input_kernel, rows, count),
        grid=(tokens // TB,),
        out_shape=sds((tokens, width), BF16),
        in_specs=[SMEM]
        + [once] * 4
        + [pl.BlockSpec((width, 128), lambda i: (0, 0))]
        + [pl.BlockSpec((wide, TB), lambda i: (0, i))]
        + [block, block, pl.BlockSpec((1, TB), lambda i: (0, i))],
        out_specs=pl.BlockSpec((TB, width), lambda i: (i, 0)),
        scratch_shapes=[pltpu.VMEM((width, TB), F32), pltpu.VMEM((width, TB), kind)],
        compiler_params=params(18),
        cost_estimate=cost(2 * width * tokens * wide, 12 * width * tokens + 2 * wide * tokens),
        name="input_of",
    )(tab, *keep_far(*bufs), gains, grads, *keep_far(dres, xt), r1)


def split_columns(total):
    tiles = -(-total // TILE)
    first = -(-tiles // 3)
    second = -(-(tiles - first) // 2)
    return [n * TILE for n in (tiles - first - second, second, first)]


def per_device(
    inputs, w_query, w_key, w_value, w_out, w_gate, w_up, w_down, gain_one, gain_two, cotangent
):
    dp = lax.axis_size("dp")
    bits = dp.bit_length() - 1
    count = 2 * dp
    micro, _, half, width = inputs.shape
    rows = width // count
    kind = BF16 if rows % 16 == 0 else F32
    hidden = w_gate.shape[1]
    groups = split_columns(hidden)
    padded = sum(groups)
    tab, core = block_tables(dp, bits)
    plan = Plan(dp, bits)
    plan.quarter = width // 4
    live = lambda: plan.live
    last = bits - 1

    x = inputs.reshape(micro, half, width)
    y = cotangent.reshape(micro, half, width)
    wide = w_query.shape[1] + w_key.shape[1] + w_value.shape[1]
    pair = jnp.pad(jnp.stack([gain_one, gain_two], axis=1), ((0, 0), (0, 126)))
    own_qkv = jnp.concatenate([w_query, w_key, w_value], axis=1)
    fill = ((0, 0), (0, padded - hidden))
    plan.gather("q", jnp.concatenate([own_qkv, pair], axis=1))
    plan.live.update(x=x, y=y, tab=tab)

    names = ["a", "b", "c"]
    downs = w_down.T

    def shard(k):
        at, size = sum(groups[:k]), groups[k]
        parts = [v[:, at : at + size] for v in (w_gate, w_up, downs)]
        short = size - parts[0].shape[1]
        if short:
            parts = [jnp.pad(p, ((0, 0), (0, short))) for p in parts]
        return jnp.stack(parts)

    def early(name, first=last):
        for stage in range(first, 1, -1):
            plan.double(name, stage)

    n = plan.live

    plan.double("q", last)
    plan.gather("o", w_out)
    n.update(w_gate=w_gate, w_up=w_up, downs=downs)
    plan.fence()
    early("q", last - 1)
    n["x_came"] = plan.send(lax.dynamic_index_in_dim(x, 1 - core, 0, keepdims=False), -1)
    n["y_came"] = plan.send(lax.dynamic_index_in_dim(y, 1 - core, 0, keepdims=False), -1)
    plan.fence()
    plan.double("q", 1)
    plan.double("o", last)
    w_gate, w_up, downs = n["w_gate"], n["w_up"], n["downs"]
    plan.gather("a", shard(0))
    plan.fence()
    plan.double("q", 0)
    early("o", last - 1)
    plan.double("a", last)
    n["xt"], n["r1"], n["yt"], n["yn"] = pre(
        n.pop("tab"), n.pop("x"), n.pop("x_came"), n.pop("y"), n.pop("y_came"), rows, count, kind
    )
    w_gate, w_up, downs = n.pop("w_gate"), n.pop("w_up"), n.pop("downs")
    plan.gather("b", shard(1))
    plan.gather("c", shard(2))
    plan.fence()
    plan.double("q", -1)
    plan.double("o", 1)
    early("a", last - 1)
    plan.fence()

    qkv_bufs = plan.gathered("q")
    n["gains"] = gains = jnp.concatenate([b[:, wide:] for b in qkv_bufs], axis=0)
    plan.double("o", 0)
    plan.double("a", 1)
    plan.double("b", last)
    n["normed"], n["qkv"] = project(n["xt"].astype(BF16), n["r1"], gains, qkv_bufs, wide)
    plan.fence()
    plan.double("o", -1)
    plan.double("a", 0)
    early("b", last - 1)
    n["att"], n["den"] = attend(tab, n["qkv"], rows, count, kind)
    plan.fence()
    plan.double("a", -1)
    plan.double("b", 1)
    plan.double("c", last)
    n["res"], n["r2"], n["x2t"], n["x2"] = middle(
        tab, n["att"].astype(BF16), plan.gathered("o"), n["xt"].astype(BF16), n["gains"], rows, count
    )
    plan.fence()

    def feed_group(name):
        sums = (n["pull"], n["push"]) if "pull" in n else ()
        send, keep, n["pull"], n["push"] = feed(
            n["x2"], n["x2t"], n["yn"], n["yt"].astype(BF16), plan.gathered(name), sums,
            4 if name == names[-1] else 3,
        )
        for end in ("", "+", "-", "-+"):
            n.pop(name + end)
        plan.reduce("g" + name, send, keep)

    plan.double("b", 0)
    early("c", last - 1)
    feed_group("a")
    plan.fence()
    plan.double("b", -1)
    plan.double("c", 1)
    plan.fence()
    plan.double("c", 0)
    plan.halve("ga", -1)
    feed_group("b")
    plan.fence()
    plan.double("c", -1)
    plan.fence()
    plan.halve("ga", 0)
    plan.halve("gb", -1)
    feed_group("c")
    plan.fence()
    plan.halve("gb", 0)
    n["dres"], n["dm"] = back(
        tab, n.pop("pull"), n["res"], n["r2"], n["yt"].astype(BF16), n["gains"], rows, count, kind
    )
    send, keep, n["datt"] = mixed(
        n.pop("dm").astype(BF16),
        n["att"].astype(BF16),
        plan.gathered("o"),
        n.pop("gc.send"),
        n.pop("gc"),
    )
    plan.reduce("gc", send, keep)
    plan.fence()

    def heads_back(part):
        for k, v in zip(
            ("dq", "dk", "dv"),
            attend_back(
                tab, n["qkv"], n["datt"], n["att"], n["den"], BACK_PARTS[part], rows, count
            ),
        ):
            n[k + str(part)] = v

    plan.halve("ga", 1)
    plan.halve("gc", -1)
    heads_back(0)
    plan.fence()
    plan.halve("gb", 1)
    plan.halve("ga", 2)
    heads_back(1)
    plan.fence()
    plan.halve("gc", 0)
    for stage in range(3, bits):
        plan.halve("ga", stage)
    plan.halve("gb", 2)
    heads_back(2)
    n["grads"] = jnp.concatenate(
        [n.pop(k + str(p)) for k in ("dq", "dk", "dv") for p in range(len(BACK_PARTS))], axis=0
    )
    plan.fence()
    plan.halve("gc", 1)
    for stage in range(3, bits):
        plan.halve("gb", stage)
    send, keep = weights_of(n["normed"], n["grads"])
    plan.reduce("gq", send, keep)
    plan.fence()
    plan.halve("gq", -1)
    n["sum_a"] = plan.reduced("ga")
    plan.fence()
    plan.halve("gq", 0)
    plan.halve("gc", 2)
    n["dx"] = input_of(
        tab, n["grads"], plan.gathered("q"), n["gains"], n["dres"], n["xt"].astype(BF16), n["r1"], rows, count, kind
    )
    n["out"] = output_of(tab, n.pop("push"), n["res"], rows, count, kind)
    plan.fence()

    def exchange(name):
        value = n.pop(name)
        n[name + "_own"] = lax.dynamic_slice_in_dim(value, core * half, half, 0)
        n[name + "_came"] = plan.send(lax.dynamic_slice_in_dim(value, (1 - core) * half, half, 0), -1)

    def give_back(name):
        own, came = n.pop(name + "_own"), n.pop(name + "_came")
        first = core == 0
        both = jnp.stack([jnp.where(first, own, came), jnp.where(first, came, own)])
        return both.reshape(micro, 1, half, width)

    plan.halve("gq", 1)
    for stage in range(3, bits):
        plan.halve("gc", stage)
    exchange("dx")
    exchange("out")
    n["sum_b"] = plan.reduced("gb")
    plan.fence()
    plan.halve("gq", 2)
    n["dx"] = give_back("dx")
    n["out"] = give_back("out")
    plan.fence()
    for stage in range(3, bits):
        plan.halve("gq", stage)
    last_sum = plan.reduced("gc")
    ff = jnp.concatenate([n["sum_a"], n["sum_b"], last_sum[:3]], axis=-1)[:, :, :hidden]
    n["gain_two"] = (
        jnp.sum(w_gate.astype(F32) * ff[0] + w_up.astype(F32) * ff[1], axis=1)
    ) / gain_two.astype(F32)
    n["ff0"], n["ff1"], n["ff2"] = ff[0], ff[1], ff[2].T
    n["grad_out"] = last_sum[3]
    plan.fence()
    grad_qkv = plan.reduced("gq")
    a, b = w_query.shape[1], w_query.shape[1] + w_key.shape[1]
    gain_one_grad = jnp.sum(own_qkv.astype(F32) * grad_qkv, axis=1) / gain_one.astype(F32)
    return (
        n["out"],
        n["dx"],
        grad_qkv[:, :a],
        grad_qkv[:, a:b],
        grad_qkv[:, b:],
        n["grad_out"],
        n["ff0"],
        n["ff1"],
        n["ff2"],
        gain_one_grad,
        n["gain_two"],
    )


def solution(mesh):
    shard = P(AXES, None)
    batch = P(None, "dp", "seq", None)
    return jax.shard_map(
        per_device,
        mesh=mesh,
        in_specs=(batch,) + (shard,) * 6 + (P(None, AXES), P(AXES), P(AXES), batch),
        out_specs=(batch,) * 2 + (shard,) * 6 + (P(None, AXES), P(AXES), P(AXES)),
        check_vma=False,
    )
```

```python
import functools

import jax
import jax.numpy as jnp
import numpy as np
from jax import lax
from jax.experimental import pallas as pl
from jax.experimental.pallas import tpu as pltpu
from jax.sharding import PartitionSpec as P

H = 16
F = 16
DV = 64
AXES = ("dp", "seq")
EPS = 1e-06
TB = 256
HEADS = 2
BACK_HEADS = 2
BACK_PARTS = ((0, 4), (4, 4), (8, 8))
TILE = 256
F32 = jnp.float32
BF16 = jnp.bfloat16

NN = (((1,), (0,)), ((), ()))
NT = (((1,), (1,)), ((), ()))
TN = (((0,), (0,)), ((), ()))


def dot(a, b, dims=NN):
    return lax.dot_general(a, b, dims, preferred_element_type=F32)


VMEM = pl.BlockSpec(memory_space=pltpu.VMEM)
SMEM = pl.BlockSpec(memory_space=pltpu.SMEM)


def params(mib):
    return pltpu.CompilerParams(vmem_limit_bytes=mib << 20)


def cost(flops, nbytes, trans=0):
    return pl.CostEstimate(flops=int(flops), bytes_accessed=int(nbytes), transcendentals=int(trans))


def sds(shape, dtype):
    return jax.ShapeDtypeStruct(shape, dtype)


def far(shape, dtype):
    return pltpu.HBM(shape, dtype)


def keep_far(*values):
    return [pltpu.with_memory_space_constraint(v, pltpu.HBM) for v in values]


def stage_orders(bits):
    straight = list(range(bits))
    swapped = [1, 0] + list(range(2, bits)) if bits > 1 else straight
    return (straight, swapped)


def stage_pairs(dp, bits, stage):
    orders = stage_orders(bits)
    return [
        (d * 2 + c, (d ^ (1 << orders[c][stage])) * 2 + c) for d in range(dp) for c in range(2)
    ]


def core_pairs(dp):
    return [(i, i ^ 1) for i in range(2 * dp)]


def block_tables(dp, bits):
    orders = stage_orders(bits)
    count = 2 * dp
    position = np.arange(count)
    masks, fixed = [], np.zeros(count, np.int32)
    for c in range(2):
        mask = np.zeros(count, np.int32)
        for stage in range(2):
            mask |= ((position >> (bits - 1 - stage)) & 1) << orders[c][stage]
        masks.append(mask)
    for stage in range(2, bits):
        fixed |= ((position >> (bits - 1 - stage)) & 1) << stage
    d = lax.axis_index("dp").astype(jnp.int32)
    c = lax.axis_index("seq").astype(jnp.int32)
    owner_core = jnp.asarray(position >> bits, jnp.int32) ^ c
    mask = jnp.where(owner_core == 0, jnp.asarray(masks[0]), jnp.asarray(masks[1]))
    block_at = (((d & 3) ^ mask) | jnp.asarray(fixed)) * 2 + owner_core
    block_core = jnp.asarray(position & 1, jnp.int32)
    owner = position >> 1
    low = np.zeros(count, np.int32)
    for stage in range(2, bits):
        low |= ((owner >> stage) & 1) << (bits - 1 - stage)
    apart = jnp.asarray(owner & 3, jnp.int32) ^ (d & 3)
    places = []
    for k in range(2):
        place = jnp.asarray(low)
        for stage in range(2):
            place = place | (((apart >> orders[k][stage]) & 1) << (bits - 1 - stage))
        places.append(place)
    place_of = jnp.where(block_core == 0, places[0], places[1]) | ((block_core ^ c) << bits)
    return jnp.concatenate([block_at, place_of, c[None], jnp.zeros(7, jnp.int32)]), c


class Plan:
    def __init__(self, dp, bits):
        self.dp, self.bits = dp, bits
        self.live, self.parts, self.air = {}, {}, {}

    def fence(self):
        self.live.update(lax.optimization_barrier(dict(self.live)))
        self.live.update(self.air)
        self.air = {}

    def after(self, key, names):
        tied = lax.optimization_barrier({k: self.live[k] for k in [key] + list(names)})
        self.live.update(tied)

    def pairs(self, stage):
        return core_pairs(self.dp) if stage < 0 else stage_pairs(self.dp, self.bits, stage)

    def send(self, value, stage):
        return lax.ppermute(value, AXES, self.pairs(stage))

    def gather(self, name, shard):
        self.live[name] = shard

    def bit(self, stage):
        return (lax.axis_index("dp") >> stage) & 1

    def double(self, name, stage, long=False):
        live = self.live
        if 0 <= stage < self.bits - 1:
            self.join(name, stage + 1)
        if stage >= 0:
            (self.air if long else live)[name + "+"] = self.send(live[name], stage)
            if stage == 0:
                live[name + "-"] = self.send(live[name], -1)
        else:
            live[name + "-+"] = self.send(live[name + "+"], -1)

    def join(self, name, stage):
        held, came = self.live[name], self.live.pop(name + "+")
        if stage >= 2:
            first = self.bit(stage) == 0
            held, came = jnp.where(first, held, came), jnp.where(first, came, held)
        self.live[name] = jnp.concatenate([held, came], axis=-2)

    def gathered(self, name):
        return tuple(self.live[name + end] for end in ("", "+", "-", "-+"))

    def reduce(self, name, send, keep):
        self.live[name + ".send"], self.live[name] = send, keep
        self.parts[name] = [(name, 0)]

    def prep(self, name, stage):
        if stage < 0:
            return
        half = self.live[name].shape[-2] >> (stage + 1)
        parts = self.parts[name]
        if stage < 2:
            send = self.total(parts, half, half)
        else:
            bit = self.bit(stage)
            send = self.total(parts, (1 - bit) * half, half)
            self.parts[name] = [(key, off + bit * half) for key, off in parts]
        self.live[name + ".send"] = send.astype(BF16)

    def go(self, name, stage):
        key = f"{name}.{stage}"
        self.live[key] = self.send(self.live.pop(name + ".send"), stage)
        self.parts[name] = self.parts[name] + [(key, 0)]

    def halve(self, name, stage):
        self.prep(name, stage)
        self.go(name, stage)

    def total(self, parts, start, size):
        acc = None
        for key, off in parts:
            part = self.live[key]
            part = lax.dynamic_slice_in_dim(part, off + start, size, axis=part.ndim - 2)
            acc = part.astype(F32) if acc is None else acc + part.astype(F32)
        return acc

    def prep_far(self, name):
        if self.bits > 4:
            return

        def code(place):
            out = 0
            for stage in range(2, self.bits):
                out = out | (((place >> (stage - 2)) & 1) << (self.bits - 1 - stage))
            return out

        rows = self.live[name].shape[-2] >> self.bits
        mine = lax.axis_index("dp") >> 2
        parts = self.parts[name]
        for apart in range(1, self.dp >> 2):
            send = self.total(parts, code(mine ^ apart) * rows, rows)
            self.live[f"{name}.far{apart}"] = send.astype(BF16)
        self.parts[name] = [(key, off + code(mine) * rows) for key, off in parts]

    def go_far(self, name):
        if self.bits > 4:
            for stage in range(2, self.bits):
                self.halve(name, stage)
            return
        for apart in range(1, self.dp >> 2):
            pairs = [(d * 2 + c, (d ^ (apart << 2)) * 2 + c) for d in range(self.dp) for c in range(2)]
            key = f"{name}.far{apart}"
            self.live[key] = lax.ppermute(self.live[key], AXES, pairs)
            self.parts[name] = self.parts[name] + [(key, 0)]

    def reduced(self, name):
        return self.total(self.parts[name], 0, self.live[name].shape[-2] >> self.bits)


def pre_kernel(rows, count, blocks, tab, x, xr, y, yr, xt, r1, yt, yn, buf):
    own = pl.program_id(0) // blocks == tab[2 * count]
    width = xt.shape[0]
    total = jnp.zeros(r1.shape, F32)
    for src, rec, dst in ((x, xr, xt), (y, yr, yt)):
        for i in range(width // 256):
            here = slice(i * 256, (i + 1) * 256)
            part = jnp.where(own, src[0, :, here], rec[:, here]).T
            buf[here, :] = part.astype(buf.dtype)
            if src is x:
                wide = part.astype(F32)
                total = total + jnp.sum(wide * wide, axis=0, keepdims=True)

        def move(p, _):
            at = pl.multiple_of(tab[p] * rows, rows)
            dst[pl.ds(pl.multiple_of(p * rows, rows), rows), :] = buf[pl.ds(at, rows), :]
            return 0

        lax.fori_loop(0, count, move, 0, unroll=4)
    for i in range(width // 256):
        here = slice(i * 256, (i + 1) * 256)
        yn[:, here] = yt[here, :].T.astype(BF16)
    r1[...] = lax.rsqrt(total / width + EPS)


def pre(tab, x, xr, y, yr, rows, count, kind):
    half, width = xr.shape
    tokens = 2 * half
    blocks = half // TB
    own = pl.BlockSpec((1, TB, width), lambda i, tab: (tab[2 * count], i % blocks, 0))
    came = pl.BlockSpec((TB, width), lambda i, tab: (i % blocks, 0))
    turned = pl.BlockSpec((width, TB), lambda i, tab: (0, i))
    return pl.pallas_call(
        functools.partial(pre_kernel, rows, count, blocks),
        grid_spec=pltpu.PrefetchScalarGridSpec(
            num_scalar_prefetch=1,
            grid=(tokens // TB,),
            in_specs=[own, came, own, came],
            out_specs=[
                turned,
                pl.BlockSpec((1, TB), lambda i, tab: (0, i)),
                turned,
                pl.BlockSpec((TB, width), lambda i, tab: (i, 0)),
            ],
            scratch_shapes=[pltpu.VMEM((width, TB), kind)],
        ),
        out_shape=(
            sds((width, tokens), kind),
            sds((1, tokens), F32),
            sds((width, tokens), kind),
            sds((tokens, width), BF16),
        ),
        compiler_params=params(14),
        cost_estimate=cost(8 * width * tokens, 14 * width * tokens),
        name="pre",
    )(tab, x, xr, y, yr)


def project_kernel(xt, r1, gains, w0, w1, w2, w3, normed, out):
    quarter = w0.shape[0]

    @pl.when(pl.program_id(0) == 0)
    def _():
        for q in range(4):
            here = slice(q * quarter, (q + 1) * quarter)
            part = xt[here, :].astype(F32) * r1[...] * gains[here, 0:1].astype(F32)
            normed[here, :] = part.astype(BF16)

    acc = dot(w0[...], normed[0:quarter, :], TN)
    for q, w in ((1, w1), (2, w2), (3, w3)):
        acc = acc + dot(w[...], normed[q * quarter : (q + 1) * quarter, :], TN)
    out[...] = acc.astype(BF16)


def project(xt, r1, gains, bufs, wide):
    width, tokens = xt.shape
    quarter = bufs[0].shape[0]
    return pl.pallas_call(
        project_kernel,
        grid=(wide // 256,),
        out_shape=(sds((width, tokens), BF16), sds((wide, tokens), BF16)),
        in_specs=[
            pl.BlockSpec((width, tokens), lambda i: (0, 0), pipeline_mode=pl.Buffered(1)),
            pl.BlockSpec((1, tokens), lambda i: (0, 0)),
            pl.BlockSpec((width, 128), lambda i: (0, 0)),
        ]
        + [pl.BlockSpec((quarter, 256), lambda i: (0, i))] * 4,
        out_specs=[
            pl.BlockSpec((width, tokens), lambda i: (0, 0)),
            pl.BlockSpec((256, tokens), lambda i: (i, 0)),
        ],
        compiler_params=params(16),
        cost_estimate=cost(2 * width * tokens * wide, 2 * (2 * width * tokens + 2 * wide * tokens)),
        name="project",
    )(xt, r1, gains, *keep_far(*bufs))


def unit_rows(tokens, ones):
    row = lax.broadcasted_iota(jnp.int32, (16, tokens), 0)
    return jnp.where(row < ones, 1.0, 0.0).astype(BF16)


def causal(shape):
    j = lax.broadcasted_iota(jnp.int32, shape, 0)
    t = lax.broadcasted_iota(jnp.int32, shape, 1)
    return j <= t


def attend_kernel(rows, count, tab, q, k, v, att, den):
    tokens = q.shape[1]
    blocks = tokens // TB
    one = unit_rows(tokens, 1)
    below = causal((TB, TB))
    heads = range(q.shape[0] // F)
    us, vas = [], []
    for n in heads:
        qa = q[n * F : (n + 1) * F, :] * jnp.asarray(F ** -0.5, BF16)
        qa = jnp.concatenate([qa, one], axis=0)
        ka = jnp.concatenate([k[n * F : (n + 1) * F, :], one], axis=0)
        vas.append(jnp.concatenate([v[n * DV : (n + 1) * DV, :], one], axis=0))
        us.append(
            [dot(ka[:, : (b + 1) * TB], qa[:, b * TB : (b + 1) * TB], TN) for b in range(blocks)]
        )
    ps = []
    for n in heads:
        ps.append([])
        for b in range(blocks):
            lo = b * TB
            p = us[n][b] * us[n][b] + 1.0
            last = jnp.where(below, p[lo:], 0.0).astype(BF16)
            ps[n].append(jnp.concatenate([p[:lo].astype(BF16), last], axis=0) if b else last)
    for n in heads:
        h = pl.program_id(0) * len(heads) + n
        for b in range(blocks):
            lo, hi = b * TB, (b + 1) * TB
            o = dot(vas[n][:, :hi], ps[n][b])
            d = o[DV : DV + 1]
            done = o[:DV] / d
            den[n, :, lo:hi] = d
            for i in range(DV // rows):
                at = tab[count + h * (DV // rows) + i]
                att[pl.ds(pl.multiple_of(at * rows, rows), rows), lo:hi] = done[
                    i * rows : (i + 1) * rows
                ].astype(att.dtype)


def head_specs(tokens, heads, off=0):
    return [
        pl.BlockSpec((F * heads, tokens), lambda h, *_: (off + h, 0)),
        pl.BlockSpec((F * heads, tokens), lambda h, *_: (H // heads + off + h, 0)),
        pl.BlockSpec((DV * heads, tokens), lambda h, *_: (2 * H * F // DV // heads + off + h, 0)),
    ]


def attend(tab, qkv, rows, count, kind):
    tokens = qkv.shape[1]
    heads = HEADS
    return pl.pallas_call(
        functools.partial(attend_kernel, rows, count),
        grid=(H // heads,),
        out_shape=(sds((H * DV, tokens), kind), sds((H, 1, tokens), F32)),
        in_specs=[SMEM] + head_specs(tokens, heads),
        out_specs=[
            pl.BlockSpec((H * DV, tokens), lambda h: (0, 0)),
            pl.BlockSpec((heads, 1, tokens), lambda h: (h, 0, 0)),
        ],
        compiler_params=params(28),
        cost_estimate=cost(H * tokens * tokens * 256 * 2, 4 * H * DV * tokens * 2),
        name="attend",
    )(tab, qkv, qkv, qkv)


def middle_kernel(rows, count, tab, w0, w1, w2, w3, att, xt, gains, res, r2, x2t, x2, wt, buf):
    width, tokens = xt.shape
    quarter = w0.shape[0]

    @pl.when(pl.program_id(0) == 0)
    def _():
        for q, w in enumerate((w0, w1, w2, w3)):
            for i in range(width // 256):
                wt[i * 256 : (i + 1) * 256, q * quarter : (q + 1) * quarter] = w[
                    :, i * 256 : (i + 1) * 256
                ].T

    buf[...] = dot(wt[...], att[...])

    def join(p, total):
        here = pl.ds(pl.multiple_of(p * rows, rows), rows)
        part = buf[pl.ds(pl.multiple_of(tab[p] * rows, rows), rows), :] + xt[here, :].astype(F32)
        res[here, :] = part
        return total + jnp.sum(part * part, axis=0, keepdims=True)

    total = lax.fori_loop(0, count, join, jnp.zeros((1, tokens), F32), unroll=4)
    scale = lax.rsqrt(total / width + EPS)
    r2[...] = scale
    for i in range(width // 256):
        here = slice(i * 256, (i + 1) * 256)
        low = (res[here, :] * scale * gains[here, 1:2].astype(F32)).astype(BF16)
        x2t[here, :] = low
        x2[:, here] = low.T


def middle(tab, att, bufs, xt, gains, rows, count):
    width, tokens = xt.shape
    inner = att.shape[0]
    quarter = bufs[0].shape[0]
    once = pl.BlockSpec((quarter, width), lambda i: (0, 0), pipeline_mode=pl.Buffered(1))
    return pl.pallas_call(
        functools.partial(middle_kernel, rows, count),
        grid=(tokens // TB,),
        out_shape=(
            far((width, tokens), F32),
            sds((1, tokens), F32),
            sds((width, tokens), BF16),
            sds((tokens, width), BF16),
        ),
        in_specs=[SMEM]
        + [once] * 4
        + [
            pl.BlockSpec((inner, TB), lambda i: (0, i)),
            pl.BlockSpec((width, TB), lambda i: (0, i)),
            pl.BlockSpec((width, 128), lambda i: (0, 0)),
        ],
        out_specs=[
            pl.BlockSpec((width, TB), lambda i: (0, i)),
            pl.BlockSpec((1, TB), lambda i: (0, i)),
            pl.BlockSpec((width, TB), lambda i: (0, i)),
            pl.BlockSpec((TB, width), lambda i: (i, 0)),
        ],
        scratch_shapes=[pltpu.VMEM((width, inner), BF16), pltpu.VMEM((width, TB), F32)],
        compiler_params=params(22),
        cost_estimate=cost(2 * width * tokens * inner, 16 * width * tokens),
        name="middle",
    )(tab, *keep_far(*bufs), att, *keep_far(xt), gains)


def feed_kernel(first, x2, x2t, dy, dyt, w0, w1, w2, w3, *refs):
    send, keep, pull, push = refs[-4:]
    quarter = w0.shape[1]
    bufs = (w0, w1, w2, w3)
    half = keep.shape[1]

    if first:

        @pl.when(pl.program_id(0) == 0)
        def _():
            pull[...] = jnp.zeros_like(pull)
            push[...] = jnp.zeros_like(push)

    def over(a, which):
        acc = dot(a[:, 0:quarter], w0[which])
        for q in range(1, 4):
            acc = acc + dot(a[:, q * quarter : (q + 1) * quarter], bufs[q][which])
        return acc

    def grad(i, a, b):
        whole = dot(a[...], b).astype(BF16)
        keep[i] = whole[:half]
        send[i] = whole[half:]

    gate = over(x2, 0)
    up = over(x2, 1)
    sig = 0.5 * jnp.tanh(0.5 * gate) + 0.5
    act = gate * sig
    h = (act * up).astype(BF16)
    back = over(dy, 2)
    dg = (back * up * (sig + act * (1.0 - sig))).astype(BF16)
    du = (back * act).astype(BF16)
    ht, dgt, dut = h.T, dg.T, du.T
    grad(2, dyt, h)
    for q, w in enumerate(bufs):
        here = slice(q * quarter, (q + 1) * quarter)
        push[here, :] = push[here, :] + dot(w[2], ht)
    grad(0, x2t, dg)
    grad(1, x2t, du)
    for q, w in enumerate(bufs):
        here = slice(q * quarter, (q + 1) * quarter)
        pull[here, :] = pull[here, :] + (dot(w[0], dgt) + dot(w[1], dut))


def feed(x2, x2t, dy, dyt, bufs, sums, slots=3):
    tokens, width = x2.shape
    cols = bufs[0].shape[-1]
    quarter = bufs[0].shape[1]
    return pl.pallas_call(
        functools.partial(feed_kernel, not sums),
        grid=(cols // TILE,),
        out_shape=(far((slots, width // 2, cols), BF16),) * 2 + (sds((width, tokens), F32),) * 2,
        in_specs=[VMEM] * 4
        + [pl.BlockSpec((3, quarter, TILE), lambda i: (0, 0, i))] * 4
        + [VMEM] * len(sums),
        out_specs=[pl.BlockSpec((3, width // 2, TILE), lambda i: (0, 0, i))] * 2 + [VMEM] * 2,
        input_output_aliases={8: 2, 9: 3} if sums else {},
        compiler_params=params(26),
        cost_estimate=cost(18 * tokens * width * cols, 2 * (4 * tokens * width + 9 * width * cols)),
        name="feed",
    )(x2, x2t, dy, dyt, *keep_far(*bufs), *sums)


def back_kernel(rows, count, tab, pull, res, r2, yt, gains, dres, dm, acc):
    width, tokens = acc.shape
    part = pull[...] * gains[:, 1:2].astype(F32)
    acc[...] = part
    total = jnp.sum(part * res[...], axis=0, keepdims=True)
    scale = r2[...]
    side = total / width * scale * scale * scale

    def second(p, _):
        here = pl.ds(pl.multiple_of(p * rows, rows), rows)
        part = yt[here, :].astype(F32) + scale * acc[here, :] - res[here, :] * side
        dres[here, :] = part
        dm[pl.ds(pl.multiple_of(tab[p] * rows, rows), rows), :] = part.astype(dm.dtype)
        return 0

    lax.fori_loop(0, count, second, 0, unroll=4)


def back(tab, pull, res, r2, yt, gains, rows, count, kind):
    width, tokens = res.shape
    block = pl.BlockSpec((width, TB), lambda i: (0, i))
    return pl.pallas_call(
        functools.partial(back_kernel, rows, count),
        grid=(tokens // TB,),
        out_shape=(far((width, tokens), F32), sds((width, tokens), kind)),
        in_specs=[
            SMEM,
            block,
            block,
            pl.BlockSpec((1, TB), lambda i: (0, i)),
            block,
            pl.BlockSpec((width, 128), lambda i: (0, 0)),
        ],
        out_specs=[block] * 2,
        scratch_shapes=[pltpu.VMEM((width, TB), F32)],
        compiler_params=params(20),
        cost_estimate=cost(10 * tokens * width, 16 * width * tokens),
        name="back",
    )(tab, pull, *keep_far(res), r2, *keep_far(yt), gains)


def turn_out(nat, own, other):
    width = nat.shape[0]
    for mine, ref in ((False, other), (True, own)):

        @pl.when((pl.program_id(0) >= pl.num_programs(0) // 2) == mine)
        def _(ref=ref):
            for i in range(width // 256):
                here = slice(i * 256, (i + 1) * 256)
                ref[:, here] = nat[here, :].T.astype(BF16)


def token_maps(tokens, count):
    blocks = tokens // TB // 2

    def at(i, tab):
        core = tab[2 * count]
        return jnp.where(i < blocks, (1 - core) * blocks + i, core * blocks + i - blocks)

    own = lambda i, tab: (jnp.maximum(i - blocks, 0), 0)
    other = lambda i, tab: (jnp.minimum(i, blocks - 1), 0)
    return at, own, other


def output_kernel(rows, count, tab, push, res, own, other, acc, nat):
    width, tokens = acc.shape
    acc[...] = push[...] + res[...]

    def move(p, _):
        here = pl.ds(pl.multiple_of(p * rows, rows), rows)
        to = pl.ds(pl.multiple_of(tab[p] * rows, rows), rows)
        nat[to, :] = acc[here, :].astype(nat.dtype)
        return 0

    lax.fori_loop(0, count, move, 0, unroll=4)
    turn_out(nat, own, other)


def output_of(tab, push, res, rows, count, kind):
    width, tokens = res.shape
    at, own, other = token_maps(tokens, count)
    block = pl.BlockSpec((width, TB), lambda i, tab: (0, at(i, tab)))
    return pl.pallas_call(
        functools.partial(output_kernel, rows, count),
        grid_spec=pltpu.PrefetchScalarGridSpec(
            num_scalar_prefetch=1,
            grid=(tokens // TB,),
            in_specs=[block, block],
            out_specs=[pl.BlockSpec((TB, width), own), pl.BlockSpec((TB, width), other)],
            scratch_shapes=[pltpu.VMEM((width, TB), F32), pltpu.VMEM((width, TB), kind)],
        ),
        out_shape=(sds((tokens // 2, width), BF16),) * 2,
        compiler_params=params(18),
        cost_estimate=cost(tokens * width, 10 * width * tokens),
        name="output_of",
    )(tab, *keep_far(push, res))


def mixed_kernel(dm, dm_rows, att, w0, w1, w2, w3, send_in, keep_in, send, keep, datt):
    quarter = w0.shape[0]
    half = keep.shape[1]
    right = dm[...]
    for q, w in enumerate((w0, w1, w2, w3)):
        datt[q * quarter : (q + 1) * quarter, :] = dot(w[...], right)
    whole = dot(att[...], dm_rows[...], NT).astype(BF16)
    keep[0] = whole[:half]
    send[0] = whole[half:]


def mixed(dm, att, bufs, send, keep):
    width, tokens = dm.shape
    rows = att.shape[0]
    quarter = bufs[0].shape[0]
    slot = keep.shape[0] - 1
    cols = width * TB // tokens
    return pl.pallas_call(
        mixed_kernel,
        grid=(tokens // TB,),
        out_shape=(far(send.shape, BF16), far(keep.shape, BF16), far((rows, tokens), F32)),
        in_specs=[
            pl.BlockSpec((width, TB), lambda i: (0, i)),
            pl.BlockSpec((cols, tokens), lambda i: (i, 0)),
            pl.BlockSpec((rows, tokens), lambda i: (0, 0), pipeline_mode=pl.Buffered(1)),
        ]
        + [pl.BlockSpec((quarter, width), lambda i: (0, 0), pipeline_mode=pl.Buffered(1))] * 4
        + [pl.BlockSpec(memory_space=pl.ANY)] * 2,
        out_specs=[pl.BlockSpec((1, rows // 2, cols), lambda i: (slot, 0, i))] * 2
        + [pl.BlockSpec((rows, TB), lambda i: (0, i))],
        input_output_aliases={7: 0, 8: 1},
        compiler_params=params(18),
        cost_estimate=cost(4 * width * tokens * rows, 12 * width * tokens),
        name="mixed",
    )(dm, dm, att, *keep_far(*bufs, send, keep))


def attend_back_kernel(rows, tab, q, k, v, den, *refs):
    many = q.shape[0] // F * (DV // rows)
    datts, atts = refs[:many], refs[many : 2 * many]
    dq, dk, dv, pt, st = refs[2 * many :]
    tokens = q.shape[1]
    blocks = tokens // TB
    scale = jnp.asarray(F ** -0.5, BF16)
    row = lax.broadcasted_iota(jnp.int32, (16, tokens), 0)
    one = unit_rows(tokens, 1)
    two = unit_rows(tokens, 2)
    zero = jnp.zeros((DV, tokens), BF16)
    below = causal((TB, TB))
    heads = range(q.shape[0] // F)
    us, gs, kss, rights_p, rights_s = [], [], [], [], []
    for n in heads:
        here = slice(n * (DV // rows), (n + 1) * (DV // rows))
        da = jnp.concatenate([r[...] for r in datts[here]], axis=0)
        done = jnp.concatenate([r[...].astype(F32) for r in atts[here]], axis=0)
        inv = 2.0 / den[n]
        dn = (da * inv).astype(BF16)
        dd = -jnp.sum(da * done, axis=0, keepdims=True) * inv
        dd_high = dd.astype(BF16).astype(F32)
        tail = jnp.where(row == 0, dd_high, jnp.where(row == 1, dd - dd_high, 0.0)).astype(BF16)
        qh, kh = q[n * F : (n + 1) * F, :], k[n * F : (n + 1) * F, :]
        qs = qh * scale
        kss.append(kh * scale)
        qa = jnp.concatenate([qs, one], axis=0)
        ka = jnp.concatenate([kh, one], axis=0)
        va = jnp.concatenate([v[n * DV : (n + 1) * DV, :], two], axis=0)
        na = jnp.concatenate([dn, tail], axis=0)
        rights_p.append(jnp.concatenate([dn * jnp.asarray(0.5, BF16), zero], axis=0).T)
        rights_s.append(jnp.concatenate([zero, qs, jnp.zeros((DV - F, tokens), BF16)], axis=0).T)
        us.append([dot(ka[:, : (b + 1) * TB], qa[:, b * TB : (b + 1) * TB], TN) for b in range(blocks)])
        gs.append([dot(va[:, : (b + 1) * TB], na[:, b * TB : (b + 1) * TB], TN) for b in range(blocks)])
    for n in heads:
        for b in range(blocks):
            lo, hi = b * TB, (b + 1) * TB
            u = us[n][b]
            p = u * u + 1.0
            s = gs[n][b] * u
            if b:
                pt[n, :lo, lo:hi] = p[:lo].astype(BF16)
                st[n, :lo, lo:hi] = s[:lo].astype(BF16)
            pt[n, lo:hi, lo:hi] = jnp.where(below, p[lo:], 0.0).astype(BF16)
            st[n, lo:hi, lo:hi] = jnp.where(below, s[lo:], 0.0).astype(BF16)
    for n in heads:
        for b in range(blocks):
            lo, hi = b * TB, (b + 1) * TB
            dq[n * F : (n + 1) * F, lo:hi] = dot(kss[n][:, :hi], st[n, :hi, lo:hi]).astype(BF16)
        for b in range(blocks):
            lo, hi = b * TB, (b + 1) * TB
            both = dot(pt[n, lo:hi, lo:], rights_p[n][lo:]) + dot(st[n, lo:hi, lo:], rights_s[n][lo:])
            turned = both.T
            dv[n * DV : (n + 1) * DV, lo:hi] = turned[:DV].astype(BF16)
            dk[n * F : (n + 1) * F, lo:hi] = turned[DV : DV + F].astype(BF16)


def attend_back(tab, qkv, datt, att, den, part, rows, count):
    tokens = qkv.shape[1]
    heads = BACK_HEADS
    base, many = part
    off = base // heads
    each = DV // rows

    def piece(i):
        return pl.BlockSpec(
            (rows, tokens),
            lambda h, tab: (tab[count + (base + h * heads) * each + i], 0),
        )

    pieces = [piece(i) for i in range(heads * each)]
    return pl.pallas_call(
        functools.partial(attend_back_kernel, rows),
        grid_spec=pltpu.PrefetchScalarGridSpec(
            num_scalar_prefetch=1,
            grid=(many // heads,),
            in_specs=head_specs(tokens, heads, off)
            + [pl.BlockSpec((heads, 1, tokens), lambda h, tab: (off + h, 0, 0))]
            + pieces * 2,
            out_specs=[
                pl.BlockSpec((F * heads, tokens), lambda h, tab: (h, 0)),
                pl.BlockSpec((F * heads, tokens), lambda h, tab: (h, 0)),
                pl.BlockSpec((DV * heads, tokens), lambda h, tab: (h, 0)),
            ],
            scratch_shapes=[pltpu.VMEM((heads, tokens, tokens), BF16)] * 2,
        ),
        out_shape=(
            sds((many * F, tokens), BF16),
            sds((many * F, tokens), BF16),
            sds((many * DV, tokens), BF16),
        ),
        compiler_params=params(44),
        cost_estimate=cost(many * tokens * tokens * 256 * 6, 8 * many * DV * tokens * 2),
        name="attend_back",
    )(tab, *keep_far(qkv, qkv, qkv, den), *keep_far(datt) * len(pieces), *keep_far(att) * len(pieces))


def weights_kernel(normed, right, send, keep):
    half = keep.shape[0]
    whole = dot(normed[...], right[...], NT).astype(BF16)
    keep[...] = whole[:half]
    send[...] = whole[half:]


def weights_of(normed, grads):
    width, tokens = normed.shape
    wide = grads.shape[0]
    col = pl.BlockSpec((width // 2, TILE), lambda i: (0, i))
    return pl.pallas_call(
        weights_kernel,
        grid=(wide // TILE,),
        out_shape=(far((width // 2, wide), BF16),) * 2,
        in_specs=[
            pl.BlockSpec((width, tokens), lambda i: (0, 0), pipeline_mode=pl.Buffered(1)),
            pl.BlockSpec((TILE, tokens), lambda i: (i, 0)),
        ],
        out_specs=[col] * 2,
        compiler_params=params(12),
        cost_estimate=cost(2 * width * tokens * wide, 6 * width * tokens + 4 * width * wide),
        name="weights_of",
    )(normed, grads)


def input_kernel(rows, count, tab, w0, w1, w2, w3, gains, grads, dres, xt, r1, own, other, buf, nat):
    width, tokens = xt.shape
    quarter = w0.shape[0]
    wide = grads.shape[0]
    total = jnp.zeros((1, tokens), F32)
    scale = r1[...]
    for q, w in enumerate((w0, w1, w2, w3)):
        here = slice(q * quarter, (q + 1) * quarter)
        part = dot(w[:, :wide], grads[...])
        part = part * gains[here, 0:1].astype(F32)
        buf[here, :] = part
        total = total + jnp.sum(part * xt[here, :].astype(F32), axis=0, keepdims=True)
    pull = total / width * scale * scale * scale

    def second(p, _):
        here = pl.ds(pl.multiple_of(p * rows, rows), rows)
        part = dres[here, :] + scale * buf[here, :] - xt[here, :].astype(F32) * pull
        nat[pl.ds(pl.multiple_of(tab[p] * rows, rows), rows), :] = part.astype(nat.dtype)
        return 0

    lax.fori_loop(0, count, second, 0, unroll=4)
    turn_out(nat, own, other)


def input_of(tab, grads, bufs, gains, dres, xt, r1, rows, count, kind):
    width, tokens = xt.shape
    wide = grads.shape[0]
    at, own, other = token_maps(tokens, count)
    once = pl.BlockSpec(bufs[0].shape, lambda i, tab: (0, 0), pipeline_mode=pl.Buffered(1))
    block = pl.BlockSpec((width, TB), lambda i, tab: (0, at(i, tab)))
    return pl.pallas_call(
        functools.partial(input_kernel, rows, count),
        grid_spec=pltpu.PrefetchScalarGridSpec(
            num_scalar_prefetch=1,
            grid=(tokens // TB,),
            in_specs=[once] * 4
            + [pl.BlockSpec((width, 128), lambda i, tab: (0, 0))]
            + [pl.BlockSpec((wide, TB), lambda i, tab: (0, at(i, tab)))]
            + [block, block, pl.BlockSpec((1, TB), lambda i, tab: (0, at(i, tab)))],
            out_specs=[pl.BlockSpec((TB, width), own), pl.BlockSpec((TB, width), other)],
            scratch_shapes=[pltpu.VMEM((width, TB), F32), pltpu.VMEM((width, TB), kind)],
        ),
        out_shape=(sds((tokens // 2, width), BF16),) * 2,
        compiler_params=params(20),
        cost_estimate=cost(2 * width * tokens * wide, 12 * width * tokens + 2 * wide * tokens),
        name="input_of",
    )(tab, *keep_far(*bufs), gains, grads, *keep_far(dres, xt), r1)


def split_columns(total):
    tiles = -(-total // TILE)
    first = -(-tiles // 3)
    second = -(-(tiles - first) // 2)
    return [n * TILE for n in (tiles - first - second, second, first)]


def per_device(
    inputs, w_query, w_key, w_value, w_out, w_gate, w_up, w_down, gain_one, gain_two, cotangent
):
    dp = lax.axis_size("dp")
    bits = dp.bit_length() - 1
    count = 2 * dp
    micro, _, half, width = inputs.shape
    rows = width // count
    kind = BF16 if rows % 16 == 0 else F32
    hidden = w_gate.shape[1]
    groups = split_columns(hidden)
    padded = sum(groups)
    tab, core = block_tables(dp, bits)
    plan = Plan(dp, bits)
    plan.quarter = width // 4
    live = lambda: plan.live
    last = bits - 1

    x = inputs.reshape(micro, half, width)
    y = cotangent.reshape(micro, half, width)
    wide = w_query.shape[1] + w_key.shape[1] + w_value.shape[1]
    pair = jnp.pad(jnp.stack([gain_one, gain_two], axis=1), ((0, 0), (0, 126)))
    own_qkv = jnp.concatenate([w_query, w_key, w_value], axis=1)
    fill = ((0, 0), (0, padded - hidden))
    plan.gather("q", jnp.concatenate([own_qkv, pair], axis=1))
    plan.live.update(x=x, y=y, tab=tab)

    names = ["a", "b", "c"]
    downs = w_down.T

    def shard(k):
        at, size = sum(groups[:k]), groups[k]
        parts = [v[:, at : at + size] for v in (w_gate, w_up, downs)]
        short = size - parts[0].shape[1]
        if short:
            parts = [jnp.pad(p, ((0, 0), (0, short))) for p in parts]
        return jnp.stack(parts)

    def early(name, first=last):
        for stage in range(first, 1, -1):
            plan.double(name, stage)

    n = plan.live

    plan.double("q", last)
    plan.gather("o", w_out)
    n.update(w_gate=w_gate, w_up=w_up, downs=downs)
    plan.fence()
    early("q", last - 1)
    n["x_came"] = plan.send(lax.dynamic_index_in_dim(x, 1 - core, 0, keepdims=False), -1)
    n["y_came"] = plan.send(lax.dynamic_index_in_dim(y, 1 - core, 0, keepdims=False), -1)
    plan.fence()
    plan.double("q", 1)
    plan.double("o", last)
    w_gate, w_up, downs = n["w_gate"], n["w_up"], n["downs"]
    plan.gather("a", shard(0))
    plan.fence()
    plan.double("q", 0)
    early("o", last - 1)
    plan.double("a", last)
    n["xt"], n["r1"], n["yt"], n["yn"] = pre(
        n.pop("tab"), n.pop("x"), n.pop("x_came"), n.pop("y"), n.pop("y_came"), rows, count, kind
    )
    w_gate, w_up, downs = n.pop("w_gate"), n.pop("w_up"), n.pop("downs")
    plan.gather("b", shard(1))
    plan.gather("c", shard(2))
    plan.fence()
    plan.double("q", -1)
    plan.double("o", 1)
    early("a", last - 1)
    plan.fence()

    qkv_bufs = plan.gathered("q")
    n["gains"] = gains = jnp.concatenate([b[:, wide:] for b in qkv_bufs], axis=0)
    plan.double("o", 0)
    plan.double("a", 1)
    plan.double("b", last)
    n["normed"], n["qkv"] = project(n["xt"].astype(BF16), n["r1"], gains, qkv_bufs, wide)
    plan.fence()
    plan.double("o", -1)
    plan.double("a", 0)
    early("b", last - 1)
    n["att"], n["den"] = attend(tab, n["qkv"], rows, count, kind)
    plan.fence()
    plan.double("a", -1)
    plan.double("b", 1)
    plan.double("c", last)
    n["res"], n["r2"], n["x2t"], n["x2"] = middle(
        tab, n["att"].astype(BF16), plan.gathered("o"), n["xt"].astype(BF16), n["gains"], rows, count
    )
    plan.fence()

    def feed_group(name):
        sums = (n["pull"], n["push"]) if "pull" in n else ()
        send, keep, n["pull"], n["push"] = feed(
            n["x2"], n["x2t"], n["yn"], n["yt"].astype(BF16), plan.gathered(name), sums,
            4 if name == names[-1] else 3,
        )
        for end in ("", "+", "-", "-+"):
            n.pop(name + end)
        plan.reduce("g" + name, send, keep)

    plan.double("b", 0)
    early("c", last - 1)
    feed_group("a")
    plan.fence()
    plan.double("b", -1)
    plan.double("c", 1)
    plan.fence()
    plan.double("c", 0)
    plan.halve("ga", -1)
    feed_group("b")
    plan.fence()
    plan.double("c", -1)
    plan.fence()
    plan.halve("ga", 0)
    plan.halve("gb", -1)
    feed_group("c")
    plan.fence()
    plan.halve("gb", 0)
    n["dres"], n["dm"] = back(
        tab, n.pop("pull"), n["res"], n["r2"], n["yt"].astype(BF16), n["gains"], rows, count, kind
    )
    send, keep, n["datt"] = mixed(
        n.pop("dm").astype(BF16),
        n["att"].astype(BF16),
        plan.gathered("o"),
        n.pop("gc.send"),
        n.pop("gc"),
    )
    plan.reduce("gc", send, keep)
    plan.fence()

    def heads_back(part):
        for k, v in zip(
            ("dq", "dk", "dv"),
            attend_back(
                tab, n["qkv"], n["datt"], n["att"], n["den"], BACK_PARTS[part], rows, count
            ),
        ):
            n[k + str(part)] = v

    plan.halve("ga", 1)
    plan.halve("gc", -1)
    heads_back(0)
    plan.fence()
    plan.halve("gb", 1)
    plan.halve("ga", 2)
    heads_back(1)
    plan.fence()
    plan.halve("gc", 0)
    for stage in range(3, bits):
        plan.halve("ga", stage)
    plan.halve("gb", 2)
    heads_back(2)
    n["grads"] = jnp.concatenate(
        [n.pop(k + str(p)) for k in ("dq", "dk", "dv") for p in range(len(BACK_PARTS))], axis=0
    )
    plan.fence()
    plan.halve("gc", 1)
    for stage in range(3, bits):
        plan.halve("gb", stage)
    send, keep = weights_of(n["normed"], n["grads"])
    plan.reduce("gq", send, keep)
    plan.fence()
    plan.halve("gq", -1)
    plan.prep_far("gc")
    plan.fence()
    plan.prep("gq", 0)
    plan.fence()

    def give_back(name):
        own, came = n.pop(name + "_own"), n.pop(name + "_came")
        first = core == 0
        both = jnp.stack([jnp.where(first, own, came), jnp.where(first, came, own)])
        return both.reshape(micro, 1, half, width)

    plan.go("gq", 0)
    plan.go_far("gc")
    n["dx_own"], n["dx_other"] = input_of(
        tab, n["grads"], plan.gathered("q"), n["gains"], n["dres"], n["xt"].astype(BF16), n["r1"], rows, count, kind
    )
    n["out_own"], n["out_other"] = output_of(tab, n.pop("push"), n["res"], rows, count, kind)
    plan.fence()
    plan.prep("gq", 1)
    plan.fence()
    plan.go("gq", 1)
    for name in ("dx", "out"):
        n[name + "_came"] = plan.send(n.pop(name + "_other"), -1)
    plan.after("dx_came", ["dx_own"] + [key for k in ("ga", "gb") for key, _ in plan.parts[k]])
    n["dx"] = give_back("dx")
    n["sum_a"] = plan.reduced("ga")
    n["sum_b"] = plan.reduced("gb")
    plan.fence()
    plan.prep_far("gq")
    plan.fence()
    plan.go_far("gq")
    first_landed = plan.parts["gq"][-1][0] if bits > 4 else "gq.far1"
    plan.after(
        first_landed,
        ["out_own", "out_came", "sum_a", "sum_b"] + [key for key, _ in plan.parts["gc"]],
    )
    n["out"] = give_back("out")
    last_sum = plan.reduced("gc")
    ff = jnp.concatenate([n["sum_a"], n["sum_b"], last_sum[:3]], axis=-1)[:, :, :hidden]
    n["gain_two"] = (
        jnp.sum(w_gate.astype(F32) * ff[0] + w_up.astype(F32) * ff[1], axis=1)
    ) / gain_two.astype(F32)
    n["ff0"], n["ff1"], n["ff2"] = ff[0], ff[1], ff[2].T
    n["grad_out"] = last_sum[3]
    plan.fence()
    grad_qkv = plan.reduced("gq")
    a, b = w_query.shape[1], w_query.shape[1] + w_key.shape[1]
    gain_one_grad = jnp.sum(own_qkv.astype(F32) * grad_qkv, axis=1) / gain_one.astype(F32)
    return (
        n["out"],
        n["dx"],
        grad_qkv[:, :a],
        grad_qkv[:, a:b],
        grad_qkv[:, b:],
        n["grad_out"],
        n["ff0"],
        n["ff1"],
        n["ff2"],
        gain_one_grad,
        n["gain_two"],
    )


def solution(mesh):
    shard = P(AXES, None)
    batch = P(None, "dp", "seq", None)
    return jax.shard_map(
        per_device,
        mesh=mesh,
        in_specs=(batch,) + (shard,) * 6 + (P(None, AXES), P(AXES), P(AXES), batch),
        out_specs=(batch,) * 2 + (shard,) * 6 + (P(None, AXES), P(AXES), P(AXES)),
        check_vma=False,
    )
```

```python
import functools

import jax
import jax.numpy as jnp
import numpy as np
from jax import lax
from jax.experimental import pallas as pl
from jax.experimental.pallas import tpu as pltpu
from jax.sharding import PartitionSpec as P

H = 16
F = 16
DV = 64
AXES = ("dp", "seq")
EPS = 1e-06
TB = 256
HEADS = 2
BACK_HEADS = 2
BACK_PARTS = ((0, 8), (8, 8))
TILE = 256
F32 = jnp.float32
BF16 = jnp.bfloat16

NN = (((1,), (0,)), ((), ()))
NT = (((1,), (1,)), ((), ()))
TN = (((0,), (0,)), ((), ()))


def dot(a, b, dims=NN):
    return lax.dot_general(a, b, dims, preferred_element_type=F32)


VMEM = pl.BlockSpec(memory_space=pltpu.VMEM)
SMEM = pl.BlockSpec(memory_space=pltpu.SMEM)


def params(mib):
    return pltpu.CompilerParams(vmem_limit_bytes=mib << 20)


def cost(flops, nbytes, trans=0):
    return pl.CostEstimate(flops=int(flops), bytes_accessed=int(nbytes), transcendentals=int(trans))


def sds(shape, dtype):
    return jax.ShapeDtypeStruct(shape, dtype)


def far(shape, dtype):
    return pltpu.HBM(shape, dtype)


def keep_far(*values):
    return [pltpu.with_memory_space_constraint(v, pltpu.HBM) for v in values]


def stage_orders(bits):
    straight = list(range(bits))
    swapped = [1, 0] + list(range(2, bits)) if bits > 1 else straight
    return (straight, swapped)


def stage_pairs(dp, bits, stage):
    orders = stage_orders(bits)
    return [
        (d * 2 + c, (d ^ (1 << orders[c][stage])) * 2 + c) for d in range(dp) for c in range(2)
    ]


def core_pairs(dp):
    return [(i, i ^ 1) for i in range(2 * dp)]


def block_tables(dp, bits):
    orders = stage_orders(bits)
    count = 2 * dp
    position = np.arange(count)
    masks = []
    for c in range(2):
        mask = np.zeros(count, np.int32)
        for stage in range(bits):
            mask |= ((position >> (bits - 1 - stage)) & 1) << orders[c][stage]
        masks.append(mask)
    d = lax.axis_index("dp").astype(jnp.int32)
    c = lax.axis_index("seq").astype(jnp.int32)
    owner_core = jnp.asarray(position >> bits, jnp.int32) ^ c
    mask = jnp.where(owner_core == 0, jnp.asarray(masks[0]), jnp.asarray(masks[1]))
    block_at = (d ^ mask) * 2 + owner_core
    block_core = jnp.asarray(position & 1, jnp.int32)
    apart = jnp.asarray(position >> 1, jnp.int32) ^ d
    places = []
    for k in range(2):
        place = jnp.zeros(count, jnp.int32)
        for stage in range(bits):
            place = place | (((apart >> orders[k][stage]) & 1) << (bits - 1 - stage))
        places.append(place)
    place_of = jnp.where(block_core == 0, places[0], places[1]) | ((block_core ^ c) << bits)
    return jnp.concatenate([block_at, place_of, c[None], jnp.zeros(7, jnp.int32)]), c


class Plan:
    def __init__(self, dp, bits):
        self.dp, self.bits = dp, bits
        self.live, self.parts, self.air = {}, {}, {}

    def fence(self):
        self.live.update(lax.optimization_barrier(dict(self.live)))
        self.live.update(self.air)
        self.air = {}

    def after(self, key, names):
        tied = lax.optimization_barrier({k: self.live[k] for k in [key] + list(names)})
        self.live.update(tied)

    def pairs(self, stage):
        return core_pairs(self.dp) if stage < 0 else stage_pairs(self.dp, self.bits, stage)

    def send(self, value, stage):
        return lax.ppermute(value, AXES, self.pairs(stage))

    def gather(self, name, shard):
        self.live[name] = shard

    def double(self, name, stage, long=False):
        live = self.live
        if 0 <= stage < self.bits - 1:
            self.join(name)
        if stage >= 0:
            (self.air if long else live)[name + "+"] = self.send(live[name], stage)
            if stage == 0:
                live[name + "-"] = self.send(live[name], -1)
        else:
            live[name + "-+"] = self.send(live[name + "+"], -1)

    def join(self, name):
        came = self.live.pop(name + "+")
        self.live[name] = jnp.concatenate([self.live[name], came], axis=-2)

    def gathered(self, name):
        return tuple(self.live[name + end] for end in ("", "+", "-", "-+"))

    def reduce(self, name, send, keep):
        self.live[name + ".send"], self.live[name] = send, keep
        self.parts[name] = [name]

    def prep(self, name, stage):
        if stage < 0:
            return
        half = self.live[name].shape[-2] >> (stage + 1)
        send = self.total(self.parts[name], half, half)
        self.live[name + ".send"] = send.astype(BF16)

    def go(self, name, stage):
        key = f"{name}.{stage}"
        self.live[key] = self.send(self.live.pop(name + ".send"), stage)
        self.parts[name].append(key)

    def halve(self, name, stage):
        self.prep(name, stage)
        self.go(name, stage)

    def total(self, parts, start, size):
        acc = None
        for key in parts:
            part = self.live[key]
            part = lax.slice_in_dim(part, start, start + size, axis=part.ndim - 2)
            acc = part.astype(F32) if acc is None else acc + part.astype(F32)
        return acc

    def prep_far(self, name):
        if self.bits > 4:
            return

        rows = self.live[name].shape[-2] >> self.bits
        for apart in range(1, self.dp >> 2):
            at = 0
            for stage in range(2, self.bits):
                at |= ((apart >> (stage - 2)) & 1) << (self.bits - 1 - stage)
            send = self.total(self.parts[name], at * rows, rows)
            self.live[f"{name}.far{apart}"] = send.astype(BF16)

    def go_far(self, name):
        if self.bits > 4:
            for stage in range(2, self.bits):
                self.halve(name, stage)
            return
        for apart in range(1, self.dp >> 2):
            pairs = [(d * 2 + c, (d ^ (apart << 2)) * 2 + c) for d in range(self.dp) for c in range(2)]
            key = f"{name}.far{apart}"
            self.live[key] = lax.ppermute(self.live[key], AXES, pairs)
            self.parts[name].append(key)

    def reduced(self, name):
        return self.total(self.parts[name], 0, self.live[name].shape[-2] >> self.bits)


def pre_kernel(rows, count, blocks, tab, x, xr, y, yr, xt, r1, yt, yn, buf):
    own = pl.program_id(0) // blocks == tab[2 * count]
    width = xt.shape[0]
    total = jnp.zeros(r1.shape, F32)
    for src, rec, dst in ((x, xr, xt), (y, yr, yt)):
        for i in range(width // 256):
            here = slice(i * 256, (i + 1) * 256)
            part = jnp.where(own, src[0, :, here], rec[:, here]).T
            buf[here, :] = part.astype(buf.dtype)
            if src is x:
                wide = part.astype(F32)
                total = total + jnp.sum(wide * wide, axis=0, keepdims=True)

        def move(p, _):
            at = pl.multiple_of(tab[p] * rows, rows)
            dst[pl.ds(pl.multiple_of(p * rows, rows), rows), :] = buf[pl.ds(at, rows), :]
            return 0

        lax.fori_loop(0, count, move, 0, unroll=4)
    for i in range(width // 256):
        here = slice(i * 256, (i + 1) * 256)
        yn[:, here] = yt[here, :].T.astype(BF16)
    r1[...] = lax.rsqrt(total / width + EPS)


def pre(tab, x, xr, y, yr, rows, count, kind):
    half, width = xr.shape
    tokens = 2 * half
    blocks = half // TB
    own = pl.BlockSpec((1, TB, width), lambda i, tab: (tab[2 * count], i % blocks, 0))
    came = pl.BlockSpec((TB, width), lambda i, tab: (i % blocks, 0))
    turned = pl.BlockSpec((width, TB), lambda i, tab: (0, i))
    return pl.pallas_call(
        functools.partial(pre_kernel, rows, count, blocks),
        grid_spec=pltpu.PrefetchScalarGridSpec(
            num_scalar_prefetch=1,
            grid=(tokens // TB,),
            in_specs=[own, came, own, came],
            out_specs=[
                turned,
                pl.BlockSpec((1, TB), lambda i, tab: (0, i)),
                turned,
                pl.BlockSpec((TB, width), lambda i, tab: (i, 0)),
            ],
            scratch_shapes=[pltpu.VMEM((width, TB), kind)],
        ),
        out_shape=(
            sds((width, tokens), kind),
            sds((1, tokens), F32),
            sds((width, tokens), kind),
            sds((tokens, width), BF16),
        ),
        compiler_params=params(14),
        cost_estimate=cost(8 * width * tokens, 14 * width * tokens),
        name="pre",
    )(tab, x, xr, y, yr)


def project_kernel(xt, r1, gains, w0, w1, w2, w3, normed, out):
    quarter = w0.shape[0]

    @pl.when(pl.program_id(0) == 0)
    def _():
        for q in range(4):
            here = slice(q * quarter, (q + 1) * quarter)
            part = xt[here, :].astype(F32) * r1[...] * gains[here, 0:1].astype(F32)
            normed[here, :] = part.astype(BF16)

    acc = dot(w0[...], normed[0:quarter, :], TN)
    for q, w in ((1, w1), (2, w2), (3, w3)):
        acc = acc + dot(w[...], normed[q * quarter : (q + 1) * quarter, :], TN)
    out[...] = acc.astype(BF16)


def project(xt, r1, gains, bufs, wide):
    width, tokens = xt.shape
    quarter = bufs[0].shape[0]
    return pl.pallas_call(
        project_kernel,
        grid=(wide // 256,),
        out_shape=(sds((width, tokens), BF16), sds((wide, tokens), BF16)),
        in_specs=[
            pl.BlockSpec((width, tokens), lambda i: (0, 0), pipeline_mode=pl.Buffered(1)),
            pl.BlockSpec((1, tokens), lambda i: (0, 0)),
            pl.BlockSpec((width, 128), lambda i: (0, 0)),
        ]
        + [pl.BlockSpec((quarter, 256), lambda i: (0, i))] * 4,
        out_specs=[
            pl.BlockSpec((width, tokens), lambda i: (0, 0)),
            pl.BlockSpec((256, tokens), lambda i: (i, 0)),
        ],
        compiler_params=params(16),
        cost_estimate=cost(2 * width * tokens * wide, 2 * (2 * width * tokens + 2 * wide * tokens)),
        name="project",
    )(xt, r1, gains, *keep_far(*bufs))


def unit_rows(tokens, ones):
    row = lax.broadcasted_iota(jnp.int32, (16, tokens), 0)
    return jnp.where(row < ones, 1.0, 0.0).astype(BF16)


def causal(shape):
    j = lax.broadcasted_iota(jnp.int32, shape, 0)
    t = lax.broadcasted_iota(jnp.int32, shape, 1)
    return j <= t


def attend_kernel(rows, count, tab, q, k, v, att, den):
    tokens = q.shape[1]
    blocks = tokens // TB
    one = unit_rows(tokens, 1)
    below = causal((TB, TB))
    heads = range(q.shape[0] // F)
    us, vas = [], []
    for n in heads:
        qa = q[n * F : (n + 1) * F, :] * jnp.asarray(F ** -0.5, BF16)
        qa = jnp.concatenate([qa, one], axis=0)
        ka = jnp.concatenate([k[n * F : (n + 1) * F, :], one], axis=0)
        vas.append(jnp.concatenate([v[n * DV : (n + 1) * DV, :], one], axis=0))
        us.append(
            [dot(ka[:, : (b + 1) * TB], qa[:, b * TB : (b + 1) * TB], TN) for b in range(blocks)]
        )
    ps = []
    for n in heads:
        ps.append([])
        for b in range(blocks):
            lo = b * TB
            p = us[n][b] * us[n][b] + 1.0
            last = jnp.where(below, p[lo:], 0.0).astype(BF16)
            ps[n].append(jnp.concatenate([p[:lo].astype(BF16), last], axis=0) if b else last)
    for n in heads:
        h = pl.program_id(0) * len(heads) + n
        for b in range(blocks):
            lo, hi = b * TB, (b + 1) * TB
            o = dot(vas[n][:, :hi], ps[n][b])
            d = o[DV : DV + 1]
            done = o[:DV] / d
            den[n, :, lo:hi] = d
            for i in range(DV // rows):
                at = tab[count + h * (DV // rows) + i]
                att[pl.ds(pl.multiple_of(at * rows, rows), rows), lo:hi] = done[
                    i * rows : (i + 1) * rows
                ].astype(att.dtype)


def head_specs(tokens, heads, off=0):
    return [
        pl.BlockSpec((F * heads, tokens), lambda h, *_: (off + h, 0)),
        pl.BlockSpec((F * heads, tokens), lambda h, *_: (H // heads + off + h, 0)),
        pl.BlockSpec((DV * heads, tokens), lambda h, *_: (2 * H * F // DV // heads + off + h, 0)),
    ]


def attend(tab, qkv, rows, count, kind):
    tokens = qkv.shape[1]
    heads = HEADS
    return pl.pallas_call(
        functools.partial(attend_kernel, rows, count),
        grid=(H // heads,),
        out_shape=(sds((H * DV, tokens), kind), sds((H, 1, tokens), F32)),
        in_specs=[SMEM] + head_specs(tokens, heads),
        out_specs=[
            pl.BlockSpec((H * DV, tokens), lambda h: (0, 0)),
            pl.BlockSpec((heads, 1, tokens), lambda h: (h, 0, 0)),
        ],
        compiler_params=params(28),
        cost_estimate=cost(H * tokens * tokens * 256 * 2, 4 * H * DV * tokens * 2),
        name="attend",
    )(tab, qkv, qkv, qkv)


def middle_kernel(rows, count, tab, w0, w1, w2, w3, att, xt, gains, res, r2, x2t, x2, wt, buf):
    width, tokens = xt.shape
    quarter = w0.shape[0]

    @pl.when(pl.program_id(0) == 0)
    def _():
        for q, w in enumerate((w0, w1, w2, w3)):
            for i in range(width // 256):
                wt[i * 256 : (i + 1) * 256, q * quarter : (q + 1) * quarter] = w[
                    :, i * 256 : (i + 1) * 256
                ].T

    buf[...] = dot(wt[...], att[...])

    def join(p, total):
        here = pl.ds(pl.multiple_of(p * rows, rows), rows)
        part = buf[pl.ds(pl.multiple_of(tab[p] * rows, rows), rows), :] + xt[here, :].astype(F32)
        res[here, :] = part
        return total + jnp.sum(part * part, axis=0, keepdims=True)

    total = lax.fori_loop(0, count, join, jnp.zeros((1, tokens), F32), unroll=4)
    scale = lax.rsqrt(total / width + EPS)
    r2[...] = scale
    for i in range(width // 256):
        here = slice(i * 256, (i + 1) * 256)
        low = (res[here, :] * scale * gains[here, 1:2].astype(F32)).astype(BF16)
        x2t[here, :] = low
        x2[:, here] = low.T


def middle(tab, att, bufs, xt, gains, rows, count):
    width, tokens = xt.shape
    inner = att.shape[0]
    quarter = bufs[0].shape[0]
    once = pl.BlockSpec((quarter, width), lambda i: (0, 0), pipeline_mode=pl.Buffered(1))
    return pl.pallas_call(
        functools.partial(middle_kernel, rows, count),
        grid=(tokens // TB,),
        out_shape=(
            far((width, tokens), F32),
            sds((1, tokens), F32),
            sds((width, tokens), BF16),
            sds((tokens, width), BF16),
        ),
        in_specs=[SMEM]
        + [once] * 4
        + [
            pl.BlockSpec((inner, TB), lambda i: (0, i)),
            pl.BlockSpec((width, TB), lambda i: (0, i)),
            pl.BlockSpec((width, 128), lambda i: (0, 0)),
        ],
        out_specs=[
            pl.BlockSpec((width, TB), lambda i: (0, i)),
            pl.BlockSpec((1, TB), lambda i: (0, i)),
            pl.BlockSpec((width, TB), lambda i: (0, i)),
            pl.BlockSpec((TB, width), lambda i: (i, 0)),
        ],
        scratch_shapes=[pltpu.VMEM((width, inner), BF16), pltpu.VMEM((width, TB), F32)],
        compiler_params=params(22),
        cost_estimate=cost(2 * width * tokens * inner, 16 * width * tokens),
        name="middle",
    )(tab, *keep_far(*bufs), att, *keep_far(xt), gains)


def feed_kernel(first, x2, x2t, dy, dyt, w0, w1, w2, w3, *refs):
    send, keep, pull, push = refs[-4:]
    quarter = w0.shape[1]
    bufs = (w0, w1, w2, w3)
    half = keep.shape[1]

    if first:

        @pl.when(pl.program_id(0) == 0)
        def _():
            pull[...] = jnp.zeros_like(pull)
            push[...] = jnp.zeros_like(push)

    def over(a, which):
        acc = dot(a[:, 0:quarter], w0[which])
        for q in range(1, 4):
            acc = acc + dot(a[:, q * quarter : (q + 1) * quarter], bufs[q][which])
        return acc

    def grad(i, a, b):
        whole = dot(a[...], b).astype(BF16)
        keep[i] = whole[:half]
        send[i] = whole[half:]

    gate = over(x2, 0)
    up = over(x2, 1)
    sig = 0.5 * jnp.tanh(0.5 * gate) + 0.5
    act = gate * sig
    h = (act * up).astype(BF16)
    back = over(dy, 2)
    dg = (back * up * (sig + act * (1.0 - sig))).astype(BF16)
    du = (back * act).astype(BF16)
    ht, dgt, dut = h.T, dg.T, du.T
    grad(2, dyt, h)
    for q, w in enumerate(bufs):
        here = slice(q * quarter, (q + 1) * quarter)
        push[here, :] = push[here, :] + dot(w[2], ht)
    grad(0, x2t, dg)
    grad(1, x2t, du)
    for q, w in enumerate(bufs):
        here = slice(q * quarter, (q + 1) * quarter)
        pull[here, :] = pull[here, :] + (dot(w[0], dgt) + dot(w[1], dut))


def feed(x2, x2t, dy, dyt, bufs, sums, slots=3):
    tokens, width = x2.shape
    cols = bufs[0].shape[-1]
    quarter = bufs[0].shape[1]
    return pl.pallas_call(
        functools.partial(feed_kernel, not sums),
        grid=(cols // TILE,),
        out_shape=(far((slots, width // 2, cols), BF16),) * 2 + (sds((width, tokens), F32),) * 2,
        in_specs=[VMEM] * 4
        + [pl.BlockSpec((3, quarter, TILE), lambda i: (0, 0, i))] * 4
        + [VMEM] * len(sums),
        out_specs=[pl.BlockSpec((3, width // 2, TILE), lambda i: (0, 0, i))] * 2 + [VMEM] * 2,
        input_output_aliases={8: 2, 9: 3} if sums else {},
        compiler_params=params(26),
        cost_estimate=cost(18 * tokens * width * cols, 2 * (4 * tokens * width + 9 * width * cols)),
        name="feed",
    )(x2, x2t, dy, dyt, *keep_far(*bufs), *sums)


def back_kernel(rows, count, tab, pull, res, r2, yt, gains, dres, dm, acc):
    width, tokens = acc.shape
    part = pull[...] * gains[:, 1:2].astype(F32)
    acc[...] = part
    total = jnp.sum(part * res[...], axis=0, keepdims=True)
    scale = r2[...]
    side = total / width * scale * scale * scale

    def second(p, _):
        here = pl.ds(pl.multiple_of(p * rows, rows), rows)
        part = yt[here, :].astype(F32) + scale * acc[here, :] - res[here, :] * side
        dres[here, :] = part
        dm[pl.ds(pl.multiple_of(tab[p] * rows, rows), rows), :] = part.astype(dm.dtype)
        return 0

    lax.fori_loop(0, count, second, 0, unroll=4)


def back(tab, pull, res, r2, yt, gains, rows, count, kind):
    width, tokens = res.shape
    block = pl.BlockSpec((width, TB), lambda i: (0, i))
    return pl.pallas_call(
        functools.partial(back_kernel, rows, count),
        grid=(tokens // TB,),
        out_shape=(far((width, tokens), F32), sds((width, tokens), kind)),
        in_specs=[
            SMEM,
            block,
            block,
            pl.BlockSpec((1, TB), lambda i: (0, i)),
            block,
            pl.BlockSpec((width, 128), lambda i: (0, 0)),
        ],
        out_specs=[block] * 2,
        scratch_shapes=[pltpu.VMEM((width, TB), F32)],
        compiler_params=params(20),
        cost_estimate=cost(10 * tokens * width, 16 * width * tokens),
        name="back",
    )(tab, pull, *keep_far(res), r2, *keep_far(yt), gains)


def turn_out(nat, own, other):
    width = nat.shape[0]
    for mine, ref in ((False, other), (True, own)):

        @pl.when((pl.program_id(0) >= pl.num_programs(0) // 2) == mine)
        def _(ref=ref):
            for i in range(width // 256):
                here = slice(i * 256, (i + 1) * 256)
                ref[:, here] = nat[here, :].T.astype(BF16)


def token_maps(tokens, count):
    blocks = tokens // TB // 2

    def at(i, tab):
        core = tab[2 * count]
        return jnp.where(i < blocks, (1 - core) * blocks + i, core * blocks + i - blocks)

    own = lambda i, tab: (jnp.maximum(i - blocks, 0), 0)
    other = lambda i, tab: (jnp.minimum(i, blocks - 1), 0)
    return at, own, other


def output_kernel(rows, count, tab, push, res, own, other, acc, nat):
    width, tokens = acc.shape
    acc[...] = push[...] + res[...]

    def move(p, _):
        here = pl.ds(pl.multiple_of(p * rows, rows), rows)
        to = pl.ds(pl.multiple_of(tab[p] * rows, rows), rows)
        nat[to, :] = acc[here, :].astype(nat.dtype)
        return 0

    lax.fori_loop(0, count, move, 0, unroll=4)
    turn_out(nat, own, other)


def output_of(tab, push, res, rows, count, kind):
    width, tokens = res.shape
    at, own, other = token_maps(tokens, count)
    block = pl.BlockSpec((width, TB), lambda i, tab: (0, at(i, tab)))
    return pl.pallas_call(
        functools.partial(output_kernel, rows, count),
        grid_spec=pltpu.PrefetchScalarGridSpec(
            num_scalar_prefetch=1,
            grid=(tokens // TB,),
            in_specs=[block, block],
            out_specs=[pl.BlockSpec((TB, width), own), pl.BlockSpec((TB, width), other)],
            scratch_shapes=[pltpu.VMEM((width, TB), F32), pltpu.VMEM((width, TB), kind)],
        ),
        out_shape=(sds((tokens // 2, width), BF16),) * 2,
        compiler_params=params(18),
        cost_estimate=cost(tokens * width, 10 * width * tokens),
        name="output_of",
    )(tab, *keep_far(push, res))


def mixed_kernel(dm, dm_rows, att, w0, w1, w2, w3, send_in, keep_in, send, keep, datt):
    quarter = w0.shape[0]
    half = keep.shape[1]
    right = dm[...]
    for q, w in enumerate((w0, w1, w2, w3)):
        datt[q * quarter : (q + 1) * quarter, :] = dot(w[...], right)
    whole = dot(att[...], dm_rows[...], NT).astype(BF16)
    keep[0] = whole[:half]
    send[0] = whole[half:]


def mixed(dm, att, bufs, send, keep):
    width, tokens = dm.shape
    rows = att.shape[0]
    quarter = bufs[0].shape[0]
    slot = keep.shape[0] - 1
    cols = width * TB // tokens
    return pl.pallas_call(
        mixed_kernel,
        grid=(tokens // TB,),
        out_shape=(far(send.shape, BF16), far(keep.shape, BF16), far((rows, tokens), F32)),
        in_specs=[
            pl.BlockSpec((width, TB), lambda i: (0, i)),
            pl.BlockSpec((cols, tokens), lambda i: (i, 0)),
            pl.BlockSpec((rows, tokens), lambda i: (0, 0), pipeline_mode=pl.Buffered(1)),
        ]
        + [pl.BlockSpec((quarter, width), lambda i: (0, 0), pipeline_mode=pl.Buffered(1))] * 4
        + [pl.BlockSpec(memory_space=pl.ANY)] * 2,
        out_specs=[pl.BlockSpec((1, rows // 2, cols), lambda i: (slot, 0, i))] * 2
        + [pl.BlockSpec((rows, TB), lambda i: (0, i))],
        input_output_aliases={7: 0, 8: 1},
        compiler_params=params(18),
        cost_estimate=cost(4 * width * tokens * rows, 12 * width * tokens),
        name="mixed",
    )(dm, dm, att, *keep_far(*bufs, send, keep))


def attend_back_kernel(rows, tab, q, k, v, den, *refs):
    many = q.shape[0] // F * (DV // rows)
    datts, atts = refs[:many], refs[many : 2 * many]
    dq, dk, dv, pt, st = refs[2 * many :]
    tokens = q.shape[1]
    blocks = tokens // TB
    scale = jnp.asarray(F ** -0.5, BF16)
    row = lax.broadcasted_iota(jnp.int32, (16, tokens), 0)
    one = unit_rows(tokens, 1)
    two = unit_rows(tokens, 2)
    zero = jnp.zeros((DV, tokens), BF16)
    below = causal((TB, TB))
    heads = range(q.shape[0] // F)
    us, gs, kss, rights_p, rights_s = [], [], [], [], []
    for n in heads:
        here = slice(n * (DV // rows), (n + 1) * (DV // rows))
        da = jnp.concatenate([r[...] for r in datts[here]], axis=0)
        done = jnp.concatenate([r[...].astype(F32) for r in atts[here]], axis=0)
        inv = 2.0 / den[n]
        dn = (da * inv).astype(BF16)
        dd = -jnp.sum(da * done, axis=0, keepdims=True) * inv
        dd_high = dd.astype(BF16).astype(F32)
        tail = jnp.where(row == 0, dd_high, jnp.where(row == 1, dd - dd_high, 0.0)).astype(BF16)
        qh, kh = q[n * F : (n + 1) * F, :], k[n * F : (n + 1) * F, :]
        qs = qh * scale
        kss.append(kh * scale)
        qa = jnp.concatenate([qs, one], axis=0)
        ka = jnp.concatenate([kh, one], axis=0)
        va = jnp.concatenate([v[n * DV : (n + 1) * DV, :], two], axis=0)
        na = jnp.concatenate([dn, tail], axis=0)
        rights_p.append(jnp.concatenate([dn * jnp.asarray(0.5, BF16), zero], axis=0).T)
        rights_s.append(jnp.concatenate([zero, qs, jnp.zeros((DV - F, tokens), BF16)], axis=0).T)
        us.append([dot(ka[:, : (b + 1) * TB], qa[:, b * TB : (b + 1) * TB], TN) for b in range(blocks)])
        gs.append([dot(va[:, : (b + 1) * TB], na[:, b * TB : (b + 1) * TB], TN) for b in range(blocks)])
    for n in heads:
        for b in range(blocks):
            lo, hi = b * TB, (b + 1) * TB
            u = us[n][b]
            p = u * u + 1.0
            s = gs[n][b] * u
            if b:
                pt[n, :lo, lo:hi] = p[:lo].astype(BF16)
                st[n, :lo, lo:hi] = s[:lo].astype(BF16)
            pt[n, lo:hi, lo:hi] = jnp.where(below, p[lo:], 0.0).astype(BF16)
            st[n, lo:hi, lo:hi] = jnp.where(below, s[lo:], 0.0).astype(BF16)
    for n in heads:
        for b in range(blocks):
            lo, hi = b * TB, (b + 1) * TB
            dq[n * F : (n + 1) * F, lo:hi] = dot(kss[n][:, :hi], st[n, :hi, lo:hi]).astype(BF16)
        for b in range(blocks):
            lo, hi = b * TB, (b + 1) * TB
            both = dot(pt[n, lo:hi, lo:], rights_p[n][lo:]) + dot(st[n, lo:hi, lo:], rights_s[n][lo:])
            turned = both.T
            dv[n * DV : (n + 1) * DV, lo:hi] = turned[:DV].astype(BF16)
            dk[n * F : (n + 1) * F, lo:hi] = turned[DV : DV + F].astype(BF16)


def attend_back(tab, qkv, datt, att, den, part, rows, count):
    tokens = qkv.shape[1]
    heads = BACK_HEADS
    base, many = part
    off = base // heads
    each = DV // rows

    def piece(i):
        return pl.BlockSpec(
            (rows, tokens),
            lambda h, tab: (tab[count + (base + h * heads) * each + i], 0),
        )

    pieces = [piece(i) for i in range(heads * each)]
    return pl.pallas_call(
        functools.partial(attend_back_kernel, rows),
        grid_spec=pltpu.PrefetchScalarGridSpec(
            num_scalar_prefetch=1,
            grid=(many // heads,),
            in_specs=head_specs(tokens, heads, off)
            + [pl.BlockSpec((heads, 1, tokens), lambda h, tab: (off + h, 0, 0))]
            + pieces * 2,
            out_specs=[
                pl.BlockSpec((F * heads, tokens), lambda h, tab: (h, 0)),
                pl.BlockSpec((F * heads, tokens), lambda h, tab: (h, 0)),
                pl.BlockSpec((DV * heads, tokens), lambda h, tab: (h, 0)),
            ],
            scratch_shapes=[pltpu.VMEM((heads, tokens, tokens), BF16)] * 2,
        ),
        out_shape=(
            sds((many * F, tokens), BF16),
            sds((many * F, tokens), BF16),
            sds((many * DV, tokens), BF16),
        ),
        compiler_params=params(44),
        cost_estimate=cost(many * tokens * tokens * 256 * 6, 8 * many * DV * tokens * 2),
        name="attend_back",
    )(tab, *keep_far(qkv, qkv, qkv, den), *keep_far(datt) * len(pieces), *keep_far(att) * len(pieces))


def weights_kernel(normed, right, send, keep):
    half = keep.shape[0]
    whole = dot(normed[...], right[...], NT).astype(BF16)
    keep[...] = whole[:half]
    send[...] = whole[half:]


def weights_of(normed, grads):
    width, tokens = normed.shape
    wide = grads.shape[0]
    col = pl.BlockSpec((width // 2, TILE), lambda i: (0, i))
    return pl.pallas_call(
        weights_kernel,
        grid=(wide // TILE,),
        out_shape=(far((width // 2, wide), BF16),) * 2,
        in_specs=[
            pl.BlockSpec((width, tokens), lambda i: (0, 0), pipeline_mode=pl.Buffered(1)),
            pl.BlockSpec((TILE, tokens), lambda i: (i, 0)),
        ],
        out_specs=[col] * 2,
        compiler_params=params(12),
        cost_estimate=cost(2 * width * tokens * wide, 6 * width * tokens + 4 * width * wide),
        name="weights_of",
    )(normed, grads)


def input_kernel(rows, count, tab, w0, w1, w2, w3, gains, grads, dres, xt, r1, own, other, buf, nat):
    width, tokens = xt.shape
    quarter = w0.shape[0]
    wide = grads.shape[0]
    total = jnp.zeros((1, tokens), F32)
    scale = r1[...]
    for q, w in enumerate((w0, w1, w2, w3)):
        here = slice(q * quarter, (q + 1) * quarter)
        part = dot(w[:, :wide], grads[...])
        part = part * gains[here, 0:1].astype(F32)
        buf[here, :] = part
        total = total + jnp.sum(part * xt[here, :].astype(F32), axis=0, keepdims=True)
    pull = total / width * scale * scale * scale

    def second(p, _):
        here = pl.ds(pl.multiple_of(p * rows, rows), rows)
        part = dres[here, :] + scale * buf[here, :] - xt[here, :].astype(F32) * pull
        nat[pl.ds(pl.multiple_of(tab[p] * rows, rows), rows), :] = part.astype(nat.dtype)
        return 0

    lax.fori_loop(0, count, second, 0, unroll=4)
    turn_out(nat, own, other)


def input_of(tab, grads, bufs, gains, dres, xt, r1, rows, count, kind):
    width, tokens = xt.shape
    wide = grads.shape[0]
    at, own, other = token_maps(tokens, count)
    once = pl.BlockSpec(bufs[0].shape, lambda i, tab: (0, 0), pipeline_mode=pl.Buffered(1))
    block = pl.BlockSpec((width, TB), lambda i, tab: (0, at(i, tab)))
    return pl.pallas_call(
        functools.partial(input_kernel, rows, count),
        grid_spec=pltpu.PrefetchScalarGridSpec(
            num_scalar_prefetch=1,
            grid=(tokens // TB,),
            in_specs=[once] * 4
            + [pl.BlockSpec((width, 128), lambda i, tab: (0, 0))]
            + [pl.BlockSpec((wide, TB), lambda i, tab: (0, at(i, tab)))]
            + [block, block, pl.BlockSpec((1, TB), lambda i, tab: (0, at(i, tab)))],
            out_specs=[pl.BlockSpec((TB, width), own), pl.BlockSpec((TB, width), other)],
            scratch_shapes=[pltpu.VMEM((width, TB), F32), pltpu.VMEM((width, TB), kind)],
        ),
        out_shape=(sds((tokens // 2, width), BF16),) * 2,
        compiler_params=params(20),
        cost_estimate=cost(2 * width * tokens * wide, 12 * width * tokens + 2 * wide * tokens),
        name="input_of",
    )(tab, *keep_far(*bufs), gains, grads, *keep_far(dres, xt), r1)


def split_columns(total):
    tiles = -(-total // TILE)
    first = -(-tiles // 3)
    second = -(-(tiles - first) // 2)
    return [n * TILE for n in (tiles - first - second, second, first)]


def per_device(
    inputs, w_query, w_key, w_value, w_out, w_gate, w_up, w_down, gain_one, gain_two, cotangent
):
    dp = lax.axis_size("dp")
    bits = dp.bit_length() - 1
    count = 2 * dp
    micro, _, half, width = inputs.shape
    rows = width // count
    kind = BF16 if rows % 16 == 0 else F32
    hidden = w_gate.shape[1]
    groups = split_columns(hidden)
    padded = sum(groups)
    tab, core = block_tables(dp, bits)
    plan = Plan(dp, bits)
    plan.quarter = width // 4
    live = lambda: plan.live
    last = bits - 1

    x = inputs.reshape(micro, half, width)
    y = cotangent.reshape(micro, half, width)
    wide = w_query.shape[1] + w_key.shape[1] + w_value.shape[1]
    pair = jnp.pad(jnp.stack([gain_one, gain_two], axis=1), ((0, 0), (0, 126)))
    own_qkv = jnp.concatenate([w_query, w_key, w_value], axis=1)
    fill = ((0, 0), (0, padded - hidden))
    plan.gather("q", jnp.concatenate([own_qkv, pair], axis=1))
    plan.live.update(x=x, y=y, tab=tab)

    names = ["a", "b", "c"]
    downs = w_down.T

    def shard(k):
        at, size = sum(groups[:k]), groups[k]
        parts = [v[:, at : at + size] for v in (w_gate, w_up, downs)]
        short = size - parts[0].shape[1]
        if short:
            parts = [jnp.pad(p, ((0, 0), (0, short))) for p in parts]
        return jnp.stack(parts)

    def early(name, first=last):
        for stage in range(first, 1, -1):
            plan.double(name, stage)

    n = plan.live

    plan.double("q", last)
    plan.gather("o", w_out)
    n.update(w_gate=w_gate, w_up=w_up, downs=downs)
    plan.fence()
    early("q", last - 1)
    n["x_came"] = plan.send(lax.dynamic_index_in_dim(n["x"], 1 - core, 0, keepdims=False), -1)
    n["y_came"] = plan.send(lax.dynamic_index_in_dim(n["y"], 1 - core, 0, keepdims=False), -1)
    plan.fence()
    plan.double("q", 1)
    plan.double("o", last)
    w_gate, w_up, downs = n["w_gate"], n["w_up"], n["downs"]
    plan.gather("a", shard(0))
    plan.fence()
    plan.double("q", 0)
    early("o", last - 1)
    plan.double("a", last)
    n["xt"], n["r1"], n["yt"], n["yn"] = pre(
        n.pop("tab"), n.pop("x"), n.pop("x_came"), n.pop("y"), n.pop("y_came"), rows, count, kind
    )
    w_gate, w_up, downs = n.pop("w_gate"), n.pop("w_up"), n.pop("downs")
    plan.gather("b", shard(1))
    plan.gather("c", shard(2))
    plan.fence()
    plan.double("q", -1)
    plan.double("o", 1)
    early("a", last - 1)
    plan.fence()

    qkv_bufs = plan.gathered("q")
    n["gains"] = gains = jnp.concatenate([b[:, wide:] for b in qkv_bufs], axis=0)
    plan.double("o", 0)
    plan.double("a", 1)
    plan.double("b", last)
    n["normed"], n["qkv"] = project(n["xt"].astype(BF16), n["r1"], gains, qkv_bufs, wide)
    plan.fence()
    plan.double("o", -1)
    plan.double("a", 0)
    early("b", last - 1)
    n["att"], n["den"] = attend(tab, n["qkv"], rows, count, kind)
    plan.fence()
    plan.double("a", -1)
    plan.double("b", 1)
    plan.double("c", last)
    n["res"], n["r2"], n["x2t"], n["x2"] = middle(
        tab, n["att"].astype(BF16), plan.gathered("o"), n["xt"].astype(BF16), n["gains"], rows, count
    )
    plan.fence()

    def feed_group(name):
        sums = (n["pull"], n["push"]) if "pull" in n else ()
        send, keep, n["pull"], n["push"] = feed(
            n["x2"], n["x2t"], n["yn"], n["yt"].astype(BF16), plan.gathered(name), sums,
            4 if name == names[-1] else 3,
        )
        for end in ("", "+", "-", "-+"):
            n.pop(name + end)
        plan.reduce("g" + name, send, keep)

    plan.double("b", 0)
    early("c", last - 1)
    feed_group("a")
    plan.fence()
    plan.double("b", -1)
    plan.double("c", 1)
    plan.fence()
    plan.double("c", 0)
    plan.halve("ga", -1)
    feed_group("b")
    plan.fence()
    plan.double("c", -1)
    plan.fence()
    plan.halve("ga", 0)
    plan.halve("gb", -1)
    feed_group("c")
    plan.fence()
    plan.halve("gb", 0)
    n["dres"], n["dm"] = back(
        tab, n.pop("pull"), n["res"], n["r2"], n["yt"].astype(BF16), n["gains"], rows, count, kind
    )
    send, keep, n["datt"] = mixed(
        n.pop("dm").astype(BF16),
        n["att"].astype(BF16),
        plan.gathered("o"),
        n.pop("gc.send"),
        n.pop("gc"),
    )
    plan.reduce("gc", send, keep)
    plan.fence()

    def heads_back(part):
        for k, v in zip(
            ("dq", "dk", "dv"),
            attend_back(
                tab, n["qkv"], n["datt"], n["att"], n["den"], BACK_PARTS[part], rows, count
            ),
        ):
            n[k + str(part)] = v

    plan.halve("ga", 1)
    plan.halve("gb", 1)
    plan.halve("gc", -1)
    heads_back(0)
    plan.fence()
    plan.halve("gc", 0)
    plan.halve("gb", 2)
    plan.prep_far("ga")
    plan.go_far("ga")
    heads_back(1)
    n["grads"] = jnp.concatenate(
        [n.pop(k + str(p)) for k in ("dq", "dk", "dv") for p in range(len(BACK_PARTS))], axis=0
    )
    plan.fence()
    plan.halve("gc", 1)
    for stage in range(3, bits):
        plan.halve("gb", stage)
    send, keep = weights_of(n["normed"], n["grads"])
    plan.reduce("gq", send, keep)
    plan.fence()
    plan.halve("gq", -1)
    plan.prep_far("gc")
    plan.fence()
    plan.prep("gq", 0)
    plan.fence()

    def give_back(name):
        own, came = n.pop(name + "_own"), n.pop(name + "_came")
        first = core == 0
        both = jnp.stack([jnp.where(first, own, came), jnp.where(first, came, own)])
        return both.reshape(micro, 1, half, width)

    plan.go("gq", 0)
    plan.go_far("gc")
    n["dx_own"], n["dx_other"] = input_of(
        tab, n["grads"], plan.gathered("q"), n["gains"], n["dres"], n["xt"].astype(BF16), n["r1"], rows, count, kind
    )
    n["out_own"], n["out_other"] = output_of(tab, n.pop("push"), n["res"], rows, count, kind)
    plan.fence()
    plan.prep("gq", 1)
    plan.fence()
    plan.go("gq", 1)
    for name in ("dx", "out"):
        n[name + "_came"] = plan.send(n.pop(name + "_other"), -1)
    plan.after("dx_came", ["dx_own"] + [key for k in ("ga", "gb") for key in plan.parts[k]])
    n["dx"] = give_back("dx")
    n["sum_a"] = plan.reduced("ga")
    n["sum_b"] = plan.reduced("gb")
    plan.fence()
    plan.prep_far("gq")
    plan.fence()
    plan.go_far("gq")
    first_landed = plan.parts["gq"][-1] if bits > 4 else "gq.far1"
    plan.after(
        first_landed,
        ["out_own", "out_came", "sum_a", "sum_b"] + list(plan.parts["gc"]),
    )
    n["out"] = give_back("out")
    last_sum = plan.reduced("gc")
    ff = jnp.concatenate([n["sum_a"], n["sum_b"], last_sum[:3]], axis=-1)[:, :, :hidden]
    n["gain_two"] = (
        jnp.sum(w_gate.astype(F32) * ff[0] + w_up.astype(F32) * ff[1], axis=1)
    ) / gain_two.astype(F32)
    n["ff0"], n["ff1"], n["ff2"] = ff[0], ff[1], ff[2].T
    n["grad_out"] = last_sum[3]
    plan.fence()
    grad_qkv = plan.reduced("gq")
    a, b = w_query.shape[1], w_query.shape[1] + w_key.shape[1]
    gain_one_grad = jnp.sum(own_qkv.astype(F32) * grad_qkv, axis=1) / gain_one.astype(F32)
    return (
        n["out"],
        n["dx"],
        grad_qkv[:, :a],
        grad_qkv[:, a:b],
        grad_qkv[:, b:],
        n["grad_out"],
        n["ff0"],
        n["ff1"],
        n["ff2"],
        gain_one_grad,
        n["gain_two"],
    )


def solution(mesh):
    shard = P(AXES, None)
    batch = P(None, "dp", "seq", None)
    return jax.shard_map(
        per_device,
        mesh=mesh,
        in_specs=(batch,) + (shard,) * 6 + (P(None, AXES), P(AXES), P(AXES), batch),
        out_specs=(batch,) * 2 + (shard,) * 6 + (P(None, AXES), P(AXES), P(AXES)),
        check_vma=False,
    )
```

```python
import functools

import jax
import jax.numpy as jnp
import numpy as np
from jax import lax
from jax.experimental import pallas as pl
from jax.experimental.pallas import tpu as pltpu
from jax.sharding import PartitionSpec as P

H = 16
F = 16
DV = 64
AXES = ("dp", "seq")
EPS = 1e-06
TB = 256
HEADS = 2
BACK_HEADS = 2
BACK_PARTS = ((0, 8), (8, 8))
TILE = 256
F32 = jnp.float32
BF16 = jnp.bfloat16

NN = (((1,), (0,)), ((), ()))
NT = (((1,), (1,)), ((), ()))
TN = (((0,), (0,)), ((), ()))


def dot(a, b, dims=NN):
    return lax.dot_general(a, b, dims, preferred_element_type=F32)


VMEM = pl.BlockSpec(memory_space=pltpu.VMEM)
SMEM = pl.BlockSpec(memory_space=pltpu.SMEM)


def params(mib):
    return pltpu.CompilerParams(vmem_limit_bytes=mib << 20)


def cost(flops, nbytes, trans=0):
    return pl.CostEstimate(flops=int(flops), bytes_accessed=int(nbytes), transcendentals=int(trans))


def sds(shape, dtype):
    return jax.ShapeDtypeStruct(shape, dtype)


def far(shape, dtype):
    return pltpu.HBM(shape, dtype)


def keep_far(*values):
    return [pltpu.with_memory_space_constraint(v, pltpu.HBM) for v in values]


def stage_orders(bits):
    straight = list(range(bits))
    swapped = [1, 0] + list(range(2, bits)) if bits > 1 else straight
    return (straight, swapped)


def stage_pairs(dp, bits, stage):
    orders = stage_orders(bits)
    return [
        (d * 2 + c, (d ^ (1 << orders[c][stage])) * 2 + c) for d in range(dp) for c in range(2)
    ]


def core_pairs(dp):
    return [(i, i ^ 1) for i in range(2 * dp)]


def block_tables(dp, bits):
    orders = stage_orders(bits)
    count = 2 * dp
    position = np.arange(count)
    masks = []
    for c in range(2):
        mask = np.zeros(count, np.int32)
        for stage in range(bits):
            mask |= ((position >> (bits - 1 - stage)) & 1) << orders[c][stage]
        masks.append(mask)
    d = lax.axis_index("dp").astype(jnp.int32)
    c = lax.axis_index("seq").astype(jnp.int32)
    owner_core = jnp.asarray(position >> bits, jnp.int32) ^ c
    mask = jnp.where(owner_core == 0, jnp.asarray(masks[0]), jnp.asarray(masks[1]))
    block_at = (d ^ mask) * 2 + owner_core
    block_core = jnp.asarray(position & 1, jnp.int32)
    apart = jnp.asarray(position >> 1, jnp.int32) ^ d
    places = []
    for k in range(2):
        place = jnp.zeros(count, jnp.int32)
        for stage in range(bits):
            place = place | (((apart >> orders[k][stage]) & 1) << (bits - 1 - stage))
        places.append(place)
    place_of = jnp.where(block_core == 0, places[0], places[1]) | ((block_core ^ c) << bits)
    return jnp.concatenate([block_at, place_of, c[None], jnp.zeros(7, jnp.int32)]), c


class Plan:
    def __init__(self, dp, bits):
        self.dp, self.bits = dp, bits
        self.live, self.parts, self.air = {}, {}, {}

    def fence(self):
        self.live.update(lax.optimization_barrier(dict(self.live)))
        self.live.update(self.air)
        self.air = {}

    def after(self, key, names):
        tied = lax.optimization_barrier({k: self.live[k] for k in [key] + list(names)})
        self.live.update(tied)

    def pairs(self, stage):
        return core_pairs(self.dp) if stage < 0 else stage_pairs(self.dp, self.bits, stage)

    def send(self, value, stage):
        return lax.ppermute(value, AXES, self.pairs(stage))

    def gather(self, name, shard):
        self.live[name] = shard

    def double(self, name, stage, long=False):
        live = self.live
        if 0 <= stage < self.bits - 1:
            self.join(name)
        if stage >= 0:
            (self.air if long else live)[name + "+"] = self.send(live[name], stage)
            if stage == 0:
                live[name + "-"] = self.send(live[name], -1)
        else:
            live[name + "-+"] = self.send(live[name + "+"], -1)

    def join(self, name):
        came = self.live.pop(name + "+")
        self.live[name] = jnp.concatenate([self.live[name], came], axis=-2)

    def gathered(self, name):
        return tuple(self.live[name + end] for end in ("", "+", "-", "-+"))

    def reduce(self, name, send, keep):
        self.live[name + ".send"], self.live[name] = send, keep
        self.parts[name] = [name]

    def prep(self, name, stage):
        if stage < 0:
            return
        half = self.live[name].shape[-2] >> (stage + 1)
        send = self.total(self.parts[name], half, half)
        self.live[name + ".send"] = send.astype(BF16)

    def go(self, name, stage):
        key = f"{name}.{stage}"
        self.live[key] = self.send(self.live.pop(name + ".send"), stage)
        self.parts[name].append(key)

    def halve(self, name, stage):
        self.prep(name, stage)
        self.go(name, stage)

    def total(self, parts, start, size):
        acc = None
        for key in parts:
            part = self.live[key]
            part = lax.slice_in_dim(part, start, start + size, axis=part.ndim - 2)
            acc = part.astype(F32) if acc is None else acc + part.astype(F32)
        return acc

    def prep_far(self, name):
        if self.bits > 4:
            return

        rows = self.live[name].shape[-2] >> self.bits
        for apart in range(1, self.dp >> 2):
            at = 0
            for stage in range(2, self.bits):
                at |= ((apart >> (stage - 2)) & 1) << (self.bits - 1 - stage)
            send = self.total(self.parts[name], at * rows, rows)
            self.live[f"{name}.far{apart}"] = send.astype(BF16)

    def go_far(self, name):
        if self.bits > 4:
            for stage in range(2, self.bits):
                self.halve(name, stage)
            return
        for apart in range(1, self.dp >> 2):
            pairs = [(d * 2 + c, (d ^ (apart << 2)) * 2 + c) for d in range(self.dp) for c in range(2)]
            key = f"{name}.far{apart}"
            self.live[key] = lax.ppermute(self.live[key], AXES, pairs)
            self.parts[name].append(key)

    def reduced(self, name):
        return self.total(self.parts[name], 0, self.live[name].shape[-2] >> self.bits)


def pre_kernel(rows, count, blocks, tab, x, xr, y, yr, xt, r1, yt, yn, buf):
    own = pl.program_id(0) // blocks == tab[2 * count]
    width = xt.shape[0]
    total = jnp.zeros(r1.shape, F32)
    for src, rec, dst in ((x, xr, xt), (y, yr, yt)):
        for i in range(width // 256):
            here = slice(i * 256, (i + 1) * 256)
            part = jnp.where(own, src[0, :, here], rec[0, :, here]).T
            buf[here, :] = part.astype(buf.dtype)
            if src is x:
                wide = part.astype(F32)
                total = total + jnp.sum(wide * wide, axis=0, keepdims=True)

        def move(p, _):
            at = pl.multiple_of(tab[p] * rows, rows)
            dst[pl.ds(pl.multiple_of(p * rows, rows), rows), :] = buf[pl.ds(at, rows), :]
            return 0

        lax.fori_loop(0, count, move, 0, unroll=4)
    for i in range(width // 256):
        here = slice(i * 256, (i + 1) * 256)
        yn[:, here] = yt[here, :].T.astype(BF16)
    r1[...] = lax.rsqrt(total / width + EPS)


def pre(tab, x, xr, y, yr, rows, count, kind):
    _, half, width = xr.shape
    tokens = 2 * half
    blocks = half // TB
    own = pl.BlockSpec((1, TB, width), lambda i, tab: (tab[2 * count], i % blocks, 0))
    turned = pl.BlockSpec((width, TB), lambda i, tab: (0, i))
    return pl.pallas_call(
        functools.partial(pre_kernel, rows, count, blocks),
        grid_spec=pltpu.PrefetchScalarGridSpec(
            num_scalar_prefetch=1,
            grid=(tokens // TB,),
            in_specs=[own] * 4,
            out_specs=[
                turned,
                pl.BlockSpec((1, TB), lambda i, tab: (0, i)),
                turned,
                pl.BlockSpec((TB, width), lambda i, tab: (i, 0)),
            ],
            scratch_shapes=[pltpu.VMEM((width, TB), kind)],
        ),
        out_shape=(
            sds((width, tokens), kind),
            sds((1, tokens), F32),
            sds((width, tokens), kind),
            sds((tokens, width), BF16),
        ),
        compiler_params=params(14),
        cost_estimate=cost(8 * width * tokens, 14 * width * tokens),
        name="pre",
    )(tab, x, xr, y, yr)


def project_kernel(xt, r1, gains, w0, w1, w2, w3, normed, out):
    quarter = w0.shape[0]

    @pl.when(pl.program_id(0) == 0)
    def _():
        for q in range(4):
            here = slice(q * quarter, (q + 1) * quarter)
            part = xt[here, :].astype(F32) * r1[...] * gains[here, 0:1].astype(F32)
            normed[here, :] = part.astype(BF16)

    acc = dot(w0[...], normed[0:quarter, :], TN)
    for q, w in ((1, w1), (2, w2), (3, w3)):
        acc = acc + dot(w[...], normed[q * quarter : (q + 1) * quarter, :], TN)
    out[...] = acc.astype(BF16)


def project(xt, r1, gains, bufs, wide):
    width, tokens = xt.shape
    quarter = bufs[0].shape[0]
    return pl.pallas_call(
        project_kernel,
        grid=(wide // 256,),
        out_shape=(sds((width, tokens), BF16), sds((wide, tokens), BF16)),
        in_specs=[
            pl.BlockSpec((width, tokens), lambda i: (0, 0), pipeline_mode=pl.Buffered(1)),
            pl.BlockSpec((1, tokens), lambda i: (0, 0)),
            pl.BlockSpec((width, 128), lambda i: (0, 0)),
        ]
        + [pl.BlockSpec((quarter, 256), lambda i: (0, i))] * 4,
        out_specs=[
            pl.BlockSpec((width, tokens), lambda i: (0, 0)),
            pl.BlockSpec((256, tokens), lambda i: (i, 0)),
        ],
        compiler_params=params(16),
        cost_estimate=cost(2 * width * tokens * wide, 2 * (2 * width * tokens + 2 * wide * tokens)),
        name="project",
    )(xt, r1, gains, *keep_far(*bufs))


def unit_rows(tokens, ones):
    row = lax.broadcasted_iota(jnp.int32, (16, tokens), 0)
    return jnp.where(row < ones, 1.0, 0.0).astype(BF16)


def causal(shape):
    j = lax.broadcasted_iota(jnp.int32, shape, 0)
    t = lax.broadcasted_iota(jnp.int32, shape, 1)
    return j <= t


def attend_kernel(rows, count, tab, q, k, v, att, den):
    tokens = q.shape[1]
    blocks = tokens // TB
    one = unit_rows(tokens, 1)
    below = causal((TB, TB))
    heads = range(q.shape[0] // F)
    us, vas = [], []
    for n in heads:
        qa = q[n * F : (n + 1) * F, :] * jnp.asarray(F ** -0.5, BF16)
        qa = jnp.concatenate([qa, one], axis=0)
        ka = jnp.concatenate([k[n * F : (n + 1) * F, :], one], axis=0)
        vas.append(jnp.concatenate([v[n * DV : (n + 1) * DV, :], one], axis=0))
        us.append(
            [dot(ka[:, : (b + 1) * TB], qa[:, b * TB : (b + 1) * TB], TN) for b in range(blocks)]
        )
    ps = []
    for n in heads:
        ps.append([])
        for b in range(blocks):
            lo = b * TB
            p = us[n][b] * us[n][b] + 1.0
            last = jnp.where(below, p[lo:], 0.0).astype(BF16)
            ps[n].append(jnp.concatenate([p[:lo].astype(BF16), last], axis=0) if b else last)
    for n in heads:
        h = pl.program_id(0) * len(heads) + n
        for b in range(blocks):
            lo, hi = b * TB, (b + 1) * TB
            o = dot(vas[n][:, :hi], ps[n][b])
            d = o[DV : DV + 1]
            done = o[:DV] / d
            den[n, :, lo:hi] = d
            for i in range(DV // rows):
                at = tab[count + h * (DV // rows) + i]
                att[pl.ds(pl.multiple_of(at * rows, rows), rows), lo:hi] = done[
                    i * rows : (i + 1) * rows
                ].astype(att.dtype)


def head_specs(tokens, heads, off=0):
    return [
        pl.BlockSpec((F * heads, tokens), lambda h, *_: (off + h, 0)),
        pl.BlockSpec((F * heads, tokens), lambda h, *_: (H // heads + off + h, 0)),
        pl.BlockSpec((DV * heads, tokens), lambda h, *_: (2 * H * F // DV // heads + off + h, 0)),
    ]


def attend(tab, qkv, rows, count, kind):
    tokens = qkv.shape[1]
    heads = HEADS
    return pl.pallas_call(
        functools.partial(attend_kernel, rows, count),
        grid=(H // heads,),
        out_shape=(sds((H * DV, tokens), kind), sds((H, 1, tokens), F32)),
        in_specs=[SMEM] + head_specs(tokens, heads),
        out_specs=[
            pl.BlockSpec((H * DV, tokens), lambda h: (0, 0)),
            pl.BlockSpec((heads, 1, tokens), lambda h: (h, 0, 0)),
        ],
        compiler_params=params(28),
        cost_estimate=cost(H * tokens * tokens * 256 * 2, 4 * H * DV * tokens * 2),
        name="attend",
    )(tab, qkv, qkv, qkv)


def middle_kernel(rows, count, tab, w0, w1, w2, w3, att, xt, gains, res, r2, x2t, x2, wt, buf):
    width, tokens = xt.shape
    quarter = w0.shape[0]

    @pl.when(pl.program_id(0) == 0)
    def _():
        for q, w in enumerate((w0, w1, w2, w3)):
            for i in range(width // 256):
                wt[i * 256 : (i + 1) * 256, q * quarter : (q + 1) * quarter] = w[
                    :, i * 256 : (i + 1) * 256
                ].T

    buf[...] = dot(wt[...], att[...])

    def join(p, total):
        here = pl.ds(pl.multiple_of(p * rows, rows), rows)
        part = buf[pl.ds(pl.multiple_of(tab[p] * rows, rows), rows), :] + xt[here, :].astype(F32)
        res[here, :] = part
        return total + jnp.sum(part * part, axis=0, keepdims=True)

    total = lax.fori_loop(0, count, join, jnp.zeros((1, tokens), F32), unroll=4)
    scale = lax.rsqrt(total / width + EPS)
    r2[...] = scale
    for i in range(width // 256):
        here = slice(i * 256, (i + 1) * 256)
        low = (res[here, :] * scale * gains[here, 1:2].astype(F32)).astype(BF16)
        x2t[here, :] = low
        x2[:, here] = low.T


def middle(tab, att, bufs, xt, gains, rows, count):
    width, tokens = xt.shape
    inner = att.shape[0]
    quarter = bufs[0].shape[0]
    once = pl.BlockSpec((quarter, width), lambda i: (0, 0), pipeline_mode=pl.Buffered(1))
    return pl.pallas_call(
        functools.partial(middle_kernel, rows, count),
        grid=(tokens // TB,),
        out_shape=(
            far((width, tokens), F32),
            sds((1, tokens), F32),
            sds((width, tokens), BF16),
            sds((tokens, width), BF16),
        ),
        in_specs=[SMEM]
        + [once] * 4
        + [
            pl.BlockSpec((inner, TB), lambda i: (0, i)),
            pl.BlockSpec((width, TB), lambda i: (0, i)),
            pl.BlockSpec((width, 128), lambda i: (0, 0)),
        ],
        out_specs=[
            pl.BlockSpec((width, TB), lambda i: (0, i)),
            pl.BlockSpec((1, TB), lambda i: (0, i)),
            pl.BlockSpec((width, TB), lambda i: (0, i)),
            pl.BlockSpec((TB, width), lambda i: (i, 0)),
        ],
        scratch_shapes=[pltpu.VMEM((width, inner), BF16), pltpu.VMEM((width, TB), F32)],
        compiler_params=params(22),
        cost_estimate=cost(2 * width * tokens * inner, 16 * width * tokens),
        name="middle",
    )(tab, *keep_far(*bufs), att, *keep_far(xt), gains)


def feed_kernel(first, x2, x2t, dy, dyt, w0, w1, w2, w3, *refs):
    send, keep, pull, push = refs[-4:]
    quarter = w0.shape[1]
    bufs = (w0, w1, w2, w3)
    half = keep.shape[1]

    if first:

        @pl.when(pl.program_id(0) == 0)
        def _():
            pull[...] = jnp.zeros_like(pull)
            push[...] = jnp.zeros_like(push)

    def over(a, which):
        acc = dot(a[:, 0:quarter], w0[which])
        for q in range(1, 4):
            acc = acc + dot(a[:, q * quarter : (q + 1) * quarter], bufs[q][which])
        return acc

    def grad(i, a, b):
        whole = dot(a[...], b).astype(BF16)
        keep[i] = whole[:half]
        send[i] = whole[half:]

    gate = over(x2, 0)
    up = over(x2, 1)
    sig = 0.5 * jnp.tanh(0.5 * gate) + 0.5
    act = gate * sig
    h = (act * up).astype(BF16)
    back = over(dy, 2)
    dg = (back * up * (sig + act * (1.0 - sig))).astype(BF16)
    du = (back * act).astype(BF16)
    ht, dgt, dut = h.T, dg.T, du.T
    grad(2, dyt, h)
    for q, w in enumerate(bufs):
        here = slice(q * quarter, (q + 1) * quarter)
        push[here, :] = push[here, :] + dot(w[2], ht)
    grad(0, x2t, dg)
    grad(1, x2t, du)
    for q, w in enumerate(bufs):
        here = slice(q * quarter, (q + 1) * quarter)
        pull[here, :] = pull[here, :] + (dot(w[0], dgt) + dot(w[1], dut))


def feed(x2, x2t, dy, dyt, bufs, sums, slots=3):
    tokens, width = x2.shape
    cols = bufs[0].shape[-1]
    quarter = bufs[0].shape[1]
    return pl.pallas_call(
        functools.partial(feed_kernel, not sums),
        grid=(cols // TILE,),
        out_shape=(far((slots, width // 2, cols), BF16),) * 2 + (sds((width, tokens), F32),) * 2,
        in_specs=[VMEM] * 4
        + [pl.BlockSpec((3, quarter, TILE), lambda i: (0, 0, i))] * 4
        + [VMEM] * len(sums),
        out_specs=[pl.BlockSpec((3, width // 2, TILE), lambda i: (0, 0, i))] * 2 + [VMEM] * 2,
        input_output_aliases={8: 2, 9: 3} if sums else {},
        compiler_params=params(26),
        cost_estimate=cost(18 * tokens * width * cols, 2 * (4 * tokens * width + 9 * width * cols)),
        name="feed",
    )(x2, x2t, dy, dyt, *keep_far(*bufs), *sums)


def back_kernel(rows, count, tab, pull, res, r2, yt, gains, dres, dm, acc):
    width, tokens = acc.shape
    part = pull[...] * gains[:, 1:2].astype(F32)
    acc[...] = part
    total = jnp.sum(part * res[...], axis=0, keepdims=True)
    scale = r2[...]
    side = total / width * scale * scale * scale

    def second(p, _):
        here = pl.ds(pl.multiple_of(p * rows, rows), rows)
        part = yt[here, :].astype(F32) + scale * acc[here, :] - res[here, :] * side
        dres[here, :] = part
        dm[pl.ds(pl.multiple_of(tab[p] * rows, rows), rows), :] = part.astype(dm.dtype)
        return 0

    lax.fori_loop(0, count, second, 0, unroll=4)


def back(tab, pull, res, r2, yt, gains, rows, count, kind):
    width, tokens = res.shape
    block = pl.BlockSpec((width, TB), lambda i: (0, i))
    return pl.pallas_call(
        functools.partial(back_kernel, rows, count),
        grid=(tokens // TB,),
        out_shape=(far((width, tokens), F32), sds((width, tokens), kind)),
        in_specs=[
            SMEM,
            block,
            block,
            pl.BlockSpec((1, TB), lambda i: (0, i)),
            block,
            pl.BlockSpec((width, 128), lambda i: (0, 0)),
        ],
        out_specs=[block] * 2,
        scratch_shapes=[pltpu.VMEM((width, TB), F32)],
        compiler_params=params(20),
        cost_estimate=cost(10 * tokens * width, 16 * width * tokens),
        name="back",
    )(tab, pull, *keep_far(res), r2, *keep_far(yt), gains)


def turn_out(nat, own, other):
    width = nat.shape[0]
    for mine, ref in ((False, other), (True, own)):

        @pl.when((pl.program_id(0) >= pl.num_programs(0) // 2) == mine)
        def _(ref=ref):
            for i in range(width // 256):
                here = slice(i * 256, (i + 1) * 256)
                ref[:, here] = nat[here, :].T.astype(BF16)


def token_maps(tokens, count):
    blocks = tokens // TB // 2

    def at(i, tab):
        core = tab[2 * count]
        return jnp.where(i < blocks, (1 - core) * blocks + i, core * blocks + i - blocks)

    own = lambda i, tab: (jnp.maximum(i - blocks, 0), 0)
    other = lambda i, tab: (jnp.minimum(i, blocks - 1), 0)
    return at, own, other


def output_kernel(rows, count, tab, push, res, own, other, acc, nat):
    width, tokens = acc.shape
    acc[...] = push[...] + res[...]

    def move(p, _):
        here = pl.ds(pl.multiple_of(p * rows, rows), rows)
        to = pl.ds(pl.multiple_of(tab[p] * rows, rows), rows)
        nat[to, :] = acc[here, :].astype(nat.dtype)
        return 0

    lax.fori_loop(0, count, move, 0, unroll=4)
    turn_out(nat, own, other)


def output_of(tab, push, res, rows, count, kind):
    width, tokens = res.shape
    at, own, other = token_maps(tokens, count)
    block = pl.BlockSpec((width, TB), lambda i, tab: (0, at(i, tab)))
    return pl.pallas_call(
        functools.partial(output_kernel, rows, count),
        grid_spec=pltpu.PrefetchScalarGridSpec(
            num_scalar_prefetch=1,
            grid=(tokens // TB,),
            in_specs=[block, block],
            out_specs=[pl.BlockSpec((TB, width), own), pl.BlockSpec((TB, width), other)],
            scratch_shapes=[pltpu.VMEM((width, TB), F32), pltpu.VMEM((width, TB), kind)],
        ),
        out_shape=(sds((tokens // 2, width), BF16),) * 2,
        compiler_params=params(18),
        cost_estimate=cost(tokens * width, 10 * width * tokens),
        name="output_of",
    )(tab, *keep_far(push, res))


def mixed_kernel(dm, dm_rows, att, w0, w1, w2, w3, send_in, keep_in, send, keep, datt):
    quarter = w0.shape[0]
    half = keep.shape[1]
    right = dm[...]
    for q, w in enumerate((w0, w1, w2, w3)):
        datt[q * quarter : (q + 1) * quarter, :] = dot(w[...], right)
    whole = dot(att[...], dm_rows[...], NT).astype(BF16)
    keep[0] = whole[:half]
    send[0] = whole[half:]


def mixed(dm, att, bufs, send, keep):
    width, tokens = dm.shape
    rows = att.shape[0]
    quarter = bufs[0].shape[0]
    slot = keep.shape[0] - 1
    cols = width * TB // tokens
    return pl.pallas_call(
        mixed_kernel,
        grid=(tokens // TB,),
        out_shape=(far(send.shape, BF16), far(keep.shape, BF16), far((rows, tokens), F32)),
        in_specs=[
            pl.BlockSpec((width, TB), lambda i: (0, i)),
            pl.BlockSpec((cols, tokens), lambda i: (i, 0)),
            pl.BlockSpec((rows, tokens), lambda i: (0, 0), pipeline_mode=pl.Buffered(1)),
        ]
        + [pl.BlockSpec((quarter, width), lambda i: (0, 0), pipeline_mode=pl.Buffered(1))] * 4
        + [pl.BlockSpec(memory_space=pl.ANY)] * 2,
        out_specs=[pl.BlockSpec((1, rows // 2, cols), lambda i: (slot, 0, i))] * 2
        + [pl.BlockSpec((rows, TB), lambda i: (0, i))],
        input_output_aliases={7: 0, 8: 1},
        compiler_params=params(18),
        cost_estimate=cost(4 * width * tokens * rows, 12 * width * tokens),
        name="mixed",
    )(dm, dm, att, *keep_far(*bufs, send, keep))


def attend_back_kernel(rows, tab, q, k, v, den, *refs):
    many = q.shape[0] // F * (DV // rows)
    datts, atts = refs[:many], refs[many : 2 * many]
    dq, dk, dv, pt, st = refs[2 * many :]
    tokens = q.shape[1]
    blocks = tokens // TB
    scale = jnp.asarray(F ** -0.5, BF16)
    row = lax.broadcasted_iota(jnp.int32, (16, tokens), 0)
    one = unit_rows(tokens, 1)
    two = unit_rows(tokens, 2)
    zero = jnp.zeros((DV, tokens), BF16)
    below = causal((TB, TB))
    heads = range(q.shape[0] // F)
    us, gs, kss, rights_p, rights_s = [], [], [], [], []
    for n in heads:
        here = slice(n * (DV // rows), (n + 1) * (DV // rows))
        da = jnp.concatenate([r[...] for r in datts[here]], axis=0)
        done = jnp.concatenate([r[...].astype(F32) for r in atts[here]], axis=0)
        inv = 2.0 / den[n]
        dn = (da * inv).astype(BF16)
        dd = -jnp.sum(da * done, axis=0, keepdims=True) * inv
        dd_high = dd.astype(BF16).astype(F32)
        tail = jnp.where(row == 0, dd_high, jnp.where(row == 1, dd - dd_high, 0.0)).astype(BF16)
        qh, kh = q[n * F : (n + 1) * F, :], k[n * F : (n + 1) * F, :]
        qs = qh * scale
        kss.append(kh * scale)
        qa = jnp.concatenate([qs, one], axis=0)
        ka = jnp.concatenate([kh, one], axis=0)
        va = jnp.concatenate([v[n * DV : (n + 1) * DV, :], two], axis=0)
        na = jnp.concatenate([dn, tail], axis=0)
        rights_p.append(jnp.concatenate([dn * jnp.asarray(0.5, BF16), zero], axis=0).T)
        rights_s.append(jnp.concatenate([zero, qs, jnp.zeros((DV - F, tokens), BF16)], axis=0).T)
        us.append([dot(ka[:, : (b + 1) * TB], qa[:, b * TB : (b + 1) * TB], TN) for b in range(blocks)])
        gs.append([dot(va[:, : (b + 1) * TB], na[:, b * TB : (b + 1) * TB], TN) for b in range(blocks)])
    for n in heads:
        for b in range(blocks):
            lo, hi = b * TB, (b + 1) * TB
            u = us[n][b]
            p = u * u + 1.0
            s = gs[n][b] * u
            if b:
                pt[n, :lo, lo:hi] = p[:lo].astype(BF16)
                st[n, :lo, lo:hi] = s[:lo].astype(BF16)
            pt[n, lo:hi, lo:hi] = jnp.where(below, p[lo:], 0.0).astype(BF16)
            st[n, lo:hi, lo:hi] = jnp.where(below, s[lo:], 0.0).astype(BF16)
    for n in heads:
        for b in range(blocks):
            lo, hi = b * TB, (b + 1) * TB
            dq[n * F : (n + 1) * F, lo:hi] = dot(kss[n][:, :hi], st[n, :hi, lo:hi]).astype(BF16)
        for b in range(blocks):
            lo, hi = b * TB, (b + 1) * TB
            both = dot(pt[n, lo:hi, lo:], rights_p[n][lo:]) + dot(st[n, lo:hi, lo:], rights_s[n][lo:])
            turned = both.T
            dv[n * DV : (n + 1) * DV, lo:hi] = turned[:DV].astype(BF16)
            dk[n * F : (n + 1) * F, lo:hi] = turned[DV : DV + F].astype(BF16)


def attend_back(tab, qkv, datt, att, den, part, rows, count):
    tokens = qkv.shape[1]
    heads = BACK_HEADS
    base, many = part
    off = base // heads
    each = DV // rows

    def piece(i):
        return pl.BlockSpec(
            (rows, tokens),
            lambda h, tab: (tab[count + (base + h * heads) * each + i], 0),
        )

    pieces = [piece(i) for i in range(heads * each)]
    return pl.pallas_call(
        functools.partial(attend_back_kernel, rows),
        grid_spec=pltpu.PrefetchScalarGridSpec(
            num_scalar_prefetch=1,
            grid=(many // heads,),
            in_specs=head_specs(tokens, heads, off)
            + [pl.BlockSpec((heads, 1, tokens), lambda h, tab: (off + h, 0, 0))]
            + pieces * 2,
            out_specs=[
                pl.BlockSpec((F * heads, tokens), lambda h, tab: (h, 0)),
                pl.BlockSpec((F * heads, tokens), lambda h, tab: (h, 0)),
                pl.BlockSpec((DV * heads, tokens), lambda h, tab: (h, 0)),
            ],
            scratch_shapes=[pltpu.VMEM((heads, tokens, tokens), BF16)] * 2,
        ),
        out_shape=(
            sds((many * F, tokens), BF16),
            sds((many * F, tokens), BF16),
            sds((many * DV, tokens), BF16),
        ),
        compiler_params=params(44),
        cost_estimate=cost(many * tokens * tokens * 256 * 6, 8 * many * DV * tokens * 2),
        name="attend_back",
    )(tab, *keep_far(qkv, qkv, qkv, den), *keep_far(datt) * len(pieces), *keep_far(att) * len(pieces))


def weights_kernel(normed, right, send, keep):
    half = keep.shape[0]
    whole = dot(normed[...], right[...], NT).astype(BF16)
    keep[...] = whole[:half]
    send[...] = whole[half:]


def weights_of(normed, grads):
    width, tokens = normed.shape
    wide = grads.shape[0]
    col = pl.BlockSpec((width // 2, TILE), lambda i: (0, i))
    return pl.pallas_call(
        weights_kernel,
        grid=(wide // TILE,),
        out_shape=(far((width // 2, wide), BF16),) * 2,
        in_specs=[
            pl.BlockSpec((width, tokens), lambda i: (0, 0), pipeline_mode=pl.Buffered(1)),
            pl.BlockSpec((TILE, tokens), lambda i: (i, 0)),
        ],
        out_specs=[col] * 2,
        compiler_params=params(12),
        cost_estimate=cost(2 * width * tokens * wide, 6 * width * tokens + 4 * width * wide),
        name="weights_of",
    )(normed, grads)


def input_kernel(rows, count, tab, w0, w1, w2, w3, gains, grads, dres, xt, r1, own, other, buf, nat):
    width, tokens = xt.shape
    quarter = w0.shape[0]
    wide = grads.shape[0]
    total = jnp.zeros((1, tokens), F32)
    scale = r1[...]
    for q, w in enumerate((w0, w1, w2, w3)):
        here = slice(q * quarter, (q + 1) * quarter)
        part = dot(w[:, :wide], grads[...])
        part = part * gains[here, 0:1].astype(F32)
        buf[here, :] = part
        total = total + jnp.sum(part * xt[here, :].astype(F32), axis=0, keepdims=True)
    pull = total / width * scale * scale * scale

    def second(p, _):
        here = pl.ds(pl.multiple_of(p * rows, rows), rows)
        part = dres[here, :] + scale * buf[here, :] - xt[here, :].astype(F32) * pull
        nat[pl.ds(pl.multiple_of(tab[p] * rows, rows), rows), :] = part.astype(nat.dtype)
        return 0

    lax.fori_loop(0, count, second, 0, unroll=4)
    turn_out(nat, own, other)


def input_of(tab, grads, bufs, gains, dres, xt, r1, rows, count, kind):
    width, tokens = xt.shape
    wide = grads.shape[0]
    at, own, other = token_maps(tokens, count)
    once = pl.BlockSpec(bufs[0].shape, lambda i, tab: (0, 0), pipeline_mode=pl.Buffered(1))
    block = pl.BlockSpec((width, TB), lambda i, tab: (0, at(i, tab)))
    return pl.pallas_call(
        functools.partial(input_kernel, rows, count),
        grid_spec=pltpu.PrefetchScalarGridSpec(
            num_scalar_prefetch=1,
            grid=(tokens // TB,),
            in_specs=[once] * 4
            + [pl.BlockSpec((width, 128), lambda i, tab: (0, 0))]
            + [pl.BlockSpec((wide, TB), lambda i, tab: (0, at(i, tab)))]
            + [block, block, pl.BlockSpec((1, TB), lambda i, tab: (0, at(i, tab)))],
            out_specs=[pl.BlockSpec((TB, width), own), pl.BlockSpec((TB, width), other)],
            scratch_shapes=[pltpu.VMEM((width, TB), F32), pltpu.VMEM((width, TB), kind)],
        ),
        out_shape=(sds((tokens // 2, width), BF16),) * 2,
        compiler_params=params(20),
        cost_estimate=cost(2 * width * tokens * wide, 12 * width * tokens + 2 * wide * tokens),
        name="input_of",
    )(tab, *keep_far(*bufs), gains, grads, *keep_far(dres, xt), r1)


def split_columns(total):
    tiles = -(-total // TILE)
    first = -(-tiles // 3)
    second = -(-(tiles - first) // 2)
    return [n * TILE for n in (tiles - first - second, second, first)]


def per_device(
    inputs, w_query, w_key, w_value, w_out, w_gate, w_up, w_down, gain_one, gain_two, cotangent
):
    dp = lax.axis_size("dp")
    bits = dp.bit_length() - 1
    count = 2 * dp
    micro, _, half, width = inputs.shape
    rows = width // count
    kind = BF16 if rows % 16 == 0 else F32
    hidden = w_gate.shape[1]
    groups = split_columns(hidden)
    padded = sum(groups)
    tab, core = block_tables(dp, bits)
    plan = Plan(dp, bits)
    plan.quarter = width // 4
    live = lambda: plan.live
    last = bits - 1

    x = inputs.reshape(micro, half, width)
    y = cotangent.reshape(micro, half, width)
    wide = w_query.shape[1] + w_key.shape[1] + w_value.shape[1]
    pair = jnp.pad(jnp.stack([gain_one, gain_two], axis=1), ((0, 0), (0, 126)))
    own_qkv = jnp.concatenate([w_query, w_key, w_value], axis=1)
    fill = ((0, 0), (0, padded - hidden))
    plan.gather("q", jnp.concatenate([own_qkv, pair], axis=1))
    plan.live.update(x=x, y=y, tab=tab)

    names = ["a", "b", "c"]
    downs = w_down.T

    def shard(k):
        at, size = sum(groups[:k]), groups[k]
        parts = [v[:, at : at + size] for v in (w_gate, w_up, downs)]
        short = size - parts[0].shape[1]
        if short:
            parts = [jnp.pad(p, ((0, 0), (0, short))) for p in parts]
        return jnp.stack(parts)

    def early(name, first=last):
        for stage in range(first, 1, -1):
            plan.double(name, stage)

    n = plan.live

    plan.double("q", last)
    n["x_came"], n["y_came"] = plan.send(x, -1), plan.send(y, -1)
    plan.gather("o", w_out)
    n.update(w_gate=w_gate, w_up=w_up, downs=downs)
    plan.fence()
    early("q", last - 1)
    plan.fence()
    plan.double("q", 1)
    plan.double("o", last)
    w_gate, w_up, downs = n["w_gate"], n["w_up"], n["downs"]
    plan.gather("a", shard(0))
    plan.fence()
    plan.double("q", 0)
    early("o", last - 1)
    plan.double("a", last)
    n["xt"], n["r1"], n["yt"], n["yn"] = pre(
        n.pop("tab"), n.pop("x"), n.pop("x_came"), n.pop("y"), n.pop("y_came"), rows, count, kind
    )
    w_gate, w_up, downs = n.pop("w_gate"), n.pop("w_up"), n.pop("downs")
    plan.gather("b", shard(1))
    plan.gather("c", shard(2))
    plan.fence()
    plan.double("q", -1)
    plan.double("o", 1)
    early("a", last - 1)
    plan.fence()

    qkv_bufs = plan.gathered("q")
    n["gains"] = gains = jnp.concatenate([b[:, wide:] for b in qkv_bufs], axis=0)
    plan.double("o", 0)
    plan.double("a", 1)
    plan.double("b", last)
    n["normed"], n["qkv"] = project(n["xt"].astype(BF16), n["r1"], gains, qkv_bufs, wide)
    plan.fence()
    plan.double("o", -1)
    plan.double("a", 0)
    early("b", last - 1)
    n["att"], n["den"] = attend(tab, n["qkv"], rows, count, kind)
    plan.fence()
    plan.double("a", -1)
    plan.double("b", 1)
    plan.double("c", last)
    n["res"], n["r2"], n["x2t"], n["x2"] = middle(
        tab, n["att"].astype(BF16), plan.gathered("o"), n["xt"].astype(BF16), n["gains"], rows, count
    )
    plan.fence()

    def feed_group(name):
        sums = (n["pull"], n["push"]) if "pull" in n else ()
        send, keep, n["pull"], n["push"] = feed(
            n["x2"], n["x2t"], n["yn"], n["yt"].astype(BF16), plan.gathered(name), sums,
            4 if name == names[-1] else 3,
        )
        for end in ("", "+", "-", "-+"):
            n.pop(name + end)
        plan.reduce("g" + name, send, keep)

    plan.double("b", 0)
    early("c", last - 1)
    feed_group("a")
    plan.fence()
    plan.double("b", -1)
    plan.double("c", 1)
    plan.fence()
    plan.double("c", 0)
    plan.halve("ga", -1)
    feed_group("b")
    plan.fence()
    plan.double("c", -1)
    plan.fence()
    plan.halve("ga", 0)
    plan.halve("gb", -1)
    feed_group("c")
    plan.fence()
    plan.halve("gb", 0)
    n["dres"], n["dm"] = back(
        tab, n.pop("pull"), n["res"], n["r2"], n["yt"].astype(BF16), n["gains"], rows, count, kind
    )
    send, keep, n["datt"] = mixed(
        n.pop("dm").astype(BF16),
        n["att"].astype(BF16),
        plan.gathered("o"),
        n.pop("gc.send"),
        n.pop("gc"),
    )
    plan.reduce("gc", send, keep)
    plan.fence()

    def heads_back(part):
        for k, v in zip(
            ("dq", "dk", "dv"),
            attend_back(
                tab, n["qkv"], n["datt"], n["att"], n["den"], BACK_PARTS[part], rows, count
            ),
        ):
            n[k + str(part)] = v

    plan.halve("ga", 1)
    plan.halve("gb", 1)
    plan.halve("gc", -1)
    heads_back(0)
    plan.fence()
    plan.halve("gc", 0)
    plan.halve("gb", 2)
    plan.prep_far("ga")
    plan.go_far("ga")
    heads_back(1)
    n["grads"] = jnp.concatenate(
        [n.pop(k + str(p)) for k in ("dq", "dk", "dv") for p in range(len(BACK_PARTS))], axis=0
    )
    plan.fence()
    plan.halve("gc", 1)
    for stage in range(3, bits):
        plan.halve("gb", stage)
    send, keep = weights_of(n["normed"], n["grads"])
    plan.reduce("gq", send, keep)
    plan.fence()
    plan.halve("gq", -1)
    plan.prep_far("gc")
    plan.fence()
    plan.prep("gq", 0)
    plan.fence()

    def give_back(name):
        own, came = n.pop(name + "_own"), n.pop(name + "_came")
        first = core == 0
        both = jnp.stack([jnp.where(first, own, came), jnp.where(first, came, own)])
        return both.reshape(micro, 1, half, width)

    plan.go("gq", 0)
    plan.go_far("gc")
    n["dx_own"], n["dx_other"] = input_of(
        tab, n["grads"], plan.gathered("q"), n["gains"], n["dres"], n["xt"].astype(BF16), n["r1"], rows, count, kind
    )
    n["out_own"], n["out_other"] = output_of(tab, n.pop("push"), n["res"], rows, count, kind)
    plan.fence()
    plan.prep("gq", 1)
    plan.fence()
    plan.go("gq", 1)
    for name in ("dx", "out"):
        n[name + "_came"] = plan.send(n.pop(name + "_other"), -1)
    plan.after("dx_came", ["dx_own"] + [key for k in ("ga", "gb") for key in plan.parts[k]])
    n["dx"] = give_back("dx")
    n["sum_a"] = plan.reduced("ga")
    n["sum_b"] = plan.reduced("gb")
    plan.fence()
    plan.prep_far("gq")
    plan.fence()
    plan.go_far("gq")
    first_landed = plan.parts["gq"][-1] if bits > 4 else "gq.far1"
    plan.after(
        first_landed,
        ["out_own", "out_came", "sum_a", "sum_b"] + list(plan.parts["gc"]),
    )
    n["out"] = give_back("out")
    last_sum = plan.reduced("gc")
    ff = jnp.concatenate([n["sum_a"], n["sum_b"], last_sum[:3]], axis=-1)[:, :, :hidden]
    n["gain_two"] = (
        jnp.sum(w_gate.astype(F32) * ff[0] + w_up.astype(F32) * ff[1], axis=1)
    ) / gain_two.astype(F32)
    n["ff0"], n["ff1"], n["ff2"] = ff[0], ff[1], ff[2].T
    n["grad_out"] = last_sum[3]
    plan.fence()
    grad_qkv = plan.reduced("gq")
    a, b = w_query.shape[1], w_query.shape[1] + w_key.shape[1]
    gain_one_grad = jnp.sum(own_qkv.astype(F32) * grad_qkv, axis=1) / gain_one.astype(F32)
    return (
        n["out"],
        n["dx"],
        grad_qkv[:, :a],
        grad_qkv[:, a:b],
        grad_qkv[:, b:],
        n["grad_out"],
        n["ff0"],
        n["ff1"],
        n["ff2"],
        gain_one_grad,
        n["gain_two"],
    )


def solution(mesh):
    shard = P(AXES, None)
    batch = P(None, "dp", "seq", None)
    return jax.shard_map(
        per_device,
        mesh=mesh,
        in_specs=(batch,) + (shard,) * 6 + (P(None, AXES), P(AXES), P(AXES), batch),
        out_specs=(batch,) * 2 + (shard,) * 6 + (P(None, AXES), P(AXES), P(AXES)),
        check_vma=False,
    )
```

```python
import functools

import jax
import jax.numpy as jnp
import numpy as np
from jax import lax
from jax.experimental import pallas as pl
from jax.experimental.pallas import tpu as pltpu
from jax.sharding import PartitionSpec as P

H = 16
F = 16
DV = 64
AXES = ("dp", "seq")
EPS = 1e-06
TB = 256
HEADS = 2
BACK_HEADS = 1
BACK_PARTS = ((0, 8), (8, 8))
TILE = 256
F32 = jnp.float32
BF16 = jnp.bfloat16

NN = (((1,), (0,)), ((), ()))
NT = (((1,), (1,)), ((), ()))
TN = (((0,), (0,)), ((), ()))


def dot(a, b, dims=NN):
    return lax.dot_general(a, b, dims, preferred_element_type=F32)


VMEM = pl.BlockSpec(memory_space=pltpu.VMEM)
SMEM = pl.BlockSpec(memory_space=pltpu.SMEM)


def params(mib):
    return pltpu.CompilerParams(vmem_limit_bytes=mib << 20)


def cost(flops, nbytes, trans=0):
    return pl.CostEstimate(flops=int(flops), bytes_accessed=int(nbytes), transcendentals=int(trans))


def sds(shape, dtype):
    return jax.ShapeDtypeStruct(shape, dtype)


def far(shape, dtype):
    return pltpu.HBM(shape, dtype)


def keep_far(*values):
    return [pltpu.with_memory_space_constraint(v, pltpu.HBM) for v in values]


def stage_orders(bits):
    straight = list(range(bits))
    swapped = [1, 0] + list(range(2, bits)) if bits > 1 else straight
    return (straight, swapped)


def stage_pairs(dp, bits, stage):
    orders = stage_orders(bits)
    return [
        (d * 2 + c, (d ^ (1 << orders[c][stage])) * 2 + c) for d in range(dp) for c in range(2)
    ]


def core_pairs(dp):
    return [(i, i ^ 1) for i in range(2 * dp)]


def block_tables(dp, bits):
    orders = stage_orders(bits)
    count = 2 * dp
    position = np.arange(count)
    masks = []
    for c in range(2):
        mask = np.zeros(count, np.int32)
        for stage in range(bits):
            mask |= ((position >> (bits - 1 - stage)) & 1) << orders[c][stage]
        masks.append(mask)
    d = lax.axis_index("dp").astype(jnp.int32)
    c = lax.axis_index("seq").astype(jnp.int32)
    owner_core = jnp.asarray(position >> bits, jnp.int32) ^ c
    mask = jnp.where(owner_core == 0, jnp.asarray(masks[0]), jnp.asarray(masks[1]))
    block_at = (d ^ mask) * 2 + owner_core
    block_core = jnp.asarray(position & 1, jnp.int32)
    apart = jnp.asarray(position >> 1, jnp.int32) ^ d
    places = []
    for k in range(2):
        place = jnp.zeros(count, jnp.int32)
        for stage in range(bits):
            place = place | (((apart >> orders[k][stage]) & 1) << (bits - 1 - stage))
        places.append(place)
    place_of = jnp.where(block_core == 0, places[0], places[1]) | ((block_core ^ c) << bits)
    return jnp.concatenate([block_at, place_of, c[None], jnp.zeros(7, jnp.int32)]), c


class Plan:
    def __init__(self, dp, bits):
        self.dp, self.bits = dp, bits
        self.live, self.parts, self.air = {}, {}, {}

    def fence(self):
        self.live.update(lax.optimization_barrier(dict(self.live)))
        self.live.update(self.air)
        self.air = {}

    def after(self, key, names):
        tied = lax.optimization_barrier({k: self.live[k] for k in [key] + list(names)})
        self.live.update(tied)

    def pairs(self, stage):
        return core_pairs(self.dp) if stage < 0 else stage_pairs(self.dp, self.bits, stage)

    def send(self, value, stage):
        return lax.ppermute(value, AXES, self.pairs(stage))

    def gather(self, name, shard):
        self.live[name] = shard

    def double(self, name, stage, long=False):
        live = self.live
        if 0 <= stage < self.bits - 1:
            self.join(name)
        if stage >= 0:
            (self.air if long else live)[name + "+"] = self.send(live[name], stage)
            if stage == 0:
                live[name + "-"] = self.send(live[name], -1)
        else:
            live[name + "-+"] = self.send(live[name + "+"], -1)

    def join(self, name):
        came = self.live.pop(name + "+")
        self.live[name] = jnp.concatenate([self.live[name], came], axis=-2)

    def gathered(self, name):
        return tuple(self.live[name + end] for end in ("", "+", "-", "-+"))

    def reduce(self, name, send, keep):
        self.live[name + ".send"], self.live[name] = send, keep
        self.parts[name] = [name]

    def prep(self, name, stage):
        if stage < 0:
            return
        half = self.live[name].shape[-2] >> (stage + 1)
        send = self.total(self.parts[name], half, half)
        self.live[name + ".send"] = send.astype(BF16)

    def go(self, name, stage):
        key = f"{name}.{stage}"
        self.live[key] = self.send(self.live.pop(name + ".send"), stage)
        self.parts[name].append(key)

    def halve(self, name, stage):
        self.prep(name, stage)
        self.go(name, stage)

    def total(self, parts, start, size):
        acc = None
        for key in parts:
            part = self.live[key]
            part = lax.slice_in_dim(part, start, start + size, axis=part.ndim - 2)
            acc = part.astype(F32) if acc is None else acc + part.astype(F32)
        return acc

    def prep_far(self, name):
        if self.bits > 4:
            return

        rows = self.live[name].shape[-2] >> self.bits
        for apart in range(1, self.dp >> 2):
            at = 0
            for stage in range(2, self.bits):
                at |= ((apart >> (stage - 2)) & 1) << (self.bits - 1 - stage)
            send = self.total(self.parts[name], at * rows, rows)
            self.live[f"{name}.far{apart}"] = send.astype(BF16)

    def go_far(self, name):
        if self.bits > 4:
            for stage in range(2, self.bits):
                self.halve(name, stage)
            return
        for apart in range(1, self.dp >> 2):
            pairs = [(d * 2 + c, (d ^ (apart << 2)) * 2 + c) for d in range(self.dp) for c in range(2)]
            key = f"{name}.far{apart}"
            self.live[key] = lax.ppermute(self.live[key], AXES, pairs)
            self.parts[name].append(key)

    def reduced(self, name):
        return self.total(self.parts[name], 0, self.live[name].shape[-2] >> self.bits)


def pre_kernel(rows, count, blocks, tab, x, xr, y, yr, xt, r1, yt, yn, buf):
    own = pl.program_id(0) // blocks == tab[2 * count]
    width = xt.shape[0]
    total = jnp.zeros(r1.shape, F32)
    for src, rec, dst in ((x, xr, xt), (y, yr, yt)):
        for i in range(width // 256):
            here = slice(i * 256, (i + 1) * 256)
            part = jnp.where(own, src[0, :, here], rec[0, :, here]).T
            buf[here, :] = part.astype(buf.dtype)
            if src is x:
                wide = part.astype(F32)
                total = total + jnp.sum(wide * wide, axis=0, keepdims=True)

        def move(p, _):
            at = pl.multiple_of(tab[p] * rows, rows)
            dst[pl.ds(pl.multiple_of(p * rows, rows), rows), :] = buf[pl.ds(at, rows), :]
            return 0

        lax.fori_loop(0, count, move, 0, unroll=4)
    for i in range(width // 256):
        here = slice(i * 256, (i + 1) * 256)
        yn[:, here] = yt[here, :].T.astype(BF16)
    r1[...] = lax.rsqrt(total / width + EPS)


def pre(tab, x, xr, y, yr, rows, count, kind):
    _, half, width = xr.shape
    tokens = 2 * half
    blocks = half // TB
    own = pl.BlockSpec((1, TB, width), lambda i, tab: (tab[2 * count], i % blocks, 0))
    turned = pl.BlockSpec((width, TB), lambda i, tab: (0, i))
    return pl.pallas_call(
        functools.partial(pre_kernel, rows, count, blocks),
        grid_spec=pltpu.PrefetchScalarGridSpec(
            num_scalar_prefetch=1,
            grid=(tokens // TB,),
            in_specs=[own] * 4,
            out_specs=[
                turned,
                pl.BlockSpec((1, TB), lambda i, tab: (0, i)),
                turned,
                pl.BlockSpec((TB, width), lambda i, tab: (i, 0)),
            ],
            scratch_shapes=[pltpu.VMEM((width, TB), kind)],
        ),
        out_shape=(
            sds((width, tokens), kind),
            sds((1, tokens), F32),
            sds((width, tokens), kind),
            sds((tokens, width), BF16),
        ),
        compiler_params=params(14),
        cost_estimate=cost(8 * width * tokens, 14 * width * tokens),
        name="pre",
    )(tab, x, xr, y, yr)


def project_kernel(xt, r1, gains, w0, w1, w2, w3, normed, out):
    quarter = w0.shape[0]

    @pl.when(pl.program_id(0) == 0)
    def _():
        for q in range(4):
            here = slice(q * quarter, (q + 1) * quarter)
            part = xt[here, :].astype(F32) * r1[...] * gains[here, 0:1].astype(F32)
            normed[here, :] = part.astype(BF16)

    acc = dot(w0[...], normed[0:quarter, :], TN)
    for q, w in ((1, w1), (2, w2), (3, w3)):
        acc = acc + dot(w[...], normed[q * quarter : (q + 1) * quarter, :], TN)
    out[...] = acc.astype(BF16)


def project(xt, r1, gains, bufs, wide):
    width, tokens = xt.shape
    quarter = bufs[0].shape[0]
    return pl.pallas_call(
        project_kernel,
        grid=(wide // 256,),
        out_shape=(sds((width, tokens), BF16), sds((wide, tokens), BF16)),
        in_specs=[
            pl.BlockSpec((width, tokens), lambda i: (0, 0), pipeline_mode=pl.Buffered(1)),
            pl.BlockSpec((1, tokens), lambda i: (0, 0)),
            pl.BlockSpec((width, 128), lambda i: (0, 0)),
        ]
        + [pl.BlockSpec((quarter, 256), lambda i: (0, i))] * 4,
        out_specs=[
            pl.BlockSpec((width, tokens), lambda i: (0, 0)),
            pl.BlockSpec((256, tokens), lambda i: (i, 0)),
        ],
        compiler_params=params(16),
        cost_estimate=cost(2 * width * tokens * wide, 2 * (2 * width * tokens + 2 * wide * tokens)),
        name="project",
    )(xt, r1, gains, *keep_far(*bufs))


def unit_rows(tokens, ones):
    row = lax.broadcasted_iota(jnp.int32, (16, tokens), 0)
    return jnp.where(row < ones, 1.0, 0.0).astype(BF16)


def causal(shape):
    j = lax.broadcasted_iota(jnp.int32, shape, 0)
    t = lax.broadcasted_iota(jnp.int32, shape, 1)
    return j <= t


def attend_kernel(rows, count, tab, q, k, v, att, den):
    tokens = q.shape[1]
    blocks = tokens // TB
    one = unit_rows(tokens, 1)
    below = causal((TB, TB))
    heads = range(q.shape[0] // F)
    us, vas = [], []
    for n in heads:
        qa = q[n * F : (n + 1) * F, :] * jnp.asarray(F ** -0.5, BF16)
        qa = jnp.concatenate([qa, one], axis=0)
        ka = jnp.concatenate([k[n * F : (n + 1) * F, :], one], axis=0)
        vas.append(jnp.concatenate([v[n * DV : (n + 1) * DV, :], one], axis=0))
        us.append(
            [dot(ka[:, : (b + 1) * TB], qa[:, b * TB : (b + 1) * TB], TN) for b in range(blocks)]
        )
    ps = []
    for n in heads:
        ps.append([])
        for b in range(blocks):
            lo = b * TB
            p = us[n][b] * us[n][b] + 1.0
            last = jnp.where(below, p[lo:], 0.0).astype(BF16)
            ps[n].append(jnp.concatenate([p[:lo].astype(BF16), last], axis=0) if b else last)
    for n in heads:
        h = pl.program_id(0) * len(heads) + n
        for b in range(blocks):
            lo, hi = b * TB, (b + 1) * TB
            o = dot(vas[n][:, :hi], ps[n][b])
            d = o[DV : DV + 1]
            done = o[:DV] / d
            den[n, :, lo:hi] = d
            for i in range(DV // rows):
                at = tab[count + h * (DV // rows) + i]
                att[pl.ds(pl.multiple_of(at * rows, rows), rows), lo:hi] = done[
                    i * rows : (i + 1) * rows
                ].astype(att.dtype)


def head_specs(tokens, heads, off=0):
    return [
        pl.BlockSpec((F * heads, tokens), lambda h, *_: (off + h, 0)),
        pl.BlockSpec((F * heads, tokens), lambda h, *_: (H // heads + off + h, 0)),
        pl.BlockSpec((DV * heads, tokens), lambda h, *_: (2 * H * F // DV // heads + off + h, 0)),
    ]


def attend(tab, qkv, rows, count, kind):
    tokens = qkv.shape[1]
    heads = HEADS
    return pl.pallas_call(
        functools.partial(attend_kernel, rows, count),
        grid=(H // heads,),
        out_shape=(sds((H * DV, tokens), kind), sds((H, 1, tokens), F32)),
        in_specs=[SMEM] + head_specs(tokens, heads),
        out_specs=[
            pl.BlockSpec((H * DV, tokens), lambda h: (0, 0)),
            pl.BlockSpec((heads, 1, tokens), lambda h: (h, 0, 0)),
        ],
        compiler_params=params(28),
        cost_estimate=cost(H * tokens * tokens * 256 * 2, 4 * H * DV * tokens * 2),
        name="attend",
    )(tab, qkv, qkv, qkv)


def middle_kernel(rows, count, tab, w0, w1, w2, w3, att, xt, gains, res, r2, x2t, x2, wt, buf):
    width, tokens = xt.shape
    quarter = w0.shape[0]

    @pl.when(pl.program_id(0) == 0)
    def _():
        for q, w in enumerate((w0, w1, w2, w3)):
            for i in range(width // 256):
                wt[i * 256 : (i + 1) * 256, q * quarter : (q + 1) * quarter] = w[
                    :, i * 256 : (i + 1) * 256
                ].T

    buf[...] = dot(wt[...], att[...])

    def join(p, total):
        here = pl.ds(pl.multiple_of(p * rows, rows), rows)
        part = buf[pl.ds(pl.multiple_of(tab[p] * rows, rows), rows), :] + xt[here, :].astype(F32)
        res[here, :] = part
        return total + jnp.sum(part * part, axis=0, keepdims=True)

    total = lax.fori_loop(0, count, join, jnp.zeros((1, tokens), F32), unroll=4)
    scale = lax.rsqrt(total / width + EPS)
    r2[...] = scale
    for i in range(width // 256):
        here = slice(i * 256, (i + 1) * 256)
        low = (res[here, :] * scale * gains[here, 1:2].astype(F32)).astype(BF16)
        x2t[here, :] = low
        x2[:, here] = low.T


def middle(tab, att, bufs, xt, gains, rows, count):
    width, tokens = xt.shape
    inner = att.shape[0]
    quarter = bufs[0].shape[0]
    once = pl.BlockSpec((quarter, width), lambda i: (0, 0), pipeline_mode=pl.Buffered(1))
    return pl.pallas_call(
        functools.partial(middle_kernel, rows, count),
        grid=(tokens // TB,),
        out_shape=(
            far((width, tokens), F32),
            sds((1, tokens), F32),
            sds((width, tokens), BF16),
            sds((tokens, width), BF16),
        ),
        in_specs=[SMEM]
        + [once] * 4
        + [
            pl.BlockSpec((inner, TB), lambda i: (0, i)),
            pl.BlockSpec((width, TB), lambda i: (0, i)),
            pl.BlockSpec((width, 128), lambda i: (0, 0)),
        ],
        out_specs=[
            pl.BlockSpec((width, TB), lambda i: (0, i)),
            pl.BlockSpec((1, TB), lambda i: (0, i)),
            pl.BlockSpec((width, TB), lambda i: (0, i)),
            pl.BlockSpec((TB, width), lambda i: (i, 0)),
        ],
        scratch_shapes=[pltpu.VMEM((width, inner), BF16), pltpu.VMEM((width, TB), F32)],
        compiler_params=params(22),
        cost_estimate=cost(2 * width * tokens * inner, 16 * width * tokens),
        name="middle",
    )(tab, *keep_far(*bufs), att, *keep_far(xt), gains)


def feed_kernel(first, x2, x2t, dy, dyt, w0, w1, w2, w3, *refs):
    send, keep, pull, push = refs[-4:]
    quarter = w0.shape[1]
    bufs = (w0, w1, w2, w3)
    half = keep.shape[1]

    if first:

        @pl.when(pl.program_id(0) == 0)
        def _():
            pull[...] = jnp.zeros_like(pull)
            push[...] = jnp.zeros_like(push)

    def over(a, which):
        acc = dot(a[:, 0:quarter], w0[which])
        for q in range(1, 4):
            acc = acc + dot(a[:, q * quarter : (q + 1) * quarter], bufs[q][which])
        return acc

    def grad(i, a, b):
        whole = dot(a[...], b).astype(BF16)
        keep[i] = whole[:half]
        send[i] = whole[half:]

    gate = over(x2, 0)
    up = over(x2, 1)
    sig = 0.5 * jnp.tanh(0.5 * gate) + 0.5
    act = gate * sig
    h = (act * up).astype(BF16)
    back = over(dy, 2)
    dg = (back * up * (sig + act * (1.0 - sig))).astype(BF16)
    du = (back * act).astype(BF16)
    ht, dgt, dut = h.T, dg.T, du.T
    grad(2, dyt, h)
    for q, w in enumerate(bufs):
        here = slice(q * quarter, (q + 1) * quarter)
        push[here, :] = push[here, :] + dot(w[2], ht)
    grad(0, x2t, dg)
    grad(1, x2t, du)
    for q, w in enumerate(bufs):
        here = slice(q * quarter, (q + 1) * quarter)
        pull[here, :] = pull[here, :] + (dot(w[0], dgt) + dot(w[1], dut))


def feed(x2, x2t, dy, dyt, bufs, sums, slots=3):
    tokens, width = x2.shape
    cols = bufs[0].shape[-1]
    quarter = bufs[0].shape[1]
    return pl.pallas_call(
        functools.partial(feed_kernel, not sums),
        grid=(cols // TILE,),
        out_shape=(far((slots, width // 2, cols), BF16),) * 2 + (sds((width, tokens), F32),) * 2,
        in_specs=[VMEM] * 4
        + [pl.BlockSpec((3, quarter, TILE), lambda i: (0, 0, i))] * 4
        + [VMEM] * len(sums),
        out_specs=[pl.BlockSpec((3, width // 2, TILE), lambda i: (0, 0, i))] * 2 + [VMEM] * 2,
        input_output_aliases={8: 2, 9: 3} if sums else {},
        compiler_params=params(26),
        cost_estimate=cost(18 * tokens * width * cols, 2 * (4 * tokens * width + 9 * width * cols)),
        name="feed",
    )(x2, x2t, dy, dyt, *keep_far(*bufs), *sums)


def back_kernel(rows, count, tab, pull, res, r2, yt, gains, dres, dm, acc):
    width, tokens = acc.shape
    part = pull[...] * gains[:, 1:2].astype(F32)
    acc[...] = part
    total = jnp.sum(part * res[...], axis=0, keepdims=True)
    scale = r2[...]
    side = total / width * scale * scale * scale

    def second(p, _):
        here = pl.ds(pl.multiple_of(p * rows, rows), rows)
        part = yt[here, :].astype(F32) + scale * acc[here, :] - res[here, :] * side
        dres[here, :] = part
        dm[pl.ds(pl.multiple_of(tab[p] * rows, rows), rows), :] = part.astype(dm.dtype)
        return 0

    lax.fori_loop(0, count, second, 0, unroll=4)


def back(tab, pull, res, r2, yt, gains, rows, count, kind):
    width, tokens = res.shape
    block = pl.BlockSpec((width, TB), lambda i: (0, i))
    return pl.pallas_call(
        functools.partial(back_kernel, rows, count),
        grid=(tokens // TB,),
        out_shape=(far((width, tokens), F32), sds((width, tokens), kind)),
        in_specs=[
            SMEM,
            block,
            block,
            pl.BlockSpec((1, TB), lambda i: (0, i)),
            block,
            pl.BlockSpec((width, 128), lambda i: (0, 0)),
        ],
        out_specs=[block] * 2,
        scratch_shapes=[pltpu.VMEM((width, TB), F32)],
        compiler_params=params(20),
        cost_estimate=cost(10 * tokens * width, 16 * width * tokens),
        name="back",
    )(tab, pull, *keep_far(res), r2, *keep_far(yt), gains)


def turn_out(nat, own, other):
    width = nat.shape[0]
    for mine, ref in ((False, other), (True, own)):

        @pl.when((pl.program_id(0) >= pl.num_programs(0) // 2) == mine)
        def _(ref=ref):
            for i in range(width // 256):
                here = slice(i * 256, (i + 1) * 256)
                ref[:, here] = nat[here, :].T.astype(BF16)


def token_maps(tokens, count):
    blocks = tokens // TB // 2

    def at(i, tab):
        core = tab[2 * count]
        return jnp.where(i < blocks, (1 - core) * blocks + i, core * blocks + i - blocks)

    own = lambda i, tab: (jnp.maximum(i - blocks, 0), 0)
    other = lambda i, tab: (jnp.minimum(i, blocks - 1), 0)
    return at, own, other


def output_kernel(rows, count, tab, push, res, own, other, acc, nat):
    width, tokens = acc.shape
    acc[...] = push[...] + res[...]

    def move(p, _):
        here = pl.ds(pl.multiple_of(p * rows, rows), rows)
        to = pl.ds(pl.multiple_of(tab[p] * rows, rows), rows)
        nat[to, :] = acc[here, :].astype(nat.dtype)
        return 0

    lax.fori_loop(0, count, move, 0, unroll=4)
    turn_out(nat, own, other)


def output_of(tab, push, res, rows, count, kind):
    width, tokens = res.shape
    at, own, other = token_maps(tokens, count)
    block = pl.BlockSpec((width, TB), lambda i, tab: (0, at(i, tab)))
    return pl.pallas_call(
        functools.partial(output_kernel, rows, count),
        grid_spec=pltpu.PrefetchScalarGridSpec(
            num_scalar_prefetch=1,
            grid=(tokens // TB,),
            in_specs=[block, block],
            out_specs=[pl.BlockSpec((TB, width), own), pl.BlockSpec((TB, width), other)],
            scratch_shapes=[pltpu.VMEM((width, TB), F32), pltpu.VMEM((width, TB), kind)],
        ),
        out_shape=(sds((tokens // 2, width), BF16),) * 2,
        compiler_params=params(18),
        cost_estimate=cost(tokens * width, 10 * width * tokens),
        name="output_of",
    )(tab, *keep_far(push, res))


def mixed_kernel(dm, dm_rows, att, w0, w1, w2, w3, send_in, keep_in, send, keep, datt):
    quarter = w0.shape[0]
    half = keep.shape[1]
    right = dm[...]
    for q, w in enumerate((w0, w1, w2, w3)):
        datt[q * quarter : (q + 1) * quarter, :] = dot(w[...], right)
    whole = dot(att[...], dm_rows[...], NT).astype(BF16)
    keep[0] = whole[:half]
    send[0] = whole[half:]


def mixed(dm, att, bufs, send, keep):
    width, tokens = dm.shape
    rows = att.shape[0]
    quarter = bufs[0].shape[0]
    slot = keep.shape[0] - 1
    cols = width * TB // tokens
    return pl.pallas_call(
        mixed_kernel,
        grid=(tokens // TB,),
        out_shape=(far(send.shape, BF16), far(keep.shape, BF16), far((rows, tokens), F32)),
        in_specs=[
            pl.BlockSpec((width, TB), lambda i: (0, i)),
            pl.BlockSpec((cols, tokens), lambda i: (i, 0)),
            pl.BlockSpec((rows, tokens), lambda i: (0, 0), pipeline_mode=pl.Buffered(1)),
        ]
        + [pl.BlockSpec((quarter, width), lambda i: (0, 0), pipeline_mode=pl.Buffered(1))] * 4
        + [pl.BlockSpec(memory_space=pl.ANY)] * 2,
        out_specs=[pl.BlockSpec((1, rows // 2, cols), lambda i: (slot, 0, i))] * 2
        + [pl.BlockSpec((rows, TB), lambda i: (0, i))],
        input_output_aliases={7: 0, 8: 1},
        compiler_params=params(18),
        cost_estimate=cost(4 * width * tokens * rows, 12 * width * tokens),
        name="mixed",
    )(dm, dm, att, *keep_far(*bufs, send, keep))


def attend_back_kernel(rows, tab, q, k, v, den, *refs):
    many = q.shape[0] // F * (DV // rows)
    datts, atts = refs[:many], refs[many : 2 * many]
    dq, dk, dv, pt, st = refs[2 * many :]
    tokens = q.shape[1]
    blocks = tokens // TB
    scale = jnp.asarray(F ** -0.5, BF16)
    row = lax.broadcasted_iota(jnp.int32, (16, tokens), 0)
    one = unit_rows(tokens, 1)
    two = unit_rows(tokens, 2)
    zero = jnp.zeros((DV, tokens), BF16)
    below = causal((TB, TB))
    heads = range(q.shape[0] // F)
    us, gs, kss, rights_p, rights_s = [], [], [], [], []
    for n in heads:
        here = slice(n * (DV // rows), (n + 1) * (DV // rows))
        da = jnp.concatenate([r[...] for r in datts[here]], axis=0)
        done = jnp.concatenate([r[...].astype(F32) for r in atts[here]], axis=0)
        inv = 2.0 / den[n]
        dn = (da * inv).astype(BF16)
        dd = -jnp.sum(da * done, axis=0, keepdims=True) * inv
        dd_high = dd.astype(BF16).astype(F32)
        tail = jnp.where(row == 0, dd_high, jnp.where(row == 1, dd - dd_high, 0.0)).astype(BF16)
        qh, kh = q[n * F : (n + 1) * F, :], k[n * F : (n + 1) * F, :]
        qs = qh * scale
        kss.append(kh * scale)
        qa = jnp.concatenate([qs, one], axis=0)
        ka = jnp.concatenate([kh, one], axis=0)
        va = jnp.concatenate([v[n * DV : (n + 1) * DV, :], two], axis=0)
        na = jnp.concatenate([dn, tail], axis=0)
        rights_p.append(jnp.concatenate([dn * jnp.asarray(0.5, BF16), zero], axis=0).T)
        rights_s.append(jnp.concatenate([zero, qs, jnp.zeros((DV - F, tokens), BF16)], axis=0).T)
        us.append([dot(ka[:, : (b + 1) * TB], qa[:, b * TB : (b + 1) * TB], TN) for b in range(blocks)])
        gs.append([dot(va[:, : (b + 1) * TB], na[:, b * TB : (b + 1) * TB], TN) for b in range(blocks)])
    for n in heads:
        for b in range(blocks):
            lo, hi = b * TB, (b + 1) * TB
            u = us[n][b]
            p = u * u + 1.0
            s = gs[n][b] * u
            if b:
                pt[n, :lo, lo:hi] = p[:lo].astype(BF16)
                st[n, :lo, lo:hi] = s[:lo].astype(BF16)
            pt[n, lo:hi, lo:hi] = jnp.where(below, p[lo:], 0.0).astype(BF16)
            st[n, lo:hi, lo:hi] = jnp.where(below, s[lo:], 0.0).astype(BF16)
    for n in heads:
        for b in range(blocks):
            lo, hi = b * TB, (b + 1) * TB
            dq[n * F : (n + 1) * F, lo:hi] = dot(kss[n][:, :hi], st[n, :hi, lo:hi]).astype(BF16)
        for b in range(blocks):
            lo, hi = b * TB, (b + 1) * TB
            both = dot(pt[n, lo:hi, lo:], rights_p[n][lo:]) + dot(st[n, lo:hi, lo:], rights_s[n][lo:])
            turned = both.T
            dv[n * DV : (n + 1) * DV, lo:hi] = turned[:DV].astype(BF16)
            dk[n * F : (n + 1) * F, lo:hi] = turned[DV : DV + F].astype(BF16)


def attend_back(tab, qkv, datt, att, den, part, rows, count):
    tokens = qkv.shape[1]
    heads = BACK_HEADS
    base, many = part
    off = base // heads
    each = DV // rows

    def piece(i):
        return pl.BlockSpec(
            (rows, tokens),
            lambda h, tab: (tab[count + (base + h * heads) * each + i], 0),
        )

    pieces = [piece(i) for i in range(heads * each)]
    return pl.pallas_call(
        functools.partial(attend_back_kernel, rows),
        grid_spec=pltpu.PrefetchScalarGridSpec(
            num_scalar_prefetch=1,
            grid=(many // heads,),
            in_specs=head_specs(tokens, heads, off)
            + [pl.BlockSpec((heads, 1, tokens), lambda h, tab: (off + h, 0, 0))]
            + pieces * 2,
            out_specs=[
                pl.BlockSpec((F * heads, tokens), lambda h, tab: (h, 0)),
                pl.BlockSpec((F * heads, tokens), lambda h, tab: (h, 0)),
                pl.BlockSpec((DV * heads, tokens), lambda h, tab: (h, 0)),
            ],
            scratch_shapes=[pltpu.VMEM((heads, tokens, tokens), BF16)] * 2,
        ),
        out_shape=(
            sds((many * F, tokens), BF16),
            sds((many * F, tokens), BF16),
            sds((many * DV, tokens), BF16),
        ),
        compiler_params=params(44),
        cost_estimate=cost(many * tokens * tokens * 256 * 6, 8 * many * DV * tokens * 2),
        name="attend_back",
    )(tab, *keep_far(qkv, qkv, qkv, den), *keep_far(datt) * len(pieces), *keep_far(att) * len(pieces))


def weights_kernel(normed, right, send, keep):
    half = keep.shape[0]
    whole = dot(normed[...], right[...], NT).astype(BF16)
    keep[...] = whole[:half]
    send[...] = whole[half:]


def weights_of(normed, grads):
    width, tokens = normed.shape
    wide = grads.shape[0]
    col = pl.BlockSpec((width // 2, TILE), lambda i: (0, i))
    return pl.pallas_call(
        weights_kernel,
        grid=(wide // TILE,),
        out_shape=(far((width // 2, wide), BF16),) * 2,
        in_specs=[
            pl.BlockSpec((width, tokens), lambda i: (0, 0), pipeline_mode=pl.Buffered(1)),
            pl.BlockSpec((TILE, tokens), lambda i: (i, 0)),
        ],
        out_specs=[col] * 2,
        compiler_params=params(12),
        cost_estimate=cost(2 * width * tokens * wide, 6 * width * tokens + 4 * width * wide),
        name="weights_of",
    )(normed, grads)


def input_kernel(rows, count, tab, w0, w1, w2, w3, gains, grads, dres, xt, r1, own, other, buf, nat):
    width, tokens = xt.shape
    quarter = w0.shape[0]
    wide = grads.shape[0]
    total = jnp.zeros((1, tokens), F32)
    scale = r1[...]
    for q, w in enumerate((w0, w1, w2, w3)):
        here = slice(q * quarter, (q + 1) * quarter)
        part = dot(w[:, :wide], grads[...])
        part = part * gains[here, 0:1].astype(F32)
        buf[here, :] = part
        total = total + jnp.sum(part * xt[here, :].astype(F32), axis=0, keepdims=True)
    pull = total / width * scale * scale * scale

    def second(p, _):
        here = pl.ds(pl.multiple_of(p * rows, rows), rows)
        part = dres[here, :] + scale * buf[here, :] - xt[here, :].astype(F32) * pull
        nat[pl.ds(pl.multiple_of(tab[p] * rows, rows), rows), :] = part.astype(nat.dtype)
        return 0

    lax.fori_loop(0, count, second, 0, unroll=4)
    turn_out(nat, own, other)


def input_of(tab, grads, bufs, gains, dres, xt, r1, rows, count, kind):
    width, tokens = xt.shape
    wide = grads.shape[0]
    at, own, other = token_maps(tokens, count)
    once = pl.BlockSpec(bufs[0].shape, lambda i, tab: (0, 0), pipeline_mode=pl.Buffered(1))
    block = pl.BlockSpec((width, TB), lambda i, tab: (0, at(i, tab)))
    return pl.pallas_call(
        functools.partial(input_kernel, rows, count),
        grid_spec=pltpu.PrefetchScalarGridSpec(
            num_scalar_prefetch=1,
            grid=(tokens // TB,),
            in_specs=[once] * 4
            + [pl.BlockSpec((width, 128), lambda i, tab: (0, 0))]
            + [pl.BlockSpec((wide, TB), lambda i, tab: (0, at(i, tab)))]
            + [block, block, pl.BlockSpec((1, TB), lambda i, tab: (0, at(i, tab)))],
            out_specs=[pl.BlockSpec((TB, width), own), pl.BlockSpec((TB, width), other)],
            scratch_shapes=[pltpu.VMEM((width, TB), F32), pltpu.VMEM((width, TB), kind)],
        ),
        out_shape=(sds((tokens // 2, width), BF16),) * 2,
        compiler_params=params(20),
        cost_estimate=cost(2 * width * tokens * wide, 12 * width * tokens + 2 * wide * tokens),
        name="input_of",
    )(tab, *keep_far(*bufs), gains, grads, *keep_far(dres, xt), r1)


def split_columns(total):
    tiles = -(-total // TILE)
    first = -(-tiles // 3)
    second = -(-(tiles - first) // 2)
    return [n * TILE for n in (tiles - first - second, second, first)]


def per_device(
    inputs, w_query, w_key, w_value, w_out, w_gate, w_up, w_down, gain_one, gain_two, cotangent
):
    dp = lax.axis_size("dp")
    bits = dp.bit_length() - 1
    count = 2 * dp
    micro, _, half, width = inputs.shape
    rows = width // count
    kind = BF16 if rows % 16 == 0 else F32
    hidden = w_gate.shape[1]
    groups = split_columns(hidden)
    padded = sum(groups)
    tab, core = block_tables(dp, bits)
    plan = Plan(dp, bits)
    plan.quarter = width // 4
    live = lambda: plan.live
    last = bits - 1

    x = inputs.reshape(micro, half, width)
    y = cotangent.reshape(micro, half, width)
    wide = w_query.shape[1] + w_key.shape[1] + w_value.shape[1]
    pair = jnp.pad(jnp.stack([gain_one, gain_two], axis=1), ((0, 0), (0, 126)))
    own_qkv = jnp.concatenate([w_query, w_key, w_value], axis=1)
    fill = ((0, 0), (0, padded - hidden))
    plan.gather("q", jnp.concatenate([own_qkv, pair], axis=1))
    plan.live.update(x=x, y=y, tab=tab)

    names = ["a", "b", "c"]
    downs = w_down.T

    def shard(k):
        at, size = sum(groups[:k]), groups[k]
        parts = [v[:, at : at + size] for v in (w_gate, w_up, downs)]
        short = size - parts[0].shape[1]
        if short:
            parts = [jnp.pad(p, ((0, 0), (0, short))) for p in parts]
        return jnp.stack(parts)

    def early(name, first=last):
        for stage in range(first, 1, -1):
            plan.double(name, stage)

    n = plan.live

    plan.double("q", last)
    n["x_came"], n["y_came"] = plan.send(x, -1), plan.send(y, -1)
    plan.gather("o", w_out)
    n.update(w_gate=w_gate, w_up=w_up, downs=downs)
    plan.fence()
    early("q", last - 1)
    plan.fence()
    plan.double("q", 1)
    plan.double("o", last)
    w_gate, w_up, downs = n["w_gate"], n["w_up"], n["downs"]
    plan.gather("a", shard(0))
    plan.fence()
    plan.double("q", 0)
    early("o", last - 1)
    plan.double("a", last)
    n["xt"], n["r1"], n["yt"], n["yn"] = pre(
        n.pop("tab"), n.pop("x"), n.pop("x_came"), n.pop("y"), n.pop("y_came"), rows, count, kind
    )
    w_gate, w_up, downs = n.pop("w_gate"), n.pop("w_up"), n.pop("downs")
    plan.gather("b", shard(1))
    plan.gather("c", shard(2))
    plan.fence()
    plan.double("q", -1)
    plan.double("o", 1)
    early("a", last - 1)
    plan.fence()

    qkv_bufs = plan.gathered("q")
    n["gains"] = gains = jnp.concatenate([b[:, wide:] for b in qkv_bufs], axis=0)
    plan.double("o", 0)
    plan.double("a", 1)
    plan.double("b", last)
    n["normed"], n["qkv"] = project(n["xt"].astype(BF16), n["r1"], gains, qkv_bufs, wide)
    plan.fence()
    plan.double("o", -1)
    plan.double("a", 0)
    early("b", last - 1)
    n["att"], n["den"] = attend(tab, n["qkv"], rows, count, kind)
    plan.fence()
    plan.double("a", -1)
    plan.double("b", 1)
    plan.double("c", last)
    n["res"], n["r2"], n["x2t"], n["x2"] = middle(
        tab, n["att"].astype(BF16), plan.gathered("o"), n["xt"].astype(BF16), n["gains"], rows, count
    )
    plan.fence()

    def feed_group(name):
        sums = (n["pull"], n["push"]) if "pull" in n else ()
        send, keep, n["pull"], n["push"] = feed(
            n["x2"], n["x2t"], n["yn"], n["yt"].astype(BF16), plan.gathered(name), sums,
            4 if name == names[-1] else 3,
        )
        for end in ("", "+", "-", "-+"):
            n.pop(name + end)
        plan.reduce("g" + name, send, keep)

    plan.double("b", 0)
    early("c", last - 1)
    feed_group("a")
    plan.fence()
    plan.double("b", -1)
    plan.double("c", 1)
    plan.fence()
    plan.double("c", 0)
    plan.halve("ga", -1)
    feed_group("b")
    plan.fence()
    plan.double("c", -1)
    plan.fence()
    plan.halve("ga", 0)
    plan.halve("gb", -1)
    feed_group("c")
    plan.fence()
    plan.halve("gb", 0)
    n["dres"], n["dm"] = back(
        tab, n.pop("pull"), n["res"], n["r2"], n["yt"].astype(BF16), n["gains"], rows, count, kind
    )
    send, keep, n["datt"] = mixed(
        n.pop("dm").astype(BF16),
        n["att"].astype(BF16),
        plan.gathered("o"),
        n.pop("gc.send"),
        n.pop("gc"),
    )
    plan.reduce("gc", send, keep)
    plan.fence()

    def heads_back(part):
        for k, v in zip(
            ("dq", "dk", "dv"),
            attend_back(
                tab, n["qkv"], n["datt"], n["att"], n["den"], BACK_PARTS[part], rows, count
            ),
        ):
            n[k + str(part)] = v

    plan.halve("ga", 1)
    plan.halve("gb", 1)
    plan.halve("gc", -1)
    heads_back(0)
    plan.fence()
    plan.halve("gc", 0)
    plan.halve("gb", 2)
    plan.prep_far("ga")
    plan.go_far("ga")
    heads_back(1)
    n["grads"] = jnp.concatenate(
        [n.pop(k + str(p)) for k in ("dq", "dk", "dv") for p in range(len(BACK_PARTS))], axis=0
    )
    plan.fence()
    plan.halve("gc", 1)
    for stage in range(3, bits):
        plan.halve("gb", stage)
    send, keep = weights_of(n["normed"], n["grads"])
    plan.reduce("gq", send, keep)
    plan.fence()
    plan.halve("gq", -1)
    plan.prep_far("gc")
    plan.fence()
    plan.prep("gq", 0)
    plan.fence()

    def give_back(name):
        own, came = n.pop(name + "_own"), n.pop(name + "_came")
        first = core == 0
        both = jnp.stack([jnp.where(first, own, came), jnp.where(first, came, own)])
        return both.reshape(micro, 1, half, width)

    plan.go("gq", 0)
    plan.go_far("gc")
    n["dx_own"], n["dx_other"] = input_of(
        tab, n["grads"], plan.gathered("q"), n["gains"], n["dres"], n["xt"].astype(BF16), n["r1"], rows, count, kind
    )
    n["out_own"], n["out_other"] = output_of(tab, n.pop("push"), n["res"], rows, count, kind)
    plan.fence()
    plan.prep("gq", 1)
    plan.fence()
    plan.go("gq", 1)
    for name in ("dx", "out"):
        n[name + "_came"] = plan.send(n.pop(name + "_other"), -1)
    plan.after("dx_came", ["dx_own"] + [key for k in ("ga", "gb") for key in plan.parts[k]])
    n["dx"] = give_back("dx")
    n["sum_a"] = plan.reduced("ga")
    n["sum_b"] = plan.reduced("gb")
    plan.fence()
    plan.prep_far("gq")
    plan.fence()
    plan.go_far("gq")
    first_landed = plan.parts["gq"][-1] if bits > 4 else "gq.far1"
    plan.after(
        first_landed,
        ["out_own", "out_came", "sum_a", "sum_b"] + list(plan.parts["gc"]),
    )
    n["out"] = give_back("out")
    last_sum = plan.reduced("gc")
    ff = jnp.concatenate([n["sum_a"], n["sum_b"], last_sum[:3]], axis=-1)[:, :, :hidden]
    n["gain_two"] = (
        jnp.sum(w_gate.astype(F32) * ff[0] + w_up.astype(F32) * ff[1], axis=1)
    ) / gain_two.astype(F32)
    n["ff0"], n["ff1"], n["ff2"] = ff[0], ff[1], ff[2].T
    n["grad_out"] = last_sum[3]
    plan.fence()
    grad_qkv = plan.reduced("gq")
    a, b = w_query.shape[1], w_query.shape[1] + w_key.shape[1]
    gain_one_grad = jnp.sum(own_qkv.astype(F32) * grad_qkv, axis=1) / gain_one.astype(F32)
    return (
        n["out"],
        n["dx"],
        grad_qkv[:, :a],
        grad_qkv[:, a:b],
        grad_qkv[:, b:],
        n["grad_out"],
        n["ff0"],
        n["ff1"],
        n["ff2"],
        gain_one_grad,
        n["gain_two"],
    )


def solution(mesh):
    shard = P(AXES, None)
    batch = P(None, "dp", "seq", None)
    return jax.shard_map(
        per_device,
        mesh=mesh,
        in_specs=(batch,) + (shard,) * 6 + (P(None, AXES), P(AXES), P(AXES), batch),
        out_specs=(batch,) * 2 + (shard,) * 6 + (P(None, AXES), P(AXES), P(AXES)),
        check_vma=False,
    )
```
